32 devices in a mesh: rep: 4 (over y, core), shard: 8 (over z, x).
Axes of the slice: x: 2, y: 2, z: 4, core: 2. Of those that a mesh axis runs over, the one named last changes fastest.
Arguments:
- hidden_in: bfloat16 [4096, 1088], P(('rep', 'shard')), may hold values from -6 to 6
- cotangent: bfloat16 [4096, 1088], P(('rep', 'shard')), may hold values from -6 to 6
- segment_ids: int32 [32, 128], P(('rep', 'shard')), may hold values from 0 to 3, never falling along the last dimension, each value on 1 to 64 neighbouring positions
- attn_weight: float32 [1088, 4352], P('shard'), may hold values from -0.36380344 to 0.36380344
- attn_moments: float32 [2, 1088, 4352], P(None, 'shard'), may hold values from -20 to 21, as said below
- up_weight: float32 [1088, 4352], P('shard'), may hold values from -0.1875 to 0.1875
- up_moments: float32 [2, 1088, 4352], P(None, 'shard'), may hold values from -20 to 21, as said below
- down_weight: float32 [4352, 1088], P('shard'), may hold values from -0.09375 to 0.09375
- down_moments: float32 [2, 4352, 1088], P(None, 'shard'), may hold values from -20 to 21, as said below
- vectors: float32 [12, 1088], P(None, 'shard'), may hold values from -2 to 3
- vector_moments: float32 [2, 12, 1088], P(None, None, 'shard'), may hold values from -20 to 21, as said below
Outputs:
- block_out: bfloat16 [4096, 1088], P(('rep', 'shard'))
- input_grad: bfloat16 [4096, 1088], P(('rep', 'shard'))
- attn_grad: float32 [1088, 4352], P('shard')
- up_grad: float32 [1088, 4352], P('shard')
- down_grad: float32 [4352, 1088], P('shard')
- vector_grad: float32 [12, 1088], P(None, 'shard')
- new_attn_weight: float32 [1088, 4352], P('shard')
- new_attn_moments: float32 [2, 1088, 4352], P(None, 'shard')
- new_up_weight: float32 [1088, 4352], P('shard')
- new_up_moments: float32 [2, 1088, 4352], P(None, 'shard')
- new_down_weight: float32 [4352, 1088], P('shard')
- new_down_moments: float32 [2, 4352, 1088], P(None, 'shard')
- new_vectors: float32 [12, 1088], P(None, 'shard')
- new_vector_moments: float32 [2, 12, 1088], P(None, None, 'shard')
The draws below stay inside these ranges and needn't reach their ends.
Inputs may be any that keep to these rules, and one draw needn't show every extreme that they name: `segment_ids`: each row holds the sequence ids of one device's 128 tokens; ids never fall along a row; a sequence spans at most 64 tokens. `attn_moments`: the second moments are positive. `up_moments`: the second moments are positive. `down_moments`: the second moments are positive. `vector_moments`: the second moments are positive.
All inputs are finite; a program needn't handle non-finite values.
Results may differ from the reference program's by a relative error of at most 0.02.
Values may be sent and summed in bfloat16 or wider, within the bound.
A program may use at most 256 MiB of HBM per device.

```python
import math
import jax
import jax.numpy as jnp
import numpy as np
from jax import lax

D = 1088
HEAD_DIM = 64
FF = 4352
TOK_DEV = 128
SEGS = 4
ADAM_STEP = 3
SEQ_MAX = 64
TOKENS = 4096
N_REP = 4
N_SHARD = 8
DEVICES = 32


def spread_normal(key, array_shape, scale):
    return jax.random.truncated_normal(key, -4.0, 4.0, array_shape, jnp.float32) * scale


def moments_of(key, array_shape, salt):
    own_key = jax.random.fold_in(key, salt)
    key_first = jax.random.fold_in(own_key, 11)
    key_second = jax.random.fold_in(own_key, 23)
    first_moment = spread_normal(key_first, array_shape, 5.0)
    second_moment = jnp.exp(jax.random.uniform(key_second, array_shape, jnp.float32, 0.0, 3.0))
    return jnp.stack([first_moment, second_moment])


def draw_attn_weight(key, part):
    key_base = jax.random.fold_in(key, 5)
    base = spread_normal(key_base, (D, 4 * D), D ** (-0.5))
    column = jnp.arange(4 * D)
    return base * jnp.where(column >= 3 * D, 3.0, 1.0)[None, :]


def draw_vectors(key, part):
    noises = spread_normal(jax.random.fold_in(key, 3), (12, D), 0.3)
    row_ids = jnp.arange(12)[:, None]
    gain_rows = jnp.logical_or(row_ids == 0, row_ids == 5)
    return jnp.where(gain_rows, 1.0 + noises, noises)


def draw_attn_moments(key, part):
    return moments_of(key, (D, 4 * D), 101)


def draw_up_moments(key, part):
    return moments_of(key, (D, FF), 202)


def draw_down_moments(key, part):
    return moments_of(key, (FF, D), 303)


def draw_vector_moments(key, part):
    return moments_of(key, (12, D), 404)


def level_of(key, extent, split, smallest, high):
    gain = 1.0
    for position, parts in split:
        heights = jax.random.uniform(jax.random.fold_in(jax.random.fold_in(key, 6), position), (parts,), jnp.float32, smallest / len(split), high / len(split))
        gain = gain * jnp.repeat(jnp.exp(heights), extent[position] // parts).reshape((-1,) + (1,) * (len(extent) - 1 - position))
    return gain


def profile(number_of, total, bound, slope):
    loads = [(1 << 20) // math.isqrt(standing ** slope) + 1 for standing in range(2, number_of + 1)]
    rest, holding = total - bound - (number_of - 1), [1] * (number_of - 1)
    while rest > 0:
        candidates = [i for i in range(number_of - 1) if holding[i] < bound]
        whole, budget = sum([loads[i] for i in candidates]), rest
        for i in candidates:
            addition = min(bound - holding[i], max(1, budget * loads[i] // whole), rest)
            holding[i] = holding[i] + addition
            rest = rest - addition
    return np.array([bound] + holding)


def uneven(key, number_of, total, most, slope):
    if number_of == 2:
        one = jax.random.randint(key, (), max(1, total - most), min(most, total - 1) + 1)
        return jnp.stack([one, total - one])
    sizes = jnp.asarray(profile(number_of, total, most, slope), jnp.int32)
    twos = (number_of - 1) // 2
    donor, sink = sizes[1:1 + 2 * twos:2], sizes[2:2 + 2 * twos:2]
    margin = jnp.minimum(donor - 1, most - sink)
    passed = jax.random.randint(jax.random.fold_in(key, 1), (twos,), 0, 1 << 20) % (margin + 1)
    sizes = sizes.at[1:1 + 2 * twos:2].set(donor - passed).at[2:2 + 2 * twos:2].set(sink + passed)
    return sizes[jax.random.permutation(jax.random.fold_in(key, 2), number_of)]


def normal_values(stream_key, shape, spread, reach, split=(), dtype=jnp.bfloat16):
    gain = level_of(stream_key, shape, split, -0.22, 0.18) if split else 1.0
    values = jax.random.normal(stream_key, shape, jnp.float32) * spread * gain
    return jnp.minimum(jnp.maximum(values, -reach), reach).astype(dtype)


def setup_inputs(seed: int = 0) -> dict:
    keys = jax.random.split(jax.random.key(seed), 12)
    hidden_in = normal_values(keys[0], (TOKENS, D), 1.0, 6.0, ((0, 32),))
    cotangent = normal_values(keys[1], (TOKENS, D), 1.0, 6.0, ((0, 32),))
    segment_ids = jax.vmap(lambda own: jnp.searchsorted(jnp.cumsum(uneven(own, SEGS, TOK_DEV, SEQ_MAX, 2)), jnp.arange(TOK_DEV), side="right"))(jax.random.split(keys[2], DEVICES)).reshape((DEVICES, TOK_DEV)).astype(jnp.int32)
    attn_weight = draw_attn_weight(jax.random.fold_in(keys[11], 71), 0)
    attn_moments = draw_attn_moments(jax.random.fold_in(keys[11], 71), 0)
    up_weight = normal_values(keys[5], (D, FF), D ** -0.5, 0.1875, ((0, 8),), jnp.float32)
    up_moments = draw_up_moments(jax.random.fold_in(keys[11], 71), 0)
    down_weight = normal_values(keys[7], (FF, D), FF ** -0.5, 0.09375, ((0, 8),), jnp.float32)
    down_moments = draw_down_moments(jax.random.fold_in(keys[11], 71), 0)
    vectors = draw_vectors(jax.random.fold_in(keys[11], 71), 0)
    vector_moments = draw_vector_moments(jax.random.fold_in(keys[11], 71), 0)
    return dict(hidden_in=hidden_in, cotangent=cotangent, segment_ids=segment_ids, attn_weight=attn_weight, attn_moments=attn_moments, up_weight=up_weight, up_moments=up_moments, down_weight=down_weight, down_moments=down_moments, vectors=vectors, vector_moments=vector_moments)


beta_one = 0.9
beta_two = 0.999
adam_eps = 1e-08
learn_rate = 0.25
weight_decay = 0.1

def matmul(left_arg, right_arg):
    return jnp.dot(left_arg, right_arg, preferred_element_type=jnp.float32)

def product(pattern, left_arg, right_arg):
    return jnp.einsum(pattern, left_arg.astype(jnp.float32), right_arg.astype(jnp.float32))

def normalize(values):
    average = lax.optimization_barrier(jnp.mean(values, axis=-1, keepdims=True))
    centred = values - average
    inv_std = lax.rsqrt(lax.optimization_barrier(jnp.mean(centred * centred, axis=-1, keepdims=True)) + 1e-05)
    return (centred * inv_std, inv_std)

def normalize_back(grad_in, normed, inv_std, gain_row):
    scaled = grad_in * gain_row
    return inv_std * (scaled - lax.optimization_barrier(jnp.mean(scaled, axis=-1, keepdims=True)) - normed * lax.optimization_barrier(jnp.mean(scaled * normed, axis=-1, keepdims=True)))

def allowed(segments):
    row_count = segments.shape[-1]
    causal = lax.broadcasted_iota(jnp.int32, (row_count, row_count), 0) >= lax.broadcasted_iota(jnp.int32, (row_count, row_count), 1)
    same_doc = segments[:, :, None] == segments[:, None, :]
    return jnp.logical_and(same_doc, causal)[:, None, :, :]

def scores_of(queries, keys_all, segments):
    logits = product('bqhe,bkhe->bhqk', queries, keys_all) * HEAD_DIM ** (-0.5)
    return jnp.where(allowed(segments), logits, -1e+30)

def forward(activations, segments, params):
    attn_full, up_full, down_full, vector_full = params
    batch_size, row_count, features = activations.shape
    head_count = features // HEAD_DIM
    head_shape = (batch_size, row_count, head_count, HEAD_DIM)
    vector_rows = vector_full.astype(jnp.float32)
    inputs_flat = activations.astype(jnp.float32).reshape(batch_size * row_count, features)
    normed_one, inv_one = normalize(inputs_flat)
    attn_input = (normed_one * vector_rows[0] + vector_rows[1]).astype(jnp.bfloat16)
    projected = matmul(attn_input, attn_full[:, :3 * features])
    queries = (projected[:, :features] + vector_rows[2]).astype(jnp.bfloat16).reshape(head_shape)
    keys_all = projected[:, features:2 * features].astype(jnp.bfloat16).reshape(head_shape)
    values_all = (projected[:, 2 * features:] + vector_rows[3]).astype(jnp.bfloat16).reshape(head_shape)
    logits = scores_of(queries, keys_all, segments)
    row_max = lax.optimization_barrier(jnp.max(logits, axis=-1, keepdims=True))
    exponent = jnp.exp(logits - row_max)
    totals = lax.optimization_barrier(jnp.sum(exponent, axis=-1, keepdims=True))
    log_total = row_max + jnp.log(totals)
    soft_probs = (exponent / totals).astype(jnp.bfloat16)
    attended = product('bhqk,bkhe->bqhe', soft_probs, values_all).reshape(batch_size * row_count, features).astype(jnp.bfloat16)
    residual = inputs_flat + matmul(attended, attn_full[:, 3 * features:]) + vector_rows[4]
    normed_two, inv_two = normalize(residual)
    dense_input = (normed_two * vector_rows[5] + vector_rows[6]).astype(jnp.bfloat16)
    pre_act = matmul(dense_input, up_full) + vector_rows[8:].reshape(-1)
    normal_cdf = 0.5 * (1.0 + lax.erf(pre_act * 0.7071067811865476))
    hidden_act = (pre_act * normal_cdf).astype(jnp.bfloat16)
    block_out = (residual + matmul(hidden_act, down_full) + vector_rows[7]).astype(jnp.bfloat16).reshape(batch_size, row_count, features)
    stored = (normed_one, inv_one, attn_input, queries, keys_all, values_all, log_total, attended, normed_two, inv_two, dense_input, pre_act, normal_cdf, hidden_act)
    return (block_out, stored)

def backward(cotangent, segments, stored, params):
    normed_one, inv_one, attn_input, queries, keys_all, values_all, log_total, attended, normed_two, inv_two, dense_input, pre_act, normal_cdf, hidden_act = stored
    attn_full, up_full, down_full, vector_full = params
    batch_size, row_count, features = cotangent.shape
    head_count = features // HEAD_DIM
    head_shape = (batch_size, row_count, head_count, HEAD_DIM)
    vector_rows = vector_full.astype(jnp.float32)
    out_grad = cotangent.reshape(batch_size * row_count, features)
    out_float = out_grad.astype(jnp.float32)
    down_grad = matmul(hidden_act.T, out_grad)
    density = jnp.exp(-0.5 * pre_act * pre_act) * 0.3989422804014327
    pre_grad = matmul(out_grad, down_full.T) * (normal_cdf + pre_act * density)
    pre_round = pre_grad.astype(jnp.bfloat16)
    up_grad = matmul(dense_input.T, pre_round)
    dense_input_grad = matmul(pre_round, up_full.T)
    resid_grad = out_float + normalize_back(dense_input_grad, normed_two, inv_two, vector_rows[5])
    resid_round = resid_grad.astype(jnp.bfloat16)
    out_proj_grad = matmul(attended.T, resid_round)
    attended_grad = matmul(resid_round, attn_full[:, 3 * features:].T).astype(jnp.bfloat16)
    heads_grad = attended_grad.reshape(head_shape)
    logits = scores_of(queries, keys_all, segments)
    recomputed = jnp.exp(logits - log_total)
    prob_round = recomputed.astype(jnp.bfloat16)
    prob_grad = product('bqhe,bkhe->bhqk', heads_grad, values_all)
    delta_row = product('bqhe,bqhe->bhq', heads_grad, attended.reshape(head_shape))[..., None]
    logit_grad = (recomputed * (prob_grad - delta_row)).astype(jnp.bfloat16)
    scale_factor = HEAD_DIM ** (-0.5)
    query_grad = product('bhqk,bkhe->bqhe', logit_grad, keys_all) * scale_factor
    key_grad = product('bhqk,bqhe->bkhe', logit_grad, queries) * scale_factor
    value_grad = product('bhqk,bqhe->bkhe', prob_round, heads_grad)
    joined_grad = jnp.concatenate([query_grad.reshape(-1, features), key_grad.reshape(-1, features), value_grad.reshape(-1, features)], axis=1)
    joined_round = joined_grad.astype(jnp.bfloat16)
    qkv_grad = matmul(attn_input.T, joined_round)
    attn_input_grad = matmul(joined_round, attn_full[:, :3 * features].T)
    input_grad = (resid_grad + normalize_back(attn_input_grad, normed_one, inv_one, vector_rows[0])).astype(jnp.bfloat16).reshape(batch_size, row_count, features)
    small_rows = jnp.stack([lax.optimization_barrier(jnp.sum(attn_input_grad * normed_one, axis=0)), lax.optimization_barrier(jnp.sum(attn_input_grad, axis=0)), lax.optimization_barrier(jnp.sum(joined_grad[:, :features], axis=0)), lax.optimization_barrier(jnp.sum(joined_grad[:, 2 * features:], axis=0)), lax.optimization_barrier(jnp.sum(resid_grad, axis=0)), lax.optimization_barrier(jnp.sum(dense_input_grad * normed_two, axis=0)), lax.optimization_barrier(jnp.sum(dense_input_grad, axis=0)), lax.optimization_barrier(jnp.sum(out_float, axis=0))])
    vector_grad = jnp.concatenate([small_rows, lax.optimization_barrier(jnp.sum(pre_grad, axis=0)).reshape(4, features)], axis=0)
    attn_grad = jnp.concatenate([qkv_grad, out_proj_grad], axis=1)
    return (input_grad, (attn_grad, up_grad, down_grad, vector_grad))

def adam_update(weight, moments, grad_in, decay):
    first_moment = beta_one * moments[0] + (1.0 - beta_one) * grad_in
    second_moment = beta_two * moments[1] + (1.0 - beta_two) * grad_in * grad_in
    correct_one = 1.0 - beta_one ** ADAM_STEP
    correct_two = 1.0 - beta_two ** ADAM_STEP
    step_size = first_moment / correct_one / (jnp.sqrt(second_moment / correct_two) + adam_eps)
    updated = weight - learn_rate * (step_size + decay * weight)
    return (updated, jnp.stack([first_moment, second_moment]))

def reference(hidden_in, cotangent, segment_ids, attn_weight, attn_moments, up_weight, up_moments, down_weight, down_moments, vectors, vector_moments):
    params = (attn_weight.astype(jnp.bfloat16), up_weight.astype(jnp.bfloat16), down_weight.astype(jnp.bfloat16), vectors.astype(jnp.bfloat16))
    grouped_in = hidden_in.reshape(N_REP, N_SHARD, TOK_DEV, D)
    grouped_cot = cotangent.reshape(N_REP, N_SHARD, TOK_DEV, D)
    grouped_seg = segment_ids.reshape(N_REP, N_SHARD, TOK_DEV)

    def group_step(running, item):
        group_in, group_cot, group_seg = item
        group_out, stored = forward(group_in, group_seg, params)
        group_grad, gradients = backward(group_cot, group_seg, stored, params)
        summed = tuple((before + adding for before, adding in zip(running, gradients)))
        return (summed, (group_out, group_grad))
    zero_grads = (jnp.zeros((D, 4 * D), jnp.float32), jnp.zeros((D, FF), jnp.float32), jnp.zeros((FF, D), jnp.float32), jnp.zeros((12, D), jnp.float32))
    totals, (outs_all, grads_all) = lax.scan(group_step, zero_grads, (grouped_in, grouped_cot, grouped_seg))
    new_attn, attn_next = adam_update(attn_weight, attn_moments, totals[0], weight_decay)
    new_up, up_next = adam_update(up_weight, up_moments, totals[1], weight_decay)
    new_down, down_next = adam_update(down_weight, down_moments, totals[2], weight_decay)
    new_vectors, vector_next = adam_update(vectors, vector_moments, totals[3], 0.0)
    return (outs_all.reshape(TOKENS, D), grads_all.reshape(TOKENS, D), totals[0], totals[1], totals[2], totals[3], new_attn, attn_next, new_up, up_next, new_down, down_next, new_vectors, vector_next)
```

```python
import functools

import jax
import jax.numpy as jnp
from jax import lax
from jax.experimental import pallas as pl
from jax.experimental.pallas import tpu as pltpu
from jax.sharding import PartitionSpec as P

HEAD_DIM = 64
ADAM_STEP = 3
MESH = pl.DeviceIdType.MESH


beta_one = 0.9
beta_two = 0.999
adam_eps = 1e-08
learn_rate = 0.25
weight_decay = 0.1


def matmul(left_arg, right_arg):
    return jnp.dot(left_arg, right_arg, preferred_element_type=jnp.float32)


def inner_rows(left_arg, right_arg):
    return lax.dot_general(
        left_arg, right_arg, (((0,), (0,)), ((), ())), preferred_element_type=jnp.float32
    )


def product(pattern, left_arg, right_arg):
    return jnp.einsum(pattern, left_arg, right_arg, preferred_element_type=jnp.float32)


def normalize(values):
    average = jnp.mean(values, axis=-1, keepdims=True)
    centred = values - average
    inv_std = lax.rsqrt(jnp.mean(centred * centred, axis=-1, keepdims=True) + 1e-05)
    return (centred * inv_std, inv_std)


def normalize_back(grad_in, normed, inv_std, gain_row):
    scaled = grad_in * gain_row
    return inv_std * (
        scaled
        - jnp.mean(scaled, axis=-1, keepdims=True)
        - normed * jnp.mean(scaled * normed, axis=-1, keepdims=True)
    )


def allowed(segments):
    row_count = segments.shape[-1]
    causal = lax.broadcasted_iota(jnp.int32, (row_count, row_count), 0) >= lax.broadcasted_iota(
        jnp.int32, (row_count, row_count), 1
    )
    same_doc = segments[:, :, None] == segments[:, None, :]
    return jnp.logical_and(same_doc, causal)[:, None, :, :]


def scores_of(queries, keys_all, segments):
    logits = product("bqhe,bkhe->bhqk", queries, keys_all) * HEAD_DIM ** (-0.5)
    return jnp.where(allowed(segments), logits, -1e30)


def attention_forward(activations, segments, attn_full, vector_full):
    batch_size, row_count, features = activations.shape
    head_count = features // HEAD_DIM
    head_shape = (batch_size, row_count, head_count, HEAD_DIM)
    vector_rows = vector_full.astype(jnp.float32)
    inputs_flat = activations.astype(jnp.float32).reshape(batch_size * row_count, features)
    normed_one, inv_one = normalize(inputs_flat)
    attn_input = (normed_one * vector_rows[0] + vector_rows[1]).astype(jnp.bfloat16)
    projected = matmul(attn_input, attn_full[:, : 3 * features])
    queries = (projected[:, :features] + vector_rows[2]).astype(jnp.bfloat16).reshape(head_shape)
    keys_all = projected[:, features : 2 * features].astype(jnp.bfloat16).reshape(head_shape)
    values_all = (
        (projected[:, 2 * features :] + vector_rows[3]).astype(jnp.bfloat16).reshape(head_shape)
    )
    logits = scores_of(queries, keys_all, segments)
    row_max = jnp.max(logits, axis=-1, keepdims=True)
    exponent = jnp.exp(logits - row_max)
    totals = jnp.sum(exponent, axis=-1, keepdims=True)
    log_total = row_max + jnp.log(totals)
    soft_probs = (exponent / totals).astype(jnp.bfloat16)
    attended = (
        product("bhqk,bkhe->bqhe", soft_probs, values_all)
        .reshape(batch_size * row_count, features)
        .astype(jnp.bfloat16)
    )
    residual = inputs_flat + matmul(attended, attn_full[:, 3 * features :]) + vector_rows[4]
    normed_two, inv_two = normalize(residual)
    dense_input = (normed_two * vector_rows[5] + vector_rows[6]).astype(jnp.bfloat16)
    stored = (
        normed_one,
        inv_one,
        attn_input,
        queries,
        keys_all,
        values_all,
        log_total,
        attended,
        normed_two,
        inv_two,
    )
    return (residual, dense_input, stored)


def attention_backward(cotangent, segments, stored, attn_full, vector_full, dense_input_grad):
    (
        normed_one,
        inv_one,
        attn_input,
        queries,
        keys_all,
        values_all,
        log_total,
        attended,
        normed_two,
        inv_two,
    ) = stored
    batch_size, row_count, features = cotangent.shape
    head_count = features // HEAD_DIM
    head_shape = (batch_size, row_count, head_count, HEAD_DIM)
    vector_rows = vector_full.astype(jnp.float32)
    out_float = cotangent.reshape(batch_size * row_count, features).astype(jnp.float32)
    resid_grad = out_float + normalize_back(dense_input_grad, normed_two, inv_two, vector_rows[5])
    resid_round = resid_grad.astype(jnp.bfloat16)
    attended_grad = lax.dot_general(
        resid_round,
        attn_full[:, 3 * features :],
        (((1,), (1,)), ((), ())),
        preferred_element_type=jnp.float32,
    ).astype(jnp.bfloat16)
    heads_grad = attended_grad.reshape(head_shape)
    logits = scores_of(queries, keys_all, segments)
    recomputed = jnp.exp(logits - log_total)
    prob_round = recomputed.astype(jnp.bfloat16)
    prob_grad = product("bqhe,bkhe->bhqk", heads_grad, values_all)
    delta_row = product("bqhe,bqhe->bhq", heads_grad, attended.reshape(head_shape))[..., None]
    logit_grad = (recomputed * (prob_grad - delta_row)).astype(jnp.bfloat16)
    scale_factor = HEAD_DIM ** (-0.5)
    query_grad = product("bhqk,bkhe->bqhe", logit_grad, keys_all) * scale_factor
    key_grad = product("bhqk,bqhe->bkhe", logit_grad, queries) * scale_factor
    value_grad = product("bhqk,bqhe->bkhe", prob_round, heads_grad)
    joined_grad = jnp.concatenate(
        [
            query_grad.reshape(-1, features),
            key_grad.reshape(-1, features),
            value_grad.reshape(-1, features),
        ],
        axis=1,
    )
    joined_round = joined_grad.astype(jnp.bfloat16)
    attn_input_grad = lax.dot_general(
        joined_round,
        attn_full[:, : 3 * features],
        (((1,), (1,)), ((), ())),
        preferred_element_type=jnp.float32,
    )
    input_grad = (
        (resid_grad + normalize_back(attn_input_grad, normed_one, inv_one, vector_rows[0]))
        .astype(jnp.bfloat16)
        .reshape(batch_size, row_count, features)
    )
    small_rows = jnp.stack(
        [
            jnp.sum(attn_input_grad * normed_one, axis=0),
            jnp.sum(attn_input_grad, axis=0),
            jnp.sum(joined_grad[:, :features], axis=0),
            jnp.sum(joined_grad[:, 2 * features :], axis=0),
            jnp.sum(resid_grad, axis=0),
            jnp.sum(dense_input_grad * normed_two, axis=0),
            jnp.sum(dense_input_grad, axis=0),
            jnp.sum(out_float, axis=0),
        ]
    )
    return (input_grad, small_rows, attn_input, joined_round, attended, resid_round)


def adam_update(weight, moments, grad_in, decay):
    first_moment = beta_one * moments[0] + (1.0 - beta_one) * grad_in
    second_moment = beta_two * moments[1] + (1.0 - beta_two) * grad_in * grad_in
    correct_one = 1.0 - beta_one**ADAM_STEP
    correct_two = 1.0 - beta_two**ADAM_STEP
    step_size = first_moment / correct_one / (jnp.sqrt(second_moment / correct_two) + adam_eps)
    updated = weight - learn_rate * (step_size + decay * weight)
    return (updated, jnp.stack([first_moment, second_moment]))


CORES = 2
ROW_UNIT = 16
LANE_UNIT = 128
GATHER_VMEM = 16 * 2**20
REDUCE_VMEM = 32 * 2**20
DENSE_VMEM = 52 * 2**20


class Grid:
    def __init__(self, rep_size, shard_size):
        self.cores = CORES
        self.y_size = rep_size // CORES
        self.x_size = self.y_size if shard_size % self.y_size == 0 else 1
        self.z_size = shard_size // self.x_size

    def locate(self):
        rep = lax.axis_index("rep")
        shard = lax.axis_index("shard")
        self.y, self.c = lax.div(rep, CORES), lax.rem(rep, CORES)
        self.z, self.x = lax.div(shard, self.x_size), lax.rem(shard, self.x_size)
        return self

    def device(self, dz=0, dx=0, dy=0, dc=0):
        rep = lax.rem(self.y + dy, self.y_size) * CORES + lax.rem(self.c + dc, CORES)
        shard = lax.rem(self.z + dz, self.z_size) * self.x_size + lax.rem(self.x + dx, self.x_size)
        return (rep, shard)

    def partners(self):
        found = [self.device(dz=k) for k in range(1, self.z_size)]
        found += [self.device(dx=k) for k in range(1, self.x_size)]
        found += [self.device(dy=k) for k in range(1, self.y_size)]
        return found + [self.device(dc=1)]

    def greet(self):
        barrier = pltpu.get_barrier_semaphore()
        partners = self.partners()
        for partner in partners:
            pl.semaphore_signal(barrier, inc=1, device_id=partner, device_id_type=MESH)
        pl.semaphore_wait(barrier, len(partners))


class Split:
    def __init__(self, rows, columns, y_size, share=0.7, array=0, chunk=0, chunks=1):
        self.rows, self.columns, self.array = rows, columns, array
        self.by_lane = columns % (2 * LANE_UNIT) == 0
        unit = LANE_UNIT if self.by_lane else ROW_UNIT
        extent = columns if self.by_lane else rows
        padded = -(-extent // (2 * unit)) * 2 * unit
        if not self.by_lane:
            self.rows = padded
        pairs = padded // (2 * unit)
        chunks = max(1, min(chunks, pairs // (y_size + 1)))
        self.chunks = chunks
        starts = [n * (pairs // chunks) + min(n, pairs % chunks) for n in range(chunks + 1)]
        units = starts[chunk + 1] - starts[chunk]
        self.unit = unit
        self.start = 2 * unit * starts[chunk]
        self.half = units * unit
        taken = min(max(1, int(units * share / y_size + 0.5)), (units - 1) // y_size)
        self.a_size = taken * unit
        self.b_start = y_size * self.a_size
        self.b_size = self.half - self.b_start

    def chunked(self, y_size, share, array, chunks):
        found = Split(self.rows, self.columns, y_size, share, array, 0, chunks)
        return [found] + [
            Split(self.rows, self.columns, y_size, share, array, n, chunks)
            for n in range(1, found.chunks)
        ]

    def block(self):
        return (self.rows, self.columns)

    def shape(self, size):
        return (self.rows, size) if self.by_lane else (size, self.columns)

    def cut(self, start, size):
        window = pl.ds(pl.multiple_of(self.start + start, self.unit), size)
        return (slice(None), window) if self.by_lane else (window, slice(None))

    def piece_a(self, y, c):
        return self.cut(c * self.half + y * self.a_size, self.a_size)

    def piece_b(self, c):
        return self.cut(c * self.half + self.b_start, self.b_size)

    def piece_half(self, c):
        return self.cut(c * self.half, self.half)

    def pad(self, values):
        extra = self.rows - values.shape[-2]
        if extra == 0:
            return values
        return jnp.pad(values, [(0, 0)] * (values.ndim - 2) + [(0, extra), (0, 0)])


def remote(source, target, send, recv, device):
    return pltpu.make_async_remote_copy(
        src_ref=source,
        dst_ref=target,
        send_sem=send,
        recv_sem=recv,
        device_id=device,
        device_id_type=MESH,
    )


class Semaphores:
    def __init__(self, array):
        self.array, self.used = array, 0

    def take(self):
        self.used += 1
        return self.array.at[self.used - 1]


def gather_kernel(grid, splits, *refs):
    count = len(splits)
    own, full = refs[: count + 1], refs[count + 1 : 2 * count + 2]
    send_array, recv_array, local_array = refs[2 * count + 2 :]
    sends, recvs, locals_ = (
        Semaphores(send_array),
        Semaphores(recv_array),
        Semaphores(local_array),
    )
    g = grid.locate()
    z_size, x_size, y_size = g.z_size, g.x_size, g.y_size
    started = []
    copies = {}

    def launch(key, source, target, device):
        copy = remote(source, target, sends.take(), recvs.take(), device)
        copy.start()
        copies[key] = copy

    place = lambda j, i: (lax.rem(g.z + z_size - j, z_size), lax.rem(g.x + x_size - i, x_size))

    def windows(t):
        if t == count:
            return [(slice(None), slice(None))]
        return [splits[t].piece_a(g.y, g.c), splits[t].piece_b(g.c)]

    g.greet()
    order = [count] + list(range(count))

    def stage_z(t):
        for k in range(1, z_size):
            for p, window in enumerate(windows(t)):
                launch(
                    ("z", t, p, k),
                    own[t].at[window],
                    full[t].at[(g.z, g.x) + window],
                    g.device(dz=k),
                )
        copy = pltpu.make_async_copy(own[t], full[t].at[g.z, g.x], locals_.take())
        copy.start()
        started.append(copy)

    def unit_x(t, j):
        for p, window in enumerate(windows(t)):
            here = place(j, 0) + window
            if j > 0:
                copies["z", t, p, j].wait_recv()
            source = own[t].at[window] if j == 0 else full[t].at[here]
            for i in range(1, x_size):
                launch(("x", t, p, j, i), source, full[t].at[here], g.device(dx=i))
            if t < count and p == 0 and j > 0:
                for k in range(1, y_size):
                    launch(("y", t, j, 0, k), source, full[t].at[here], g.device(dy=k))

    def unit_y(t, j):
        for i in range(1, x_size):
            for p, window in enumerate(windows(t)):
                copies["x", t, p, j, i].wait_recv()
                if t < count and p == 0:
                    here = full[t].at[place(j, i) + window]
                    for k in range(1, y_size):
                        launch(("y", t, j, i, k), here, here, g.device(dy=k))

    def unit_core(t, j):
        if t == count:
            return
        for i in range(x_size):
            if (j, i) == (0, 0):
                continue
            for k in range(1, y_size):
                copies["y", t, j, i, k].wait_recv()
            here = full[t].at[place(j, i) + splits[t].piece_half(g.c)]
            launch(("c", t, j, i), here, here, g.device(dc=1))

    for t in order:
        stage_z(t)
    units = [(t, j) for t in order for j in range(z_size)]
    for step in range(len(units) + 2):
        for lag, unit in enumerate((unit_x, unit_y, unit_core)):
            if 0 <= step - lag < len(units):
                unit(*units[step - lag])
    for key, copy in copies.items():
        if key[0] == "c":
            copy.wait_recv()
        copy.wait_send()
    for copy in started:
        copy.wait()


def gather_params(grid, splits, blocks, vector_block):
    z, x, y = grid.z_size, grid.x_size, grid.y_size
    per_tensor = 2 * (z - 1) + 2 * z * (x - 1) + (z * x - 1) * y
    total = len(splits) * per_tensor + (z - 1) + z * (x - 1)
    shapes = [
        jax.ShapeDtypeStruct((z, x) + split.block(), jnp.bfloat16) for split in splits
    ] + [jax.ShapeDtypeStruct((z, x) + vector_block.shape, jnp.bfloat16)]
    return pl.pallas_call(
        functools.partial(gather_kernel, grid, splits),
        out_shape=shapes,
        in_specs=[pl.BlockSpec(memory_space=pltpu.VMEM)] * (len(splits) + 1),
        out_specs=[pl.BlockSpec(memory_space=pl.ANY)] * (len(splits) + 1),
        scratch_shapes=[
            pltpu.SemaphoreType.DMA((total,)),
            pltpu.SemaphoreType.DMA((total,)),
            pltpu.SemaphoreType.DMA((len(splits) + 1,)),
        ],
        compiler_params=pltpu.CompilerParams(
            collective_id=0, has_side_effects=True, vmem_limit_bytes=GATHER_VMEM
        ),
        name="gather_params",
    )(*blocks, vector_block)


def plus(left_arg, right_arg):
    return left_arg.astype(jnp.float32) + right_arg.astype(jnp.float32)


def reduce_kernel(grid, splits, *refs):
    count = len(splits)
    arrays = splits[-1].array + 1
    vector_in, vector_out = refs[arrays], refs[2 * arrays + 1]
    grads = [refs[split.array] for split in splits]
    outs = [refs[arrays + 1 + split.array] for split in splits]
    scratch = refs[2 * arrays + 2 :]
    per = 12
    buffers = [scratch[per * t : per * (t + 1)] for t in range(count)]
    v_core, v_y, v_x, v_z, v_one, v_two, v_three, send_array, recv_array, local_array = scratch[
        per * count :
    ]
    sends, recvs, locals_ = (
        Semaphores(send_array),
        Semaphores(recv_array),
        Semaphores(local_array),
    )
    g = grid.locate()
    z_size, x_size, y_size = g.z_size, g.x_size, g.y_size
    copies, moves = {}, {}

    def launch(key, source, target, device):
        copy = remote(source, target, sends.take(), recvs.take(), device)
        copy.start()
        copies[key] = copy

    def move(key, source, target):
        copy = pltpu.make_async_copy(source, target, locals_.take())
        copy.start()
        moves[key] = copy

    def each_block(body):
        @pl.loop(0, z_size * x_size)
        def _(index):
            body(lax.div(index, x_size), lax.rem(index, x_size))

    everything = (slice(None), slice(None))
    other_y = lambda k: lax.rem(g.y + k, y_size)
    other_x = lambda k: lax.rem(g.x + k, x_size)
    other_z = lambda k: lax.rem(g.z + k, z_size)

    def stage_core(t):
        acc_a, acc_b, got_a, got_b = buffers[t][:4]
        split = splits[t]
        for q in range(y_size):
            launch(
                ("ca", t, q),
                grads[t].at[everything + split.piece_a(q, 1 - g.c)],
                got_a.at[q],
                g.device(dc=1),
            )
            move(("la", t, q), grads[t].at[everything + split.piece_a(q, g.c)], acc_a.at[q])
        launch(
            ("cb", t),
            grads[t].at[everything + split.piece_b(1 - g.c)],
            got_b,
            g.device(dc=1),
        )
        move(("lb", t), grads[t].at[everything + split.piece_b(g.c)], acc_b)

    def stage_y(t):
        acc_a, acc_b, got_a, got_b, got_y = buffers[t][:5]
        for q in range(y_size):
            copies["ca", t, q].wait_recv()
            moves["la", t, q].wait()

            def add_a(i, j, q=q):
                acc_a[q, i, j] = plus(acc_a[q, i, j], got_a[q, i, j]).astype(jnp.bfloat16)

            each_block(add_a)
        for k in range(1, y_size):
            launch(("ya", t, k), acc_a.at[other_y(k)], got_y.at[k - 1], g.device(dy=k))
        copies["cb", t].wait_recv()
        moves["lb", t].wait()

        def add_b(i, j):
            acc_b[i, j] = plus(acc_b[i, j], got_b[i, j]).astype(jnp.bfloat16)

        each_block(add_b)
        for k in range(1, x_size):
            launch(
                ("xb", t, k), acc_b.at[:, other_x(k)], buffers[t][6].at[k - 1], g.device(dx=k)
            )

    def stage_x(t):
        acc_a, got_y, got_xa = buffers[t][0], buffers[t][4], buffers[t][5]
        for k in range(1, y_size):
            copies["ya", t, k].wait_recv()

        def add(i, j):
            value = acc_a[g.y, i, j].astype(jnp.float32)
            for k in range(1, y_size):
                value = plus(value, got_y[k - 1, i, j])
            acc_a[g.y, i, j] = value.astype(jnp.bfloat16)

        each_block(add)
        for k in range(1, x_size):
            launch(
                ("xa", t, k), acc_a.at[g.y, :, other_x(k)], got_xa.at[k - 1], g.device(dx=k)
            )

    def stage_z(t):
        acc_a, acc_b = buffers[t][:2]
        got_xa, got_xb, got_za, got_zb = buffers[t][5:9]
        for k in range(1, x_size):
            copies["xb", t, k].wait_recv()
            copies["xa", t, k].wait_recv()

        @pl.loop(0, z_size)
        def _(i):
            value_a = acc_a[g.y, i, g.x].astype(jnp.float32)
            for k in range(1, x_size):
                value_a = plus(value_a, got_xa[k - 1, i])
            acc_a[g.y, i, g.x] = value_a.astype(jnp.bfloat16)
            value_b = acc_b[i, g.x].astype(jnp.float32)
            for k in range(1, x_size):
                value_b = plus(value_b, got_xb[k - 1, i])
            acc_b[i, g.x] = value_b.astype(jnp.bfloat16)

        for k in range(1, z_size):
            launch(
                ("zb", t, k), acc_b.at[other_z(k), g.x], got_zb.at[k - 1], g.device(dz=k)
            )
            launch(
                ("za", t, k),
                acc_a.at[g.y, other_z(k), g.x],
                got_za.at[k - 1],
                g.device(dz=k),
            )

    def stage_final(t):
        acc_a, acc_b = buffers[t][:2]
        got_za, got_zb, final_a, ring_b, final_b = buffers[t][7:12]
        split = splits[t]
        for k in range(1, z_size):
            copies["zb", t, k].wait_recv()
        value = acc_b[g.z, g.x].astype(jnp.float32)
        for k in range(1, z_size):
            value = plus(value, got_zb[k - 1])
        ring_b[0] = value.astype(jnp.bfloat16)
        for k in range(1, y_size):
            launch(("yb", t, k), ring_b.at[0], ring_b.at[k], g.device(dy=k))
        for k in range(1, z_size):
            copies["za", t, k].wait_recv()
        value = acc_a[g.y, g.z, g.x].astype(jnp.float32)
        for k in range(1, z_size):
            value = plus(value, got_za[k - 1])
        final_a[...] = value.astype(jnp.bfloat16)
        target = outs[t].at[split.piece_a(g.y, g.c)]
        for k in range(1, y_size):
            launch(("oa", t, k), final_a, target, g.device(dy=k))
        move(("fa", t), final_a, target)

    def stage_share(t):
        ring_b, final_b = buffers[t][10:12]
        split = splits[t]
        for k in range(1, y_size):
            copies["yb", t, k].wait_recv()
        value = ring_b[g.y].astype(jnp.float32)
        for k in range(1, y_size):
            value = plus(value, ring_b[lax.rem(g.y + y_size - k, y_size)])
        final_b[...] = value.astype(jnp.bfloat16)
        move(("fb", t), final_b, outs[t].at[split.piece_b(g.c)])
        for k in range(1, y_size):
            copies["oa", t, k].wait_recv()
        moves["fa", t].wait()
        moves["fb", t].wait()
        half = outs[t].at[split.piece_half(g.c)]
        launch(("h", t), half, half, g.device(dc=1))

    def sum_ring(buffer, place, size):
        value = buffer[place]
        for k in range(1, size):
            value = value + buffer[lax.rem(place + size - k, size)]
        return value

    def vector_step(name, source, got, size, **direction):
        (axis,) = direction
        got[0] = source[...]
        for k in range(1, size):
            launch((name, k), source, got.at[k], g.device(**{axis: k}))

    def vector_sum(name, got, place, size, target):
        for k in range(1, size):
            copies[name, k].wait_recv()
        target[...] = sum_ring(got, place, size)

    g.greet()
    vector_step("vc", vector_in, v_core, CORES, dc=1)
    for t in range(count):
        stage_core(t)
    vector_sum("vc", v_core, g.c, CORES, v_one)
    vector_step("vy", v_one, v_y, y_size, dy=1)
    stages = [stage_y, stage_x, stage_z, stage_final, stage_share]
    for step in range(count + len(stages) - 1):
        for s in range(len(stages)):
            t = step - s
            if 0 <= t < count:
                stages[s](t)
        if step == 0:
            vector_sum("vy", v_y, g.y, y_size, v_two)
            vector_step("vx", v_two, v_x, x_size, dx=1)
        if step == 1:
            vector_sum("vx", v_x, g.x, x_size, v_three)
            vector_step("vz", v_three, v_z, z_size, dz=1)
        if step == 2:
            vector_sum("vz", v_z, g.z, z_size, vector_out)
    for key, copy in copies.items():
        if key[0] == "h":
            copy.wait_recv()
        copy.wait_send()


def reduce_grads(grid, whole, grads, vector_terms):
    z, x, y = grid.z_size, grid.x_size, grid.y_size
    splits = []
    for array, split in enumerate(whole):
        splits += split.chunked(y, 0.58, array, 3)
    scratch = []
    for split in splits:
        a, b = split.shape(split.a_size), split.shape(split.b_size)
        scratch += [
            pltpu.VMEM(shape, jnp.bfloat16)
            for shape in (
                (y, z, x) + a,
                (z, x) + b,
                (y, z, x) + a,
                (z, x) + b,
                (y - 1, z, x) + a,
                (x - 1, z) + a,
                (x - 1, z) + b,
                (z - 1,) + a,
                (z - 1,) + b,
                a,
                (y,) + b,
                b,
            )
        ]
    small = vector_terms.shape
    scratch += [pltpu.VMEM((size,) + small, jnp.float32) for size in (CORES, y, x, z)]
    scratch += [pltpu.VMEM(small, jnp.float32)] * 3
    per_tensor = (y + 1) + (y - 1) + 2 * (x - 1) + 2 * (z - 1) + 2 * (y - 1) + 1
    total = len(splits) * per_tensor + 1 + (y - 1) + (x - 1) + (z - 1)
    scratch += [
        pltpu.SemaphoreType.DMA((total,)),
        pltpu.SemaphoreType.DMA((total,)),
        pltpu.SemaphoreType.DMA((len(splits) * (y + 3),)),
    ]
    return pl.pallas_call(
        functools.partial(reduce_kernel, grid, splits),
        out_shape=[jax.ShapeDtypeStruct(split.block(), jnp.bfloat16) for split in whole]
        + [jax.ShapeDtypeStruct(small, jnp.float32)],
        in_specs=[pl.BlockSpec(memory_space=pl.ANY)] * len(whole)
        + [pl.BlockSpec(memory_space=pltpu.VMEM)],
        out_specs=[pl.BlockSpec(memory_space=pl.ANY)] * len(whole)
        + [pl.BlockSpec(memory_space=pltpu.VMEM)],
        scratch_shapes=scratch,
        compiler_params=pltpu.CompilerParams(
            collective_id=1, has_side_effects=True, vmem_limit_bytes=REDUCE_VMEM
        ),
        name="reduce_grads",
    )(*grads, vector_terms)


def outer_rows(left_arg, right_arg):
    return lax.dot_general(
        left_arg, right_arg, (((1,), (1,)), ((), ())), preferred_element_type=jnp.float32
    )


def dense_kernel(grid, rep_size, *refs):
    dense_ref, cot_ref, up_ref, down_ref, bias_ref = refs[:5]
    out_ref, back_ref, sums_ref, up_out, down_out = refs[5:10]
    (
        dense_all,
        cot_all,
        up_full,
        down_full,
        inputs_cut,
        hidden_cut,
        slope,
        hidden_grad,
        hidden_round,
        wide_grad,
        up_grad,
        down_grad,
        up_x,
        down_x,
        up_z,
        down_z,
        up_own,
        down_own,
        out_part,
        back_part,
        out_got,
        back_got,
        send_array,
        recv_array,
        local_array,
    ) = refs[10:]
    sends, recvs, locals_ = (
        Semaphores(send_array),
        Semaphores(recv_array),
        Semaphores(local_array),
    )
    g = grid.locate()
    z_size, x_size = g.z_size, g.x_size
    shard_size = z_size * x_size
    rep, shard = lax.axis_index("rep"), lax.axis_index("shard")
    tokens, features = dense_ref.shape
    rows, width = up_ref.shape
    units = down_ref.shape[0]
    total = rep_size * tokens
    copies, moves = {}, {}
    place = lambda j, i: (lax.rem(g.z + z_size - j, z_size), lax.rem(g.x + x_size - i, x_size))
    peer = lambda k: (lax.rem(rep + k, rep_size), shard)
    split = lambda n: (n // x_size, n % x_size)

    def launch(key, source, target, device):
        copy = remote(source, target, sends.take(), recvs.take(), device)
        copy.start()
        copies[key] = copy

    barrier = pltpu.get_barrier_semaphore()
    partners = [g.device(dz=k) for k in range(1, z_size)]
    partners += [g.device(dx=k) for k in range(1, x_size)]
    partners += [peer(k) for k in range(1, rep_size)]
    for partner in partners:
        pl.semaphore_signal(barrier, inc=1, device_id=partner, device_id_type=MESH)
    pl.semaphore_wait(barrier, len(partners))

    def spread(name, source, target):
        for k in range(1, rep_size):
            launch((name, k), source, target.at[rep], peer(k))

    def arrived(name, size):
        for k in range(1, size):
            copies[name, k].wait_recv()

    own = {"u": up_ref, "d": down_ref}
    full = {"u": up_full, "d": down_full}

    def send_z(t):
        for k in range(1, z_size):
            launch(("z" + t, k), own[t], full[t].at[g.z, g.x], g.device(dz=k))

    def send_x(t, j):
        if j > 0:
            copies["z" + t, j].wait_recv()
        here = place(j, 0)
        source = own[t] if j == 0 else full[t].at[here]
        for i in range(1, x_size):
            launch(("x" + t, j, i), source, full[t].at[here], g.device(dx=i))

    def whole(t):
        for j in range(z_size):
            for i in range(1, x_size):
                copies["x" + t, j, i].wait_recv()

    spread("dense", dense_ref, dense_all)
    send_z("u")
    send_x("u", 0)
    spread("cot", cot_ref, cot_all)
    dense_all[rep] = dense_ref[...]
    cot_all[rep] = cot_ref[...]
    up_full[g.z, g.x] = up_ref[...]
    down_full[g.z, g.x] = down_ref[...]
    arrived("dense", rep_size)

    @pl.loop(0, rep_size)
    def _(b):
        values = dense_all[b].astype(jnp.float32)
        for s in range(shard_size):
            inputs_cut[s, b] = values[:, s * rows : (s + 1) * rows].astype(jnp.bfloat16)

    for j in range(1, z_size):
        send_x("u", j)
        if j == 1:
            send_z("d")
            send_x("d", 0)
    whole("u")

    @pl.loop(0, rep_size)
    def _(b):
        pre = jnp.broadcast_to(bias_ref[...], (tokens, width))
        for s in range(shard_size):
            pre = pre + matmul(inputs_cut[s, b], up_full[split(s)])
        normal_cdf = 0.5 * (1.0 + lax.erf(pre * 0.7071067811865476))
        density = jnp.exp(-0.5 * pre * pre) * 0.3989422804014327
        slope[b] = normal_cdf + pre * density
        hidden = pre * normal_cdf
        for s in range(shard_size):
            hidden_cut[s, b] = hidden[:, s * units : (s + 1) * units].astype(jnp.bfloat16)

    for j in range(1, z_size):
        send_x("d", j)
    arrived("cot", rep_size)

    def term(target, left, right):
        @pl.loop(0, shard_size)
        def _(s):
            one = left[s].reshape(total, left.shape[-1])
            two = right[...].reshape(total, right.shape[-1])
            value = inner_rows(one, two)
            target[lax.div(s, x_size), lax.rem(s, x_size)] = value.astype(jnp.bfloat16)

    terms = {"u": up_grad, "d": down_grad}
    got_x, got_z = {"u": up_x, "d": down_x}, {"u": up_z, "d": down_z}
    owned, outs = {"u": up_own, "d": down_own}, {"u": up_out, "d": down_out}

    def reduce_x(t):
        for k in range(1, x_size):
            other = lax.rem(g.x + k, x_size)
            for n in range(z_size):
                launch(
                    ("rx" + t, k, n),
                    terms[t].at[lax.rem(g.z + n, z_size), other],
                    got_x[t].at[k - 1, lax.rem(g.z + n, z_size)],
                    g.device(dx=k),
                )

    def reduce_z(t):
        for n in list(range(1, z_size)) + [0]:
            there = lax.rem(g.z + n, z_size)
            for k in range(1, x_size):
                for m in range(z_size) if n == 1 else ():
                    copies["rx" + t, k, m].wait_recv()
            value = terms[t][there, g.x].astype(jnp.float32)
            for k in range(1, x_size):
                value = value + got_x[t][k - 1, there].astype(jnp.float32)
            terms[t][there, g.x] = value.astype(jnp.bfloat16)
            if n > 0:
                launch(("rz" + t, n), terms[t].at[there, g.x], got_z[t].at[n - 1], g.device(dz=n))

    def reduce_end(t):
        arrived("rz" + t, z_size)
        value = terms[t][g.z, g.x].astype(jnp.float32)
        for k in range(1, z_size):
            value = value + got_z[t][k - 1].astype(jnp.float32)
        owned[t][...] = value.astype(jnp.bfloat16)
        spread("own" + t, owned[t], outs[t])
        copy = pltpu.make_async_copy(owned[t], outs[t].at[rep], locals_.take())
        copy.start()
        moves[t] = copy

    term(down_grad, hidden_cut, cot_all)
    reduce_x("d")
    whole("d")

    for s in range(shard_size):
        value = outer_rows(cot_all[...].reshape(total, features), down_full[split(s)])
        hidden_grad[:, :, s * units : (s + 1) * units] = value.reshape(rep_size, tokens, units)
    sums_ref[...] = jnp.zeros_like(sums_ref)

    @pl.loop(0, rep_size)
    def _(b):
        value = hidden_grad[b] * slope[b]
        sums_ref[...] += jnp.sum(value, axis=0, keepdims=True)
        hidden_round[b] = value.astype(jnp.bfloat16)

    for s in range(shard_size):
        value = outer_rows(hidden_round[...].reshape(total, width), up_full[split(s)])
        wide_grad[:, :, s * rows : (s + 1) * rows] = value.reshape(rep_size, tokens, rows)

    def scatter(name, part, got):
        for k in range(1, rep_size):
            there = lax.rem(rep + k, rep_size)
            launch((name, k), part.at[there], got.at[k - 1], peer(k))

    def collect(name, part, got, target):
        arrived(name, rep_size)
        value = part[rep].astype(jnp.float32)
        for k in range(1, rep_size):
            value = value + got[k - 1].astype(jnp.float32)
        target[...] = value

    @pl.loop(0, rep_size)
    def _(b):
        back_part[b] = wide_grad[b].astype(jnp.bfloat16)

    scatter("back", back_part, back_got)
    term(up_grad, inputs_cut, hidden_round)
    reduce_x("u")

    @pl.loop(0, rep_size)
    def _(b):
        value = matmul(hidden_cut[0, b], down_full[split(0)])
        for s in range(1, shard_size):
            value = value + matmul(hidden_cut[s, b], down_full[split(s)])
        out_part[b] = value.astype(jnp.bfloat16)

    scatter("out", out_part, out_got)
    reduce_z("d")
    collect("back", back_part, back_got, back_ref)
    collect("out", out_part, out_got, out_ref)
    reduce_z("u")
    reduce_end("d")
    reduce_end("u")
    for t in ("d", "u"):
        arrived("own" + t, rep_size)
        moves[t].wait()
    for copy in copies.values():
        copy.wait_send()


def dense_step(grid, rep_size, dense_input, cotangent, up_block, down_block, bias):
    z, x = grid.z_size, grid.x_size
    tokens, features = dense_input.shape
    rows, width = up_block.shape
    units = down_block.shape[0]
    low, high = jnp.bfloat16, jnp.float32
    vmem = lambda dtype, *shape: pltpu.VMEM(shape, dtype)
    total = 4 * (rep_size - 1) + 2 * ((z - 1) + z * (x - 1))
    total += 2 * (z * (x - 1) + (z - 1) + (rep_size - 1))
    shape = lambda dtype, *sizes: jax.ShapeDtypeStruct(sizes, dtype)
    return pl.pallas_call(
        functools.partial(dense_kernel, grid, rep_size),
        out_shape=[
            shape(high, tokens, features),
            shape(high, tokens, features),
            shape(high, 1, width),
            shape(low, rep_size, rows, width),
            shape(low, rep_size, units, features),
        ],
        in_specs=[pl.BlockSpec(memory_space=pltpu.VMEM)] * 5,
        out_specs=[pl.BlockSpec(memory_space=pltpu.VMEM)] * 3
        + [pl.BlockSpec(memory_space=pl.ANY)] * 2,
        scratch_shapes=[
            vmem(low, rep_size, tokens, features),
            vmem(low, rep_size, tokens, features),
            vmem(low, z, x, rows, width),
            vmem(low, z, x, units, features),
            vmem(low, z * x, rep_size, tokens, rows),
            vmem(low, z * x, rep_size, tokens, units),
            vmem(high, rep_size, tokens, width),
            vmem(high, rep_size, tokens, width),
            vmem(low, rep_size, tokens, width),
            vmem(high, rep_size, tokens, features),
            vmem(low, z, x, rows, width),
            vmem(low, z, x, units, features),
            vmem(low, x - 1, z, rows, width),
            vmem(low, x - 1, z, units, features),
            vmem(low, z - 1, rows, width),
            vmem(low, z - 1, units, features),
            vmem(low, rows, width),
            vmem(low, units, features),
            vmem(low, rep_size, tokens, features),
            vmem(low, rep_size, tokens, features),
            vmem(low, rep_size - 1, tokens, features),
            vmem(low, rep_size - 1, tokens, features),
            pltpu.SemaphoreType.DMA((total,)),
            pltpu.SemaphoreType.DMA((total,)),
            pltpu.SemaphoreType.DMA((2,)),
        ],
        compiler_params=pltpu.CompilerParams(
            collective_id=2, has_side_effects=True, vmem_limit_bytes=DENSE_VMEM
        ),
        name="dense_step",
    )(dense_input, cotangent, up_block, down_block, bias)


def shards(
    rep_size,
    shard_size,
    hidden_in,
    cotangent,
    segment_ids,
    attn_weight,
    attn_moments,
    up_weight,
    up_moments,
    down_weight,
    down_moments,
    vectors,
    vector_moments,
):
    grid = Grid(rep_size, shard_size)
    rep = lax.axis_index("rep")
    tokens, features = hidden_in.shape
    rows, width = up_weight.shape
    units = width // (shard_size * rep_size)
    own_cols = shard_size * units
    attn_block = attn_weight.astype(jnp.bfloat16)
    attn_split = Split(*attn_block.shape, grid.y_size)
    attn_wide, vector_wide = gather_params(
        grid, [attn_split], [attn_split.pad(attn_block)], vectors.astype(jnp.bfloat16)
    )
    attn_full = attn_wide[:, :, :rows].reshape(-1, width)
    vector_full = vector_wide.transpose(2, 0, 1, 3).reshape(vectors.shape[0], -1)

    mine = lambda values, axis: lax.dynamic_index_in_dim(values, rep, axis, keepdims=False)
    up_block = mine(
        up_weight.reshape(rows, shard_size, rep_size, units), 2
    ).reshape(rows, own_cols).astype(jnp.bfloat16)
    down_block = mine(down_weight.reshape(rep_size, units, features), 0).astype(jnp.bfloat16)
    bias = mine(
        vector_full[8:].astype(jnp.float32).reshape(shard_size, rep_size, units), 1
    ).reshape(1, own_cols)

    residual, dense_input, stored = attention_forward(
        hidden_in[None], segment_ids, attn_full, vector_full
    )
    dense_out, dense_input_grad, unit_sums, up_slices, down_slices = dense_step(
        grid, rep_size, dense_input, cotangent, up_block, down_block, bias
    )
    block_out = (residual + dense_out + vector_full[7].astype(jnp.float32)).astype(jnp.bfloat16)
    input_grad, small_rows, attn_input, joined_round, attended, resid_round = attention_backward(
        cotangent[None], segment_ids, stored, attn_full, vector_full, dense_input_grad
    )
    unit_rows = lax.dynamic_update_index_in_dim(
        jnp.zeros((shard_size, rep_size, units), jnp.float32),
        unit_sums.reshape(shard_size, units),
        rep,
        1,
    ).reshape(-1, features)
    vector_terms = jnp.concatenate([small_rows, unit_rows], axis=0)
    attn_term = jnp.concatenate(
        [inner_rows(attn_input, joined_round), inner_rows(attended, resid_round)], axis=1
    )
    grads = [
        attn_split.pad(
            attn_term.astype(jnp.bfloat16).reshape((grid.z_size, grid.x_size, rows, width))
        )
    ]
    attn_owned, vector_total = reduce_grads(grid, [attn_split], grads, vector_terms)
    attn_grad = attn_owned[:rows].astype(jnp.float32)
    up_grad = (
        up_slices.reshape(rep_size, rows, shard_size, units)
        .transpose(1, 2, 0, 3)
        .reshape(rows, width)
        .astype(jnp.float32)
    )
    down_grad = down_slices.reshape(-1, features).astype(jnp.float32)
    own_width = vectors.shape[1]
    vector_own = lax.dynamic_slice_in_dim(
        vector_total, lax.axis_index("shard") * own_width, own_width, 1
    )
    new_attn, attn_next = adam_update(attn_weight, attn_moments, attn_grad, weight_decay)
    new_up, up_next = adam_update(up_weight, up_moments, up_grad, weight_decay)
    new_down, down_next = adam_update(down_weight, down_moments, down_grad, weight_decay)
    new_vectors, vector_next = adam_update(vectors, vector_moments, vector_own, 0.0)
    return (
        block_out,
        input_grad[0],
        attn_grad,
        up_grad,
        down_grad,
        vector_own,
        new_attn,
        attn_next,
        new_up,
        up_next,
        new_down,
        down_next,
        new_vectors,
        vector_next,
    )


def solution(mesh):
    in_specs = (
        P(("rep", "shard"), None),
        P(("rep", "shard"), None),
        P(("rep", "shard"), None),
        P("shard", None),
        P(None, "shard", None),
        P("shard", None),
        P(None, "shard", None),
        P("shard", None),
        P(None, "shard", None),
        P(None, "shard"),
        P(None, None, "shard"),
    )
    out_specs = (
        P(("rep", "shard"), None),
        P(("rep", "shard"), None),
        P("shard", None),
        P("shard", None),
        P("shard", None),
        P(None, "shard"),
        P("shard", None),
        P(None, "shard", None),
        P("shard", None),
        P(None, "shard", None),
        P("shard", None),
        P(None, "shard", None),
        P(None, "shard"),
        P(None, None, "shard"),
    )
    body = functools.partial(shards, mesh.shape["rep"], mesh.shape["shard"])
    return jax.shard_map(body, mesh=mesh, in_specs=in_specs, out_specs=out_specs, check_vma=False)
```

```python
import functools

import jax
import jax.numpy as jnp
from jax import lax
from jax.experimental import pallas as pl
from jax.experimental.pallas import tpu as pltpu
from jax.sharding import PartitionSpec as P

HEAD_DIM = 64
ADAM_STEP = 3
MESH = pl.DeviceIdType.MESH


beta_one = 0.9
beta_two = 0.999
adam_eps = 1e-08
learn_rate = 0.25
weight_decay = 0.1


def matmul(left_arg, right_arg):
    return jnp.dot(left_arg, right_arg, preferred_element_type=jnp.float32)


def inner_rows(left_arg, right_arg):
    return lax.dot_general(
        left_arg, right_arg, (((0,), (0,)), ((), ())), preferred_element_type=jnp.float32
    )


def product(pattern, left_arg, right_arg):
    return jnp.einsum(pattern, left_arg, right_arg, preferred_element_type=jnp.float32)


def normalize(values):
    average = jnp.mean(values, axis=-1, keepdims=True)
    centred = values - average
    inv_std = lax.rsqrt(jnp.mean(centred * centred, axis=-1, keepdims=True) + 1e-05)
    return (centred * inv_std, inv_std)


def normalize_back(grad_in, normed, inv_std, gain_row):
    scaled = grad_in * gain_row
    return inv_std * (
        scaled
        - jnp.mean(scaled, axis=-1, keepdims=True)
        - normed * jnp.mean(scaled * normed, axis=-1, keepdims=True)
    )


def allowed(segments):
    row_count = segments.shape[-1]
    causal = lax.broadcasted_iota(jnp.int32, (row_count, row_count), 0) >= lax.broadcasted_iota(
        jnp.int32, (row_count, row_count), 1
    )
    same_doc = segments[:, :, None] == segments[:, None, :]
    return jnp.logical_and(same_doc, causal)[:, None, :, :]


def scores_of(queries, keys_all, segments):
    logits = product("bqhe,bkhe->bhqk", queries, keys_all) * HEAD_DIM ** (-0.5)
    return jnp.where(allowed(segments), logits, -1e30)


def attention_forward(activations, segments, attn_full, vector_full):
    batch_size, row_count, features = activations.shape
    head_count = features // HEAD_DIM
    head_shape = (batch_size, row_count, head_count, HEAD_DIM)
    vector_rows = vector_full.astype(jnp.float32)
    inputs_flat = activations.astype(jnp.float32).reshape(batch_size * row_count, features)
    normed_one, inv_one = normalize(inputs_flat)
    attn_input = (normed_one * vector_rows[0] + vector_rows[1]).astype(jnp.bfloat16)
    projected = matmul(attn_input, attn_full[:, : 3 * features])
    queries = (projected[:, :features] + vector_rows[2]).astype(jnp.bfloat16).reshape(head_shape)
    keys_all = projected[:, features : 2 * features].astype(jnp.bfloat16).reshape(head_shape)
    values_all = (
        (projected[:, 2 * features :] + vector_rows[3]).astype(jnp.bfloat16).reshape(head_shape)
    )
    logits = scores_of(queries, keys_all, segments)
    row_max = jnp.max(logits, axis=-1, keepdims=True)
    exponent = jnp.exp(logits - row_max)
    totals = jnp.sum(exponent, axis=-1, keepdims=True)
    log_total = row_max + jnp.log(totals)
    soft_probs = (exponent / totals).astype(jnp.bfloat16)
    attended = (
        product("bhqk,bkhe->bqhe", soft_probs, values_all)
        .reshape(batch_size * row_count, features)
        .astype(jnp.bfloat16)
    )
    residual = inputs_flat + matmul(attended, attn_full[:, 3 * features :]) + vector_rows[4]
    normed_two, inv_two = normalize(residual)
    dense_input = (normed_two * vector_rows[5] + vector_rows[6]).astype(jnp.bfloat16)
    stored = (
        normed_one,
        inv_one,
        attn_input,
        queries,
        keys_all,
        values_all,
        log_total,
        attended,
        normed_two,
        inv_two,
    )
    return (residual, dense_input, stored)


def attention_backward(cotangent, segments, stored, attn_full, vector_full, dense_input_grad):
    (
        normed_one,
        inv_one,
        attn_input,
        queries,
        keys_all,
        values_all,
        log_total,
        attended,
        normed_two,
        inv_two,
    ) = stored
    batch_size, row_count, features = cotangent.shape
    head_count = features // HEAD_DIM
    head_shape = (batch_size, row_count, head_count, HEAD_DIM)
    vector_rows = vector_full.astype(jnp.float32)
    out_float = cotangent.reshape(batch_size * row_count, features).astype(jnp.float32)
    resid_grad = out_float + normalize_back(dense_input_grad, normed_two, inv_two, vector_rows[5])
    resid_round = resid_grad.astype(jnp.bfloat16)
    attended_grad = lax.dot_general(
        resid_round,
        attn_full[:, 3 * features :],
        (((1,), (1,)), ((), ())),
        preferred_element_type=jnp.float32,
    ).astype(jnp.bfloat16)
    heads_grad = attended_grad.reshape(head_shape)
    logits = scores_of(queries, keys_all, segments)
    recomputed = jnp.exp(logits - log_total)
    prob_round = recomputed.astype(jnp.bfloat16)
    prob_grad = product("bqhe,bkhe->bhqk", heads_grad, values_all)
    delta_row = product("bqhe,bqhe->bhq", heads_grad, attended.reshape(head_shape))[..., None]
    logit_grad = (recomputed * (prob_grad - delta_row)).astype(jnp.bfloat16)
    scale_factor = HEAD_DIM ** (-0.5)
    query_grad = product("bhqk,bkhe->bqhe", logit_grad, keys_all) * scale_factor
    key_grad = product("bhqk,bqhe->bkhe", logit_grad, queries) * scale_factor
    value_grad = product("bhqk,bqhe->bkhe", prob_round, heads_grad)
    joined_grad = jnp.concatenate(
        [
            query_grad.reshape(-1, features),
            key_grad.reshape(-1, features),
            value_grad.reshape(-1, features),
        ],
        axis=1,
    )
    joined_round = joined_grad.astype(jnp.bfloat16)
    attn_input_grad = lax.dot_general(
        joined_round,
        attn_full[:, : 3 * features],
        (((1,), (1,)), ((), ())),
        preferred_element_type=jnp.float32,
    )
    input_grad = (
        (resid_grad + normalize_back(attn_input_grad, normed_one, inv_one, vector_rows[0]))
        .astype(jnp.bfloat16)
        .reshape(batch_size, row_count, features)
    )
    small_rows = jnp.stack(
        [
            jnp.sum(attn_input_grad * normed_one, axis=0),
            jnp.sum(attn_input_grad, axis=0),
            jnp.sum(joined_grad[:, :features], axis=0),
            jnp.sum(joined_grad[:, 2 * features :], axis=0),
            jnp.sum(resid_grad, axis=0),
            jnp.sum(dense_input_grad * normed_two, axis=0),
            jnp.sum(dense_input_grad, axis=0),
            jnp.sum(out_float, axis=0),
        ]
    )
    return (input_grad, small_rows, attn_input, joined_round, attended, resid_round)


CORES = 2
ROW_UNIT = 16
LANE_UNIT = 128
GATHER_VMEM = 16 * 2**20
REDUCE_VMEM = 32 * 2**20
DENSE_VMEM = 60 * 2**20
ADAM_VMEM = 56 * 2**20


class Grid:
    def __init__(self, rep_size, shard_size):
        self.cores = CORES
        self.y_size = rep_size // CORES
        self.x_size = self.y_size if shard_size % self.y_size == 0 else 1
        self.z_size = shard_size // self.x_size

    def locate(self):
        rep = lax.axis_index("rep")
        shard = lax.axis_index("shard")
        self.y, self.c = lax.div(rep, CORES), lax.rem(rep, CORES)
        self.z, self.x = lax.div(shard, self.x_size), lax.rem(shard, self.x_size)
        return self

    def device(self, dz=0, dx=0, dy=0, dc=0):
        rep = lax.rem(self.y + dy, self.y_size) * CORES + lax.rem(self.c + dc, CORES)
        shard = lax.rem(self.z + dz, self.z_size) * self.x_size + lax.rem(self.x + dx, self.x_size)
        return (rep, shard)

    def partners(self):
        found = [self.device(dz=k) for k in range(1, self.z_size)]
        found += [self.device(dx=k) for k in range(1, self.x_size)]
        found += [self.device(dy=k) for k in range(1, self.y_size)]
        return found + [self.device(dc=1)]

    def greet(self):
        barrier = pltpu.get_barrier_semaphore()
        partners = self.partners()
        for partner in partners:
            pl.semaphore_signal(barrier, inc=1, device_id=partner, device_id_type=MESH)
        pl.semaphore_wait(barrier, len(partners))


class Split:
    def __init__(self, rows, columns, y_size, share=0.7, array=0, chunk=0, chunks=1):
        self.rows, self.columns, self.array = rows, columns, array
        self.by_lane = columns % (2 * LANE_UNIT) == 0
        unit = LANE_UNIT if self.by_lane else ROW_UNIT
        extent = columns if self.by_lane else rows
        padded = -(-extent // (2 * unit)) * 2 * unit
        if not self.by_lane:
            self.rows = padded
        pairs = padded // (2 * unit)
        chunks = max(1, min(chunks, pairs // (y_size + 1)))
        self.chunks = chunks
        starts = [n * (pairs // chunks) + min(n, pairs % chunks) for n in range(chunks + 1)]
        units = starts[chunk + 1] - starts[chunk]
        self.unit = unit
        self.start = 2 * unit * starts[chunk]
        self.half = units * unit
        taken = min(max(1, int(units * share / y_size + 0.5)), (units - 1) // y_size)
        self.a_size = taken * unit
        self.b_start = y_size * self.a_size
        self.b_size = self.half - self.b_start

    def chunked(self, y_size, share, array, chunks):
        found = Split(self.rows, self.columns, y_size, share, array, 0, chunks)
        return [found] + [
            Split(self.rows, self.columns, y_size, share, array, n, chunks)
            for n in range(1, found.chunks)
        ]

    def block(self):
        return (self.rows, self.columns)

    def shape(self, size):
        return (self.rows, size) if self.by_lane else (size, self.columns)

    def cut(self, start, size):
        window = pl.ds(pl.multiple_of(self.start + start, self.unit), size)
        return (slice(None), window) if self.by_lane else (window, slice(None))

    def piece_a(self, y, c):
        return self.cut(c * self.half + y * self.a_size, self.a_size)

    def piece_b(self, c):
        return self.cut(c * self.half + self.b_start, self.b_size)

    def piece_half(self, c):
        return self.cut(c * self.half, self.half)

    def pad(self, values):
        extra = self.rows - values.shape[-2]
        if extra == 0:
            return values
        return jnp.pad(values, [(0, 0)] * (values.ndim - 2) + [(0, extra), (0, 0)])


def remote(source, target, send, recv, device):
    return pltpu.make_async_remote_copy(
        src_ref=source,
        dst_ref=target,
        send_sem=send,
        recv_sem=recv,
        device_id=device,
        device_id_type=MESH,
    )


class Semaphores:
    def __init__(self, array):
        self.array, self.used = array, 0

    def take(self):
        self.used += 1
        return self.array.at[self.used - 1]


def gather_kernel(grid, splits, *refs):
    count = len(splits)
    own, full = refs[: count + 1], refs[count + 1 : 2 * count + 2]
    send_array, recv_array, local_array = refs[2 * count + 2 :]
    sends, recvs, locals_ = (
        Semaphores(send_array),
        Semaphores(recv_array),
        Semaphores(local_array),
    )
    g = grid.locate()
    z_size, x_size, y_size = g.z_size, g.x_size, g.y_size
    started = []
    copies = {}

    def launch(key, source, target, device):
        copy = remote(source, target, sends.take(), recvs.take(), device)
        copy.start()
        copies[key] = copy

    place = lambda j, i: (lax.rem(g.z + z_size - j, z_size), lax.rem(g.x + x_size - i, x_size))

    def windows(t):
        if t == count:
            return [(slice(None), slice(None))]
        return [splits[t].piece_a(g.y, g.c), splits[t].piece_b(g.c)]

    g.greet()
    order = [count] + list(range(count))

    def stage_z(t):
        for k in range(1, z_size):
            for p, window in enumerate(windows(t)):
                launch(
                    ("z", t, p, k),
                    own[t].at[window],
                    full[t].at[(g.z, g.x) + window],
                    g.device(dz=k),
                )
        copy = pltpu.make_async_copy(own[t], full[t].at[g.z, g.x], locals_.take())
        copy.start()
        started.append(copy)

    def unit_x(t, j):
        for p, window in enumerate(windows(t)):
            here = place(j, 0) + window
            if j > 0:
                copies["z", t, p, j].wait_recv()
            source = own[t].at[window] if j == 0 else full[t].at[here]
            for i in range(1, x_size):
                launch(("x", t, p, j, i), source, full[t].at[here], g.device(dx=i))
            if t < count and p == 0 and j > 0:
                for k in range(1, y_size):
                    launch(("y", t, j, 0, k), source, full[t].at[here], g.device(dy=k))

    def unit_y(t, j):
        for i in range(1, x_size):
            for p, window in enumerate(windows(t)):
                copies["x", t, p, j, i].wait_recv()
                if t < count and p == 0:
                    here = full[t].at[place(j, i) + window]
                    for k in range(1, y_size):
                        launch(("y", t, j, i, k), here, here, g.device(dy=k))

    def unit_core(t, j):
        if t == count:
            return
        for i in range(x_size):
            if (j, i) == (0, 0):
                continue
            for k in range(1, y_size):
                copies["y", t, j, i, k].wait_recv()
            here = full[t].at[place(j, i) + splits[t].piece_half(g.c)]
            launch(("c", t, j, i), here, here, g.device(dc=1))

    for t in order:
        stage_z(t)
    units = [(t, j) for t in order for j in range(z_size)]
    for step in range(len(units) + 2):
        for lag, unit in enumerate((unit_x, unit_y, unit_core)):
            if 0 <= step - lag < len(units):
                unit(*units[step - lag])
    for key, copy in copies.items():
        if key[0] == "c":
            copy.wait_recv()
        copy.wait_send()
    for copy in started:
        copy.wait()


def gather_params(grid, splits, blocks, vector_block):
    z, x, y = grid.z_size, grid.x_size, grid.y_size
    per_tensor = 2 * (z - 1) + 2 * z * (x - 1) + (z * x - 1) * y
    total = len(splits) * per_tensor + (z - 1) + z * (x - 1)
    shapes = [
        jax.ShapeDtypeStruct((z, x) + split.block(), jnp.bfloat16) for split in splits
    ] + [jax.ShapeDtypeStruct((z, x) + vector_block.shape, jnp.bfloat16)]
    return pl.pallas_call(
        functools.partial(gather_kernel, grid, splits),
        out_shape=shapes,
        in_specs=[pl.BlockSpec(memory_space=pltpu.VMEM)] * (len(splits) + 1),
        out_specs=[pl.BlockSpec(memory_space=pl.ANY)] * (len(splits) + 1),
        scratch_shapes=[
            pltpu.SemaphoreType.DMA((total,)),
            pltpu.SemaphoreType.DMA((total,)),
            pltpu.SemaphoreType.DMA((len(splits) + 1,)),
        ],
        compiler_params=pltpu.CompilerParams(
            collective_id=0, has_side_effects=True, vmem_limit_bytes=GATHER_VMEM
        ),
        name="gather_params",
    )(*blocks, vector_block)


def plus(left_arg, right_arg):
    return left_arg.astype(jnp.float32) + right_arg.astype(jnp.float32)


def reduce_kernel(grid, splits, *refs):
    count = len(splits)
    arrays = splits[-1].array + 1
    vector_in, vector_out = refs[arrays], refs[2 * arrays + 1]
    grads = [refs[split.array] for split in splits]
    outs = [refs[arrays + 1 + split.array] for split in splits]
    scratch = refs[2 * arrays + 2 :]
    per = 12
    buffers = [scratch[per * t : per * (t + 1)] for t in range(count)]
    v_core, v_y, v_x, v_z, v_one, v_two, v_three, send_array, recv_array, local_array = scratch[
        per * count :
    ]
    sends, recvs, locals_ = (
        Semaphores(send_array),
        Semaphores(recv_array),
        Semaphores(local_array),
    )
    g = grid.locate()
    z_size, x_size, y_size = g.z_size, g.x_size, g.y_size
    copies, moves = {}, {}

    def launch(key, source, target, device):
        copy = remote(source, target, sends.take(), recvs.take(), device)
        copy.start()
        copies[key] = copy

    def move(key, source, target):
        copy = pltpu.make_async_copy(source, target, locals_.take())
        copy.start()
        moves[key] = copy

    def each_block(body):
        @pl.loop(0, z_size * x_size)
        def _(index):
            body(lax.div(index, x_size), lax.rem(index, x_size))

    everything = (slice(None), slice(None))
    other_y = lambda k: lax.rem(g.y + k, y_size)
    other_x = lambda k: lax.rem(g.x + k, x_size)
    other_z = lambda k: lax.rem(g.z + k, z_size)

    def stage_core(t):
        acc_a, acc_b, got_a, got_b = buffers[t][:4]
        split = splits[t]
        for q in range(y_size):
            launch(
                ("ca", t, q),
                grads[t].at[everything + split.piece_a(q, 1 - g.c)],
                got_a.at[q],
                g.device(dc=1),
            )
            move(("la", t, q), grads[t].at[everything + split.piece_a(q, g.c)], acc_a.at[q])
        launch(
            ("cb", t),
            grads[t].at[everything + split.piece_b(1 - g.c)],
            got_b,
            g.device(dc=1),
        )
        move(("lb", t), grads[t].at[everything + split.piece_b(g.c)], acc_b)

    def stage_y(t):
        acc_a, acc_b, got_a, got_b, got_y = buffers[t][:5]
        for q in range(y_size):
            copies["ca", t, q].wait_recv()
            moves["la", t, q].wait()

            def add_a(i, j, q=q):
                acc_a[q, i, j] = plus(acc_a[q, i, j], got_a[q, i, j]).astype(jnp.bfloat16)

            each_block(add_a)
        for k in range(1, y_size):
            launch(("ya", t, k), acc_a.at[other_y(k)], got_y.at[k - 1], g.device(dy=k))
        copies["cb", t].wait_recv()
        moves["lb", t].wait()

        def add_b(i, j):
            acc_b[i, j] = plus(acc_b[i, j], got_b[i, j]).astype(jnp.bfloat16)

        each_block(add_b)
        for k in range(1, x_size):
            launch(
                ("xb", t, k), acc_b.at[:, other_x(k)], buffers[t][6].at[k - 1], g.device(dx=k)
            )

    def stage_x(t):
        acc_a, got_y, got_xa = buffers[t][0], buffers[t][4], buffers[t][5]
        for k in range(1, y_size):
            copies["ya", t, k].wait_recv()

        def add(i, j):
            value = acc_a[g.y, i, j].astype(jnp.float32)
            for k in range(1, y_size):
                value = plus(value, got_y[k - 1, i, j])
            acc_a[g.y, i, j] = value.astype(jnp.bfloat16)

        each_block(add)
        for k in range(1, x_size):
            launch(
                ("xa", t, k), acc_a.at[g.y, :, other_x(k)], got_xa.at[k - 1], g.device(dx=k)
            )

    def stage_z(t):
        acc_a, acc_b = buffers[t][:2]
        got_xa, got_xb, got_za, got_zb = buffers[t][5:9]
        for k in range(1, x_size):
            copies["xb", t, k].wait_recv()
            copies["xa", t, k].wait_recv()

        @pl.loop(0, z_size)
        def _(i):
            value_a = acc_a[g.y, i, g.x].astype(jnp.float32)
            for k in range(1, x_size):
                value_a = plus(value_a, got_xa[k - 1, i])
            acc_a[g.y, i, g.x] = value_a.astype(jnp.bfloat16)
            value_b = acc_b[i, g.x].astype(jnp.float32)
            for k in range(1, x_size):
                value_b = plus(value_b, got_xb[k - 1, i])
            acc_b[i, g.x] = value_b.astype(jnp.bfloat16)

        for k in range(1, z_size):
            launch(
                ("zb", t, k), acc_b.at[other_z(k), g.x], got_zb.at[k - 1], g.device(dz=k)
            )
            launch(
                ("za", t, k),
                acc_a.at[g.y, other_z(k), g.x],
                got_za.at[k - 1],
                g.device(dz=k),
            )

    def stage_final(t):
        acc_a, acc_b = buffers[t][:2]
        got_za, got_zb, final_a, ring_b, final_b = buffers[t][7:12]
        split = splits[t]
        for k in range(1, z_size):
            copies["zb", t, k].wait_recv()
        value = acc_b[g.z, g.x].astype(jnp.float32)
        for k in range(1, z_size):
            value = plus(value, got_zb[k - 1])
        ring_b[0] = value.astype(jnp.bfloat16)
        for k in range(1, y_size):
            launch(("yb", t, k), ring_b.at[0], ring_b.at[k], g.device(dy=k))
        for k in range(1, z_size):
            copies["za", t, k].wait_recv()
        value = acc_a[g.y, g.z, g.x].astype(jnp.float32)
        for k in range(1, z_size):
            value = plus(value, got_za[k - 1])
        final_a[...] = value.astype(jnp.bfloat16)
        target = outs[t].at[split.piece_a(g.y, g.c)]
        for k in range(1, y_size):
            launch(("oa", t, k), final_a, target, g.device(dy=k))
        move(("fa", t), final_a, target)

    def stage_share(t):
        ring_b, final_b = buffers[t][10:12]
        split = splits[t]
        for k in range(1, y_size):
            copies["yb", t, k].wait_recv()
        value = ring_b[g.y].astype(jnp.float32)
        for k in range(1, y_size):
            value = plus(value, ring_b[lax.rem(g.y + y_size - k, y_size)])
        final_b[...] = value.astype(jnp.bfloat16)
        move(("fb", t), final_b, outs[t].at[split.piece_b(g.c)])
        for k in range(1, y_size):
            copies["oa", t, k].wait_recv()
        moves["fa", t].wait()
        moves["fb", t].wait()
        half = outs[t].at[split.piece_half(g.c)]
        launch(("h", t), half, half, g.device(dc=1))

    def sum_ring(buffer, place, size):
        value = buffer[place]
        for k in range(1, size):
            value = value + buffer[lax.rem(place + size - k, size)]
        return value

    def vector_step(name, source, got, size, **direction):
        (axis,) = direction
        got[0] = source[...]
        for k in range(1, size):
            launch((name, k), source, got.at[k], g.device(**{axis: k}))

    def vector_sum(name, got, place, size, target):
        for k in range(1, size):
            copies[name, k].wait_recv()
        target[...] = sum_ring(got, place, size)

    g.greet()
    vector_step("vc", vector_in, v_core, CORES, dc=1)
    for t in range(count):
        stage_core(t)
    vector_sum("vc", v_core, g.c, CORES, v_one)
    vector_step("vy", v_one, v_y, y_size, dy=1)
    stages = [stage_y, stage_x, stage_z, stage_final, stage_share]
    for step in range(count + len(stages) - 1):
        for s in range(len(stages)):
            t = step - s
            if 0 <= t < count:
                stages[s](t)
        if step == 0:
            vector_sum("vy", v_y, g.y, y_size, v_two)
            vector_step("vx", v_two, v_x, x_size, dx=1)
        if step == 1:
            vector_sum("vx", v_x, g.x, x_size, v_three)
            vector_step("vz", v_three, v_z, z_size, dz=1)
        if step == 2:
            vector_sum("vz", v_z, g.z, z_size, vector_out)
    for key, copy in copies.items():
        if key[0] == "h":
            copy.wait_recv()
        copy.wait_send()


def reduce_grads(grid, whole, grads, vector_terms):
    z, x, y = grid.z_size, grid.x_size, grid.y_size
    splits = []
    for array, split in enumerate(whole):
        splits += split.chunked(y, 0.58, array, 3)
    scratch = []
    for split in splits:
        a, b = split.shape(split.a_size), split.shape(split.b_size)
        scratch += [
            pltpu.VMEM(shape, jnp.bfloat16)
            for shape in (
                (y, z, x) + a,
                (z, x) + b,
                (y, z, x) + a,
                (z, x) + b,
                (y - 1, z, x) + a,
                (x - 1, z) + a,
                (x - 1, z) + b,
                (z - 1,) + a,
                (z - 1,) + b,
                a,
                (y,) + b,
                b,
            )
        ]
    small = vector_terms.shape
    scratch += [pltpu.VMEM((size,) + small, jnp.float32) for size in (CORES, y, x, z)]
    scratch += [pltpu.VMEM(small, jnp.float32)] * 3
    per_tensor = (y + 1) + (y - 1) + 2 * (x - 1) + 2 * (z - 1) + 2 * (y - 1) + 1
    total = len(splits) * per_tensor + 1 + (y - 1) + (x - 1) + (z - 1)
    scratch += [
        pltpu.SemaphoreType.DMA((total,)),
        pltpu.SemaphoreType.DMA((total,)),
        pltpu.SemaphoreType.DMA((len(splits) * (y + 3),)),
    ]
    return pl.pallas_call(
        functools.partial(reduce_kernel, grid, splits),
        out_shape=[jax.ShapeDtypeStruct(split.block(), jnp.bfloat16) for split in whole]
        + [jax.ShapeDtypeStruct(small, jnp.float32)],
        in_specs=[pl.BlockSpec(memory_space=pl.ANY)] * len(whole)
        + [pl.BlockSpec(memory_space=pltpu.VMEM)],
        out_specs=[pl.BlockSpec(memory_space=pl.ANY)] * len(whole)
        + [pl.BlockSpec(memory_space=pltpu.VMEM)],
        scratch_shapes=scratch,
        compiler_params=pltpu.CompilerParams(
            collective_id=1, has_side_effects=True, vmem_limit_bytes=REDUCE_VMEM
        ),
        name="reduce_grads",
    )(*grads, vector_terms)


def outer_rows(left_arg, right_arg):
    return lax.dot_general(
        left_arg, right_arg, (((1,), (1,)), ((), ())), preferred_element_type=jnp.float32
    )


def dense_kernel(grid, rep_size, *refs):
    dense_ref, cot_ref, up_ref, down_ref, bias_ref = refs[:5]
    out_ref, back_ref, sums_ref, up_out, down_out = refs[5:10]
    (
        dense_all,
        cot_all,
        up_full,
        down_full,
        inputs_cut,
        hidden_cut,
        slope,
        hidden_grad,
        hidden_round,
        wide_grad,
        up_grad,
        down_grad,
        up_x,
        down_x,
        up_z,
        down_z,
        up_own,
        down_own,
        out_part,
        back_part,
        out_core,
        back_core,
        out_y,
        back_y,
        send_array,
        recv_array,
        local_array,
    ) = refs[10:]
    locals_ = Semaphores(local_array)
    g = grid.locate()
    z_size, x_size, y_size = g.z_size, g.x_size, g.y_size
    shard_size = z_size * x_size
    rep = lax.axis_index("rep")
    tokens, features = dense_ref.shape
    rows, width = up_ref.shape
    units = down_ref.shape[0]
    total = rep_size * tokens
    split = lambda n: (n // x_size, n % x_size)
    near = lambda j: lax.rem(g.z + j + z_size, z_size)
    rep_at = lambda dy, dc: lax.rem(g.y + dy, y_size) * CORES + lax.rem(g.c + dc, CORES)
    copies, moves, order = {}, {}, {}

    def when(condition):
        return (lambda body: body()) if condition is True else pl.when(condition)

    def launch(key, source, target, device, sent=True, got=True):
        n = order.setdefault(key, len(order))
        copy = remote(source, target, send_array.at[n], recv_array.at[n], device)
        copies[key] = (copy, sent, got)
        when(sent)(copy.start)

    def arrived(*keys):
        for key in keys:
            copy, _, got = copies[key]
            when(got)(copy.wait_recv)

    barrier = pltpu.get_barrier_semaphore()
    partners = g.partners()
    for partner in partners:
        pl.semaphore_signal(barrier, inc=1, device_id=partner, device_id_type=MESH)
    pl.semaphore_wait(barrier, len(partners))

    own = {"u": up_ref, "d": down_ref}
    full = {"u": up_full, "d": down_full}
    hops = range(z_size - 1)

    def hop(t, k):
        source = own[t] if k == 0 else full[t].at[near(-k), g.x]
        launch(
            ("right" + t, k),
            source,
            full[t].at[near(-k), g.x],
            g.device(dz=1),
            jnp.logical_and(g.z >= k, g.z + 1 < z_size),
            g.z >= k + 1,
        )
        source = own[t] if k == 0 else full[t].at[near(k), g.x]
        launch(
            ("left" + t, k),
            source,
            full[t].at[near(k), g.x],
            g.device(dz=z_size - 1),
            jnp.logical_and(g.z + k < z_size, g.z >= 1),
            g.z + 1 + k < z_size,
        )

    def across(name, t, source, where, held):
        for i in range(1, x_size):
            launch(
                (name + t, i), source, full[t].at[where, g.x], g.device(dx=i), held, held
            )

    def begin(t):
        hop(t, 0)
        across("own", t, own[t], g.z, True)

    def advance(t, k):
        arrived(("right" + t, k), ("left" + t, k))
        if k + 1 < z_size - 1:
            hop(t, k + 1)
        across("r%d" % k, t, full[t].at[near(-k - 1), g.x], near(-k - 1), g.z >= k + 1)
        across("l%d" % k, t, full[t].at[near(k + 1), g.x], near(k + 1), g.z + 1 + k < z_size)

    def whole(t):
        for i in range(1, x_size):
            arrived(("own" + t, i))
            for k in hops:
                arrived(("r%d" % k + t, i), ("l%d" % k + t, i))

    def spread(name, source, target):
        for k in range(1, y_size):
            launch((name, "y", k), source, target.at[rep], g.device(dy=k))
        launch((name, "c", 0), source, target.at[rep], g.device(dc=1))

    def pass_on(name, target):
        for k in range(1, y_size):
            arrived((name, "y", k))
            here = target.at[rep_at(y_size - k, 0)]
            launch((name, "c", k), here, here, g.device(dc=1))

    def spread_end(name):
        for k in range(y_size):
            arrived((name, "c", k))

    spread("dense", dense_ref, dense_all)
    begin("u")
    spread("cot", cot_ref, cot_all)
    dense_all[rep] = dense_ref[...]
    cot_all[rep] = cot_ref[...]
    up_full[g.z, g.x] = up_ref[...]
    down_full[g.z, g.x] = down_ref[...]
    pass_on("dense", dense_all)
    advance("u", 0)
    pass_on("cot", cot_all)
    for k in hops[1:]:
        if k == hops[-1]:
            begin("d")
        advance("u", k)
    spread_end("dense")

    @pl.loop(0, rep_size)
    def _(b):
        values = dense_all[b].astype(jnp.float32)
        for s in range(shard_size):
            inputs_cut[s, b] = values[:, s * rows : (s + 1) * rows].astype(jnp.bfloat16)

    advance("d", 0)
    whole("u")

    @pl.loop(0, rep_size)
    def _(b):
        pre = jnp.broadcast_to(bias_ref[...], (tokens, width))
        for s in range(shard_size):
            pre = pre + matmul(inputs_cut[s, b], up_full[split(s)])
        normal_cdf = 0.5 * (1.0 + lax.erf(pre * 0.7071067811865476))
        density = jnp.exp(-0.5 * pre * pre) * 0.3989422804014327
        slope[b] = normal_cdf + pre * density
        hidden = pre * normal_cdf
        for s in range(shard_size):
            hidden_cut[s, b] = hidden[:, s * units : (s + 1) * units].astype(jnp.bfloat16)

    for k in hops[1:]:
        advance("d", k)
    spread_end("cot")

    def term(target, left, right):
        @pl.loop(0, shard_size)
        def _(s):
            one = left[s].reshape(total, left.shape[-1])
            two = right[...].reshape(total, right.shape[-1])
            value = inner_rows(one, two)
            target[lax.div(s, x_size), lax.rem(s, x_size)] = value.astype(jnp.bfloat16)

    terms = {"u": up_grad, "d": down_grad}
    got_x, got_z = {"u": up_x, "d": down_x}, {"u": up_z, "d": down_z}
    owned, outs = {"u": up_own, "d": down_own}, {"u": up_out, "d": down_out}

    def ranked(n):
        last = z_size - 1
        later = lax.div(lax.div(n + g.z, last) + 1, 2)
        return later * (n - last + g.z) + (1 - later) * (last - n)

    def reduce_x(t):
        for n in range(z_size):
            for k in range(1, x_size):
                other = lax.rem(g.x + k, x_size)
                launch(
                    ("rx" + t, k, n),
                    terms[t].at[ranked(n), other],
                    got_x[t].at[k - 1, ranked(n)],
                    g.device(dx=k),
                )

    def fold(t, n):
        for k in range(1, x_size):
            arrived(("rx" + t, k, n))
        here = ranked(n)
        value = terms[t][here, g.x].astype(jnp.float32)
        for k in range(1, x_size):
            value = value + got_x[t][k - 1, here].astype(jnp.float32)
        terms[t][here, g.x] = value.astype(jnp.bfloat16)

    def pulse(t, step):
        goal = lax.rem(2 * z_size - 1 - step + g.z, z_size)
        sent = g.z <= step
        got = jnp.logical_and(g.z >= 1, g.z <= step + 1)

        def toward(key, goal, sent, got, slot, first, device):
            slot_in = got_z[t].at[slot]

            @pl.when(sent)
            def _():
                if step > 0:

                    @pl.when(jnp.logical_not(first))
                    def _():
                        copies[key, step - 1][0].wait_recv()
                        value = plus(terms[t][goal, g.x], got_z[t][slot])
                        terms[t][goal, g.x] = value.astype(jnp.bfloat16)

            launch((key, step), terms[t].at[goal, g.x], slot_in, device, sent, got)

        toward("pr" + t, goal, sent, got, goal + 1, g.z == 0, g.device(dz=1))
        back = z_size - 1 - g.z
        goal = lax.rem(step + 1 + g.z, z_size)
        sent = back <= step
        got = jnp.logical_and(back >= 1, back <= step + 1)
        toward("pl" + t, goal, sent, got, goal, back == 0, g.device(dz=z_size - 1))

    def reduce_z(t):
        for n in range(z_size):
            fold(t, n)
            if n < z_size - 1:
                pulse(t, n)

    def reduce_end(t):
        last = z_size - 2

        @pl.when(g.z >= 1)
        def _():
            copies["pr" + t, last][0].wait_recv()
            value = plus(terms[t][g.z, g.x], got_z[t][g.z + 1])
            terms[t][g.z, g.x] = value.astype(jnp.bfloat16)

        @pl.when(g.z + 1 < z_size)
        def _():
            copies["pl" + t, last][0].wait_recv()
            value = plus(terms[t][g.z, g.x], got_z[t][g.z])
            terms[t][g.z, g.x] = value.astype(jnp.bfloat16)

        owned[t][...] = terms[t][g.z, g.x]
        spread("own" + t, owned[t], outs[t])
        copy = pltpu.make_async_copy(owned[t], outs[t].at[rep], locals_.take())
        copy.start()
        moves[t] = copy

    term(down_grad, hidden_cut, cot_all)
    reduce_x("d")
    whole("d")

    for s in range(shard_size):
        value = outer_rows(cot_all[...].reshape(total, features), down_full[split(s)])
        hidden_grad[:, :, s * units : (s + 1) * units] = value.reshape(rep_size, tokens, units)
    sums_ref[...] = jnp.zeros_like(sums_ref)

    @pl.loop(0, rep_size)
    def _(b):
        value = hidden_grad[b] * slope[b]
        sums_ref[...] += jnp.sum(value, axis=0, keepdims=True)
        hidden_round[b] = value.astype(jnp.bfloat16)

    for s in range(shard_size):
        value = outer_rows(hidden_round[...].reshape(total, width), up_full[split(s)])
        wide_grad[:, :, s * rows : (s + 1) * rows] = value.reshape(rep_size, tokens, rows)

    def scatter(name, part, got):
        for k in range(y_size):
            launch((name, "c", k), part.at[rep_at(k, 1)], got.at[k], g.device(dc=1))

    def scatter_y(name, part, core, got):
        for k in list(range(1, y_size)) + [0]:
            arrived((name, "c", k))
            there = rep_at(k, 0)
            part[there] = plus(part[there], core[k]).astype(jnp.bfloat16)
            if k > 0:
                launch((name, "y", k), part.at[there], got.at[k - 1], g.device(dy=k))

    def collect(name, part, got, target):
        value = part[rep].astype(jnp.float32)
        for k in range(1, y_size):
            arrived((name, "y", k))
            value = value + got[k - 1].astype(jnp.float32)
        target[...] = value

    @pl.loop(0, rep_size)
    def _(b):
        back_part[b] = wide_grad[b].astype(jnp.bfloat16)

    scatter("back", back_part, back_core)
    term(up_grad, inputs_cut, hidden_round)
    reduce_x("u")
    scatter_y("back", back_part, back_core, back_y)

    @pl.loop(0, rep_size)
    def _(b):
        value = matmul(hidden_cut[0, b], down_full[split(0)])
        for s in range(1, shard_size):
            value = value + matmul(hidden_cut[s, b], down_full[split(s)])
        out_part[b] = value.astype(jnp.bfloat16)

    scatter("out", out_part, out_core)
    reduce_z("d")
    scatter_y("out", out_part, out_core, out_y)
    collect("back", back_part, back_y, back_ref)
    reduce_end("d")
    reduce_z("u")
    pass_on("ownd", down_out)
    collect("out", out_part, out_y, out_ref)
    reduce_end("u")
    pass_on("ownu", up_out)
    for t in ("d", "u"):
        spread_end("own" + t)
        moves[t].wait()
    for copy, sent, _ in copies.values():
        when(sent)(copy.wait_send)


def dense_step(grid, rep_size, dense_input, cotangent, up_block, down_block, bias):
    z, x = grid.z_size, grid.x_size
    tokens, features = dense_input.shape
    rows, width = up_block.shape
    units = down_block.shape[0]
    low, high = jnp.bfloat16, jnp.float32
    vmem = lambda dtype, *shape: pltpu.VMEM(shape, dtype)
    y = grid.y_size
    total = 2 * (2 * y - 1) + 2 * (2 * (z - 1) + (x - 1) * (2 * z - 1))
    total += 2 * (z * (x - 1) + 2 * (z - 1) + 2 * y - 1) + 2 * (2 * y - 1)
    shape = lambda dtype, *sizes: jax.ShapeDtypeStruct(sizes, dtype)
    return pl.pallas_call(
        functools.partial(dense_kernel, grid, rep_size),
        out_shape=[
            shape(high, tokens, features),
            shape(high, tokens, features),
            shape(high, 1, width),
            shape(low, rep_size, rows, width),
            shape(low, rep_size, units, features),
        ],
        in_specs=[pl.BlockSpec(memory_space=pltpu.VMEM)] * 5,
        out_specs=[pl.BlockSpec(memory_space=pltpu.VMEM)] * 3
        + [pl.BlockSpec(memory_space=pl.ANY)] * 2,
        scratch_shapes=[
            vmem(low, rep_size, tokens, features),
            vmem(low, rep_size, tokens, features),
            vmem(low, z, x, rows, width),
            vmem(low, z, x, units, features),
            vmem(low, z * x, rep_size, tokens, rows),
            vmem(low, z * x, rep_size, tokens, units),
            vmem(high, rep_size, tokens, width),
            vmem(high, rep_size, tokens, width),
            vmem(low, rep_size, tokens, width),
            vmem(high, rep_size, tokens, features),
            vmem(low, z, x, rows, width),
            vmem(low, z, x, units, features),
            vmem(low, x - 1, z, rows, width),
            vmem(low, x - 1, z, units, features),
            vmem(low, z + 1, rows, width),
            vmem(low, z + 1, units, features),
            vmem(low, rows, width),
            vmem(low, units, features),
            vmem(low, rep_size, tokens, features),
            vmem(low, rep_size, tokens, features),
            vmem(low, y, tokens, features),
            vmem(low, y, tokens, features),
            vmem(low, y - 1, tokens, features),
            vmem(low, y - 1, tokens, features),
            pltpu.SemaphoreType.DMA((total,)),
            pltpu.SemaphoreType.DMA((total,)),
            pltpu.SemaphoreType.DMA((2,)),
        ],
        compiler_params=pltpu.CompilerParams(
            collective_id=2, has_side_effects=True, vmem_limit_bytes=DENSE_VMEM
        ),
        name="dense_step",
    )(dense_input, cotangent, up_block, down_block, bias)


def cut_kernel(parts, source_ref, out_ref):
    shard_size, rep_size, units = parts
    mine = lax.axis_index("rep")
    for r in range(rep_size):

        @pl.when(mine == r)
        def _():
            for s in range(shard_size):
                start = (s * rep_size + r) * units
                out_ref[:, s * units : (s + 1) * units] = source_ref[:, start : start + units]


def cut_units(weight, shard_size, rep_size):
    rows, width = weight.shape
    units = width // (shard_size * rep_size)
    return pl.pallas_call(
        functools.partial(cut_kernel, (shard_size, rep_size, units)),
        out_shape=jax.ShapeDtypeStruct((rows, shard_size * units), jnp.float32),
        in_specs=[pl.BlockSpec(memory_space=pltpu.VMEM)],
        out_specs=pl.BlockSpec(memory_space=pltpu.VMEM),
        compiler_params=pltpu.CompilerParams(vmem_limit_bytes=GATHER_VMEM),
        name="cut_units",
    )(weight)


def adam_rows(weight, first, second, grad_in, decay):
    first_next = beta_one * first + (1.0 - beta_one) * grad_in
    second_next = beta_two * second + (1.0 - beta_two) * grad_in * grad_in
    correct_one = 1.0 - beta_one**ADAM_STEP
    correct_two = 1.0 - beta_two**ADAM_STEP
    step_size = first_next / correct_one / (jnp.sqrt(second_next / correct_two) + adam_eps)
    return weight - learn_rate * (step_size + decay * weight), first_next, second_next


def adam_kernel(parts, *refs):
    shard_size, rep_size, units = parts
    vec_w, vec_m, vec_g, attn_g, up_g, down_g = refs[:6]
    streams = [refs[6 + 2 * n : 8 + 2 * n] for n in range(3)]
    vec_new, vec_next = refs[12:14]
    outs = [refs[14 + 3 * n : 17 + 3 * n] for n in range(3)]
    wides = refs[23:]
    step = pl.program_id(0)

    @pl.when(step == 0)
    def _():
        rows = attn_g.shape[0]
        wides[0][...] = attn_g[...].astype(jnp.float32)
        for r in range(rep_size):
            values = up_g[r].astype(jnp.float32)
            for s in range(shard_size):
                start = (s * rep_size + r) * units
                wides[1][:, start : start + units] = values[:, s * units : (s + 1) * units]
        for r in range(rep_size):
            wides[2][r * units : (r + 1) * units, :] = down_g[r].astype(jnp.float32)
        new, first, second = adam_rows(vec_w[...], vec_m[0], vec_m[1], vec_g[...], 0.0)
        vec_new[...] = new
        vec_next[0] = first
        vec_next[1] = second

    for (weight, moments), (grad_out, new_out, next_out), wide in zip(streams, outs, wides):
        count = weight.shape[0]
        if count == wide.shape[0]:
            grad_in = wide[...]
        else:
            grad_in = wide[pl.ds(pl.multiple_of(step * count, 8), count), :]
        new, first, second = adam_rows(
            weight[...], moments[0], moments[1], grad_in, weight_decay
        )
        grad_out[...] = grad_in
        new_out[...] = new
        next_out[0] = first
        next_out[1] = second


def adam_all(rep_size, shard_size, attn, up, down, vector):
    rows, width = attn[0].shape
    units = up[2].shape[2] // shard_size
    steps = rows // 8 if rows % 8 == 0 and down[0].shape[0] % rows == 0 else 1
    flat, lead = [], []
    for weight, moments, _ in (attn, up, down):
        tall, wide = weight.shape
        part = tall // steps
        rows_spec = pl.BlockSpec((part, wide), lambda n: (n, 0))
        pair_spec = pl.BlockSpec((2, part, wide), lambda n: (0, n, 0))
        one = jax.ShapeDtypeStruct(weight.shape, jnp.float32)
        two = jax.ShapeDtypeStruct(moments.shape, jnp.float32)
        flat.append((rows_spec, pair_spec, one, two, pltpu.VMEM(weight.shape, jnp.float32)))
    fixed = lambda values: pl.BlockSpec(values.shape, lambda n: (0,) * values.ndim)
    held = [*vector, attn[2], up[2], down[2]]
    vec_out = [jax.ShapeDtypeStruct(values.shape, jnp.float32) for values in vector[:2]]
    return pl.pallas_call(
        functools.partial(adam_kernel, (shard_size, rep_size, units)),
        grid=(steps,),
        out_shape=vec_out + [shape for f in flat for shape in (f[2], f[2], f[3])],
        in_specs=[fixed(values) for values in held]
        + [spec for f in flat for spec in (f[0], f[1])],
        out_specs=[fixed(values) for values in vector[:2]]
        + [spec for f in flat for spec in (f[0], f[0], f[1])],
        scratch_shapes=[f[4] for f in flat],
        compiler_params=pltpu.CompilerParams(vmem_limit_bytes=ADAM_VMEM),
        name="adam_all",
    )(*held, attn[0], attn[1], up[0], up[1], down[0], down[1])


def shards(
    rep_size,
    shard_size,
    hidden_in,
    cotangent,
    segment_ids,
    attn_weight,
    attn_moments,
    up_weight,
    up_moments,
    down_weight,
    down_moments,
    vectors,
    vector_moments,
):
    grid = Grid(rep_size, shard_size)
    rep = lax.axis_index("rep")
    tokens, features = hidden_in.shape
    rows, width = up_weight.shape
    units = width // (shard_size * rep_size)
    own_cols = shard_size * units
    attn_block = attn_weight.astype(jnp.bfloat16)
    attn_split = Split(*attn_block.shape, grid.y_size)
    attn_wide, vector_wide = gather_params(
        grid, [attn_split], [attn_split.pad(attn_block)], vectors.astype(jnp.bfloat16)
    )
    attn_full = attn_wide[:, :, :rows].reshape(-1, width)
    vector_full = vector_wide.transpose(2, 0, 1, 3).reshape(vectors.shape[0], -1)

    mine = lambda values, axis: lax.dynamic_index_in_dim(values, rep, axis, keepdims=False)
    up_block = cut_units(up_weight, shard_size, rep_size).astype(jnp.bfloat16)
    down_block = mine(down_weight.reshape(rep_size, units, features), 0).astype(jnp.bfloat16)
    bias = mine(
        vector_full[8:].astype(jnp.float32).reshape(shard_size, rep_size, units), 1
    ).reshape(1, own_cols)

    residual, dense_input, stored = attention_forward(
        hidden_in[None], segment_ids, attn_full, vector_full
    )
    dense_out, dense_input_grad, unit_sums, up_slices, down_slices = dense_step(
        grid, rep_size, dense_input, cotangent, up_block, down_block, bias
    )
    block_out = (residual + dense_out + vector_full[7].astype(jnp.float32)).astype(jnp.bfloat16)
    input_grad, small_rows, attn_input, joined_round, attended, resid_round = attention_backward(
        cotangent[None], segment_ids, stored, attn_full, vector_full, dense_input_grad
    )
    unit_rows = lax.dynamic_update_index_in_dim(
        jnp.zeros((shard_size, rep_size, units), jnp.float32),
        unit_sums.reshape(shard_size, units),
        rep,
        1,
    ).reshape(-1, features)
    vector_terms = jnp.concatenate([small_rows, unit_rows], axis=0)
    attn_term = jnp.concatenate(
        [inner_rows(attn_input, joined_round), inner_rows(attended, resid_round)], axis=1
    )
    grads = [
        attn_split.pad(
            attn_term.astype(jnp.bfloat16).reshape((grid.z_size, grid.x_size, rows, width))
        )
    ]
    attn_owned, vector_total = reduce_grads(grid, [attn_split], grads, vector_terms)
    own_width = vectors.shape[1]
    vector_own = lax.dynamic_slice_in_dim(
        vector_total, lax.axis_index("shard") * own_width, own_width, 1
    )
    (
        new_vectors,
        vector_next,
        attn_grad,
        new_attn,
        attn_next,
        up_grad,
        new_up,
        up_next,
        down_grad,
        new_down,
        down_next,
    ) = adam_all(
        rep_size,
        shard_size,
        (attn_weight, attn_moments, attn_owned),
        (up_weight, up_moments, up_slices),
        (down_weight, down_moments, down_slices),
        (vectors, vector_moments, vector_own),
    )
    return (
        block_out,
        input_grad[0],
        attn_grad,
        up_grad,
        down_grad,
        vector_own,
        new_attn,
        attn_next,
        new_up,
        up_next,
        new_down,
        down_next,
        new_vectors,
        vector_next,
    )


def solution(mesh):
    in_specs = (
        P(("rep", "shard"), None),
        P(("rep", "shard"), None),
        P(("rep", "shard"), None),
        P("shard", None),
        P(None, "shard", None),
        P("shard", None),
        P(None, "shard", None),
        P("shard", None),
        P(None, "shard", None),
        P(None, "shard"),
        P(None, None, "shard"),
    )
    out_specs = (
        P(("rep", "shard"), None),
        P(("rep", "shard"), None),
        P("shard", None),
        P("shard", None),
        P("shard", None),
        P(None, "shard"),
        P("shard", None),
        P(None, "shard", None),
        P("shard", None),
        P(None, "shard", None),
        P("shard", None),
        P(None, "shard", None),
        P(None, "shard"),
        P(None, None, "shard"),
    )
    body = functools.partial(shards, mesh.shape["rep"], mesh.shape["shard"])
    return jax.shard_map(body, mesh=mesh, in_specs=in_specs, out_specs=out_specs, check_vma=False)
```

```python
import functools

import jax
import jax.numpy as jnp
import numpy as np
from jax import lax
from jax.experimental import pallas as pl
from jax.experimental.pallas import tpu as pltpu
from jax.sharding import PartitionSpec as P

HEAD_DIM = 64
ADAM_STEP = 3
MESH = pl.DeviceIdType.MESH


beta_one = 0.9
beta_two = 0.999
adam_eps = 1e-08
learn_rate = 0.25
weight_decay = 0.1


def matmul(left_arg, right_arg):
    return jnp.dot(left_arg, right_arg, preferred_element_type=jnp.float32)


def inner_rows(left_arg, right_arg):
    return lax.dot_general(
        left_arg, right_arg, (((0,), (0,)), ((), ())), preferred_element_type=jnp.float32
    )


def product(pattern, left_arg, right_arg):
    return jnp.einsum(pattern, left_arg, right_arg, preferred_element_type=jnp.float32)


def normalize(values):
    average = jnp.mean(values, axis=-1, keepdims=True)
    centred = values - average
    inv_std = lax.rsqrt(jnp.mean(centred * centred, axis=-1, keepdims=True) + 1e-05)
    return (centred * inv_std, inv_std)


def normalize_back(grad_in, normed, inv_std, gain_row):
    scaled = grad_in * gain_row
    return inv_std * (
        scaled
        - jnp.mean(scaled, axis=-1, keepdims=True)
        - normed * jnp.mean(scaled * normed, axis=-1, keepdims=True)
    )


def allowed(segments):
    row_count = segments.shape[-1]
    causal = lax.broadcasted_iota(jnp.int32, (row_count, row_count), 0) >= lax.broadcasted_iota(
        jnp.int32, (row_count, row_count), 1
    )
    same_doc = segments[:, :, None] == segments[:, None, :]
    return jnp.logical_and(same_doc, causal)[:, None, :, :]


def scores_of(queries, keys_all, segments):
    logits = product("bqhe,bkhe->bhqk", queries, keys_all) * HEAD_DIM ** (-0.5)
    return jnp.where(allowed(segments), logits, -1e30)


def attention_forward(activations, segments, attn_full, vector_full):
    batch_size, row_count, features = activations.shape
    head_count = features // HEAD_DIM
    head_shape = (batch_size, row_count, head_count, HEAD_DIM)
    vector_rows = vector_full.astype(jnp.float32)
    inputs_flat = activations.astype(jnp.float32).reshape(batch_size * row_count, features)
    normed_one, inv_one = normalize(inputs_flat)
    attn_input = (normed_one * vector_rows[0] + vector_rows[1]).astype(jnp.bfloat16)
    projected = matmul(attn_input, attn_full[:, : 3 * features])
    queries = (projected[:, :features] + vector_rows[2]).astype(jnp.bfloat16).reshape(head_shape)
    keys_all = projected[:, features : 2 * features].astype(jnp.bfloat16).reshape(head_shape)
    values_all = (
        (projected[:, 2 * features :] + vector_rows[3]).astype(jnp.bfloat16).reshape(head_shape)
    )
    logits = scores_of(queries, keys_all, segments)
    row_max = jnp.max(logits, axis=-1, keepdims=True)
    exponent = jnp.exp(logits - row_max)
    totals = jnp.sum(exponent, axis=-1, keepdims=True)
    log_total = row_max + jnp.log(totals)
    soft_probs = (exponent / totals).astype(jnp.bfloat16)
    attended = (
        product("bhqk,bkhe->bqhe", soft_probs, values_all)
        .reshape(batch_size * row_count, features)
        .astype(jnp.bfloat16)
    )
    residual = inputs_flat + matmul(attended, attn_full[:, 3 * features :]) + vector_rows[4]
    normed_two, inv_two = normalize(residual)
    dense_input = (normed_two * vector_rows[5] + vector_rows[6]).astype(jnp.bfloat16)
    stored = (
        normed_one,
        inv_one,
        attn_input,
        queries,
        keys_all,
        values_all,
        log_total,
        attended,
        normed_two,
        inv_two,
    )
    return (residual, dense_input, stored)


def attention_backward(cotangent, segments, stored, attn_full, vector_full, dense_input_grad):
    (
        normed_one,
        inv_one,
        attn_input,
        queries,
        keys_all,
        values_all,
        log_total,
        attended,
        normed_two,
        inv_two,
    ) = stored
    batch_size, row_count, features = cotangent.shape
    head_count = features // HEAD_DIM
    head_shape = (batch_size, row_count, head_count, HEAD_DIM)
    vector_rows = vector_full.astype(jnp.float32)
    out_float = cotangent.reshape(batch_size * row_count, features).astype(jnp.float32)
    resid_grad = out_float + normalize_back(dense_input_grad, normed_two, inv_two, vector_rows[5])
    resid_round = resid_grad.astype(jnp.bfloat16)
    attended_grad = lax.dot_general(
        resid_round,
        attn_full[:, 3 * features :],
        (((1,), (1,)), ((), ())),
        preferred_element_type=jnp.float32,
    ).astype(jnp.bfloat16)
    heads_grad = attended_grad.reshape(head_shape)
    logits = scores_of(queries, keys_all, segments)
    recomputed = jnp.exp(logits - log_total)
    prob_round = recomputed.astype(jnp.bfloat16)
    prob_grad = product("bqhe,bkhe->bhqk", heads_grad, values_all)
    delta_row = product("bqhe,bqhe->bhq", heads_grad, attended.reshape(head_shape))[..., None]
    logit_grad = (recomputed * (prob_grad - delta_row)).astype(jnp.bfloat16)
    scale_factor = HEAD_DIM ** (-0.5)
    query_grad = product("bhqk,bkhe->bqhe", logit_grad, keys_all) * scale_factor
    key_grad = product("bhqk,bqhe->bkhe", logit_grad, queries) * scale_factor
    value_grad = product("bhqk,bqhe->bkhe", prob_round, heads_grad)
    joined_grad = jnp.concatenate(
        [
            query_grad.reshape(-1, features),
            key_grad.reshape(-1, features),
            value_grad.reshape(-1, features),
        ],
        axis=1,
    )
    joined_round = joined_grad.astype(jnp.bfloat16)
    attn_input_grad = lax.dot_general(
        joined_round,
        attn_full[:, : 3 * features],
        (((1,), (1,)), ((), ())),
        preferred_element_type=jnp.float32,
    )
    input_grad = (
        (resid_grad + normalize_back(attn_input_grad, normed_one, inv_one, vector_rows[0]))
        .astype(jnp.bfloat16)
        .reshape(batch_size, row_count, features)
    )
    small_rows = jnp.stack(
        [
            jnp.sum(attn_input_grad * normed_one, axis=0),
            jnp.sum(attn_input_grad, axis=0),
            jnp.sum(joined_grad[:, :features], axis=0),
            jnp.sum(joined_grad[:, 2 * features :], axis=0),
            jnp.sum(resid_grad, axis=0),
            jnp.sum(dense_input_grad * normed_two, axis=0),
            jnp.sum(dense_input_grad, axis=0),
            jnp.sum(out_float, axis=0),
        ]
    )
    return (input_grad, small_rows, attn_input, joined_round, attended, resid_round)


CORES = 2
ROW_UNIT = 16
LANE_UNIT = 128
GATHER_VMEM = 16 * 2**20
REDUCE_VMEM = 56 * 2**20
DENSE_VMEM = 60 * 2**20
ADAM_VMEM = 56 * 2**20


class Grid:
    def __init__(self, rep_size, shard_size):
        self.cores = CORES
        self.y_size = rep_size // CORES
        self.x_size = self.y_size if shard_size % self.y_size == 0 else 1
        self.z_size = shard_size // self.x_size

    def locate(self):
        rep = lax.axis_index("rep")
        shard = lax.axis_index("shard")
        self.y, self.c = lax.div(rep, CORES), lax.rem(rep, CORES)
        self.z, self.x = lax.div(shard, self.x_size), lax.rem(shard, self.x_size)
        return self

    def device(self, dz=0, dx=0, dy=0, dc=0):
        rep = lax.rem(self.y + dy, self.y_size) * CORES + lax.rem(self.c + dc, CORES)
        shard = lax.rem(self.z + dz, self.z_size) * self.x_size + lax.rem(self.x + dx, self.x_size)
        return (rep, shard)

    def partners(self):
        found = [self.device(dz=k) for k in range(1, self.z_size)]
        found += [self.device(dx=k) for k in range(1, self.x_size)]
        found += [self.device(dy=k) for k in range(1, self.y_size)]
        return found + [self.device(dc=1)]

    def greet(self):
        barrier = pltpu.get_barrier_semaphore()
        partners = self.partners()
        for partner in partners:
            pl.semaphore_signal(barrier, inc=1, device_id=partner, device_id_type=MESH)
        pl.semaphore_wait(barrier, len(partners))


class Split:
    def __init__(self, rows, columns, y_size, share=0.7, array=0, chunk=0, chunks=1):
        self.rows, self.columns, self.array = rows, columns, array
        self.by_lane = columns % (2 * LANE_UNIT) == 0
        unit = LANE_UNIT if self.by_lane else ROW_UNIT
        extent = columns if self.by_lane else rows
        padded = -(-extent // (2 * unit)) * 2 * unit
        if not self.by_lane:
            self.rows = padded
        pairs = padded // (2 * unit)
        chunks = max(1, min(chunks, pairs // (y_size + 1)))
        self.chunks = chunks
        starts = [n * (pairs // chunks) + min(n, pairs % chunks) for n in range(chunks + 1)]
        units = starts[chunk + 1] - starts[chunk]
        self.unit = unit
        self.start = 2 * unit * starts[chunk]
        self.half = units * unit
        taken = min(max(1, int(units * share / y_size + 0.5)), (units - 1) // y_size)
        self.a_size = taken * unit
        self.b_start = y_size * self.a_size
        self.b_size = self.half - self.b_start

    def chunked(self, y_size, share, array, chunks):
        found = Split(self.rows, self.columns, y_size, share, array, 0, chunks)
        return [found] + [
            Split(self.rows, self.columns, y_size, share, array, n, chunks)
            for n in range(1, found.chunks)
        ]

    def block(self):
        return (self.rows, self.columns)

    def shape(self, size):
        return (self.rows, size) if self.by_lane else (size, self.columns)

    def cut(self, start, size):
        window = pl.ds(pl.multiple_of(self.start + start, self.unit), size)
        return (slice(None), window) if self.by_lane else (window, slice(None))

    def piece_a(self, y, c):
        return self.cut(c * self.half + y * self.a_size, self.a_size)

    def piece_b(self, c):
        return self.cut(c * self.half + self.b_start, self.b_size)

    def piece_half(self, c):
        return self.cut(c * self.half, self.half)

    def pad(self, values):
        extra = self.rows - values.shape[-2]
        if extra == 0:
            return values
        return jnp.pad(values, [(0, 0)] * (values.ndim - 2) + [(0, extra), (0, 0)])


def remote(source, target, send, recv, device):
    return pltpu.make_async_remote_copy(
        src_ref=source,
        dst_ref=target,
        send_sem=send,
        recv_sem=recv,
        device_id=device,
        device_id_type=MESH,
    )


class Semaphores:
    def __init__(self, array):
        self.array, self.used = array, 0

    def take(self):
        self.used += 1
        return self.array.at[self.used - 1]


def chosen(condition):
    return (lambda body: body()) if condition is True else pl.when(condition)


class Links:
    def __init__(self, send_array, recv_array):
        self.sends, self.recvs = send_array, recv_array
        self.copies = {}

    def launch(self, key, source, target, device, sent=True, got=True):
        n = len(self.copies)
        copy = remote(source, target, self.sends.at[n], self.recvs.at[n], device)
        self.copies[key] = (copy, sent, got)
        chosen(sent)(copy.start)

    def arrived(self, *keys):
        for key in keys:
            copy, _, got = self.copies[key]
            chosen(got)(copy.wait_recv)

    def wait(self, key):
        self.copies[key][0].wait_recv()

    def finish(self):
        for copy, sent, _ in self.copies.values():
            chosen(sent)(copy.wait_send)


GATHER_PLAN = {
    "zv": 0,
    "ub": 1,
    "ux": 2,
    "za": 3,
    "dx": 4,
    "xv": (5, 6, 7, 8),
    "xa": (9, 11, 14, 18),
    "u": (10, 13, 17),
    "ya": (12, 15, 19, 21),
    "db": 16,
    "d": (20, 23, 25),
    "c": (22, 24, 26, 27),
}
REDUCE_PLAN = {
    "c": (0, 2, 4),
    "dx": (1, 3, 10, 11),
    "v": (5, 8, 16, 25, 28),
    "y": (6, 7, 9),
    "d": (12, 13, 17, 20),
    "x": (14, 19, 24),
    "ux": (15, 18, 27, 29),
    "z": (21, 30, 34),
    "de": 22,
    "u": (23, 26, 32, 36),
    "f": (31, 35, 40),
    "dp": 33,
    "s": (37, 39, 42),
    "ue": 38,
    "up": 41,
}


def arrange(plan, counts):
    timed = []
    for name, places in plan.items():
        if isinstance(places, int):
            timed.append((places, name, ()))
            continue
        marks = np.linspace(0.0, 1.0, counts[name])
        spots = np.interp(marks, np.linspace(0.0, 1.0, len(places)), places)
        timed += [(float(spot), name, (n,)) for n, spot in enumerate(spots)]
    return [(name, index) for _, name, index in sorted(timed)]


def gather_kernel(grid, split, *refs):
    attn_own, vec_own, up_own, down_own = refs[:4]
    attn_full, vec_full, up_full, down_full = refs[4:8]
    links, local_array = Links(refs[8], refs[9]), refs[10]
    g = grid.locate()
    z_size, x_size, y_size = g.z_size, g.x_size, g.y_size
    hops = range(z_size - 1)
    near = lambda j: lax.rem(g.z + j + z_size, z_size)
    place = lambda j, i: (lax.rem(g.z + z_size - j, z_size), lax.rem(g.x + x_size - i, x_size))
    own = {"a": attn_own, "v": vec_own, "u": up_own, "d": down_own}
    full = {"a": attn_full, "v": vec_full, "u": up_full, "d": down_full}

    def windows(t):
        if t == "v":
            return [(slice(None), slice(None))]
        return [split.piece_a(g.y, g.c), split.piece_b(g.c)]

    def stage_z(t):
        for k in range(1, z_size):
            for p, window in enumerate(windows(t)):
                links.launch(
                    ("z", t, p, k),
                    own[t].at[window],
                    full[t].at[(g.z, g.x) + window],
                    g.device(dz=k),
                )

    def unit_x(t, j):
        for p, window in enumerate(windows(t)):
            here = place(j, 0) + window
            if j > 0:
                links.arrived(("z", t, p, j))
            source = own[t].at[window] if j == 0 else full[t].at[here]
            for i in range(1, x_size):
                links.launch(("x", t, p, j, i), source, full[t].at[here], g.device(dx=i))
            if t == "a" and p == 0 and j > 0:
                for k in range(1, y_size):
                    links.launch(("y", t, j, 0, k), source, full[t].at[here], g.device(dy=k))

    def unit_y(t, j):
        for i in range(1, x_size):
            for p, window in enumerate(windows(t)):
                links.arrived(("x", t, p, j, i))
                if t == "a" and p == 0:
                    here = full[t].at[place(j, i) + window]
                    for k in range(1, y_size):
                        links.launch(("y", t, j, i, k), here, here, g.device(dy=k))

    def unit_core(j):
        for i in range(x_size):
            if (j, i) == (0, 0):
                continue
            for k in range(1, y_size):
                links.arrived(("y", "a", j, i, k))
            here = attn_full.at[place(j, i) + split.piece_half(g.c)]
            links.launch(("c", j, i), here, here, g.device(dc=1))

    def hop(t, k):
        source = own[t] if k == 0 else full[t].at[near(-k), g.x]
        links.launch(
            ("right" + t, k),
            source,
            full[t].at[near(-k), g.x],
            g.device(dz=1),
            jnp.logical_and(g.z >= k, g.z + 1 < z_size),
            g.z >= k + 1,
        )
        source = own[t] if k == 0 else full[t].at[near(k), g.x]
        links.launch(
            ("left" + t, k),
            source,
            full[t].at[near(k), g.x],
            g.device(dz=z_size - 1),
            jnp.logical_and(g.z + k < z_size, g.z >= 1),
            g.z + 1 + k < z_size,
        )

    def across(name, t, source, where, held):
        for i in range(1, x_size):
            target = full[t].at[where, g.x]
            links.launch((name + t, i), source, target, g.device(dx=i), held, held)

    def begin(t):
        hop(t, 0)

    def direct(t):
        across("own", t, own[t], g.z, True)

    def advance(t, k):
        links.arrived(("right" + t, k), ("left" + t, k))
        if k + 1 < z_size - 1:
            hop(t, k + 1)
        across("r%d" % k, t, full[t].at[near(-k - 1), g.x], near(-k - 1), g.z >= k + 1)
        across("l%d" % k, t, full[t].at[near(k + 1), g.x], near(k + 1), g.z + 1 + k < z_size)

    def whole(t):
        for i in range(1, x_size):
            links.arrived(("own" + t, i))
            for k in hops:
                links.arrived(("r%d" % k + t, i), ("l%d" % k + t, i))

    g.greet()
    kept = []
    for n, t in enumerate(own):
        copy = pltpu.make_async_copy(own[t], full[t].at[g.z, g.x], local_array.at[n])
        copy.start()
        kept.append(copy)
    table = {"zv": (stage_z, "v"), "za": (stage_z, "a"), "c": (unit_core,)}
    table.update({"x" + t: (unit_x, t) for t in "va"})
    table["ya"] = (unit_y, "a")
    for t in "ud":
        table.update({t: (advance, t), t + "b": (begin, t), t + "x": (direct, t)})
    counts = {name: z_size - 1 if name in "ud" else z_size for name in table}
    for name, index in arrange(GATHER_PLAN, counts):
        table[name][0](*table[name][1:], *index)
    for j in range(z_size):
        unit_y("v", j)
    whole("u")
    whole("d")
    for j in range(z_size):
        for i in range(x_size):
            if (j, i) != (0, 0):
                links.arrived(("c", j, i))
    links.finish()
    for copy in kept:
        copy.wait()


def gather_params(grid, split, blocks):
    z, x, y = grid.z_size, grid.x_size, grid.y_size
    total = 2 * (z - 1) + 2 * z * (x - 1) + (z * x - 1) * y
    total += (z - 1) + z * (x - 1) + 2 * (2 * (z - 1) + (x - 1) * (2 * z - 1))
    any_spec = pl.BlockSpec(memory_space=pl.ANY)
    return pl.pallas_call(
        functools.partial(gather_kernel, grid, split),
        out_shape=[jax.ShapeDtypeStruct((z, x) + block.shape, jnp.bfloat16) for block in blocks],
        in_specs=[pl.BlockSpec(memory_space=pltpu.VMEM)] * 4,
        out_specs=[any_spec] * 4,
        scratch_shapes=[
            pltpu.SemaphoreType.DMA((total,)),
            pltpu.SemaphoreType.DMA((total,)),
            pltpu.SemaphoreType.DMA((4,)),
        ],
        compiler_params=pltpu.CompilerParams(
            collective_id=0, has_side_effects=True, vmem_limit_bytes=GATHER_VMEM
        ),
        name="gather_params",
    )(*blocks)


def plus(left_arg, right_arg):
    return left_arg.astype(jnp.float32) + right_arg.astype(jnp.float32)


def reduce_kernel(grid, splits, *refs):
    count = len(splits)
    arrays = splits[-1].array + 1
    vector_in, up_terms, down_terms = refs[arrays : arrays + 3]
    grads = [refs[split.array] for split in splits]
    outs = [refs[arrays + 3 + split.array] for split in splits]
    vector_out, up_out, down_out = refs[2 * arrays + 3 : 2 * arrays + 6]
    scratch, slim = refs[2 * arrays + 6 : -11], refs[-11:]
    per = 12
    buffers = [scratch[per * t : per * (t + 1)] for t in range(count)]
    v_core, v_y, v_x, v_z, v_one, v_two, v_three, send_array, recv_array, local_array = scratch[
        per * count :
    ]
    sends, recvs, locals_ = (
        Semaphores(send_array),
        Semaphores(recv_array),
        Semaphores(local_array),
    )
    g = grid.locate()
    z_size, x_size, y_size = g.z_size, g.x_size, g.y_size
    copies, moves = {}, {}

    def launch(key, source, target, device):
        copy = remote(source, target, sends.take(), recvs.take(), device)
        copy.start()
        copies[key] = copy

    def move(key, source, target):
        copy = pltpu.make_async_copy(source, target, locals_.take())
        copy.start()
        moves[key] = copy

    def each_block(body):
        @pl.loop(0, z_size * x_size)
        def _(index):
            body(lax.div(index, x_size), lax.rem(index, x_size))

    everything = (slice(None), slice(None))
    other_y = lambda k: lax.rem(g.y + k, y_size)
    other_x = lambda k: lax.rem(g.x + k, x_size)
    other_z = lambda k: lax.rem(g.z + k, z_size)

    def stage_core(t):
        acc_a, acc_b, got_a, got_b = buffers[t][:4]
        split = splits[t]
        for q in range(y_size):
            launch(
                ("ca", t, q),
                grads[t].at[everything + split.piece_a(q, 1 - g.c)],
                got_a.at[q],
                g.device(dc=1),
            )
            move(("la", t, q), grads[t].at[everything + split.piece_a(q, g.c)], acc_a.at[q])
        launch(
            ("cb", t),
            grads[t].at[everything + split.piece_b(1 - g.c)],
            got_b,
            g.device(dc=1),
        )
        move(("lb", t), grads[t].at[everything + split.piece_b(g.c)], acc_b)

    def stage_y(t):
        acc_a, acc_b, got_a, got_b, got_y = buffers[t][:5]
        for q in range(y_size):
            copies["ca", t, q].wait_recv()
            moves["la", t, q].wait()

            def add_a(i, j, q=q):
                acc_a[q, i, j] = plus(acc_a[q, i, j], got_a[q, i, j]).astype(jnp.bfloat16)

            each_block(add_a)
        for k in range(1, y_size):
            launch(("ya", t, k), acc_a.at[other_y(k)], got_y.at[k - 1], g.device(dy=k))
        copies["cb", t].wait_recv()
        moves["lb", t].wait()

        def add_b(i, j):
            acc_b[i, j] = plus(acc_b[i, j], got_b[i, j]).astype(jnp.bfloat16)

        each_block(add_b)
        for k in range(1, x_size):
            launch(
                ("xb", t, k), acc_b.at[:, other_x(k)], buffers[t][6].at[k - 1], g.device(dx=k)
            )

    def stage_x(t):
        acc_a, got_y, got_xa = buffers[t][0], buffers[t][4], buffers[t][5]
        for k in range(1, y_size):
            copies["ya", t, k].wait_recv()

        def add(i, j):
            value = acc_a[g.y, i, j].astype(jnp.float32)
            for k in range(1, y_size):
                value = plus(value, got_y[k - 1, i, j])
            acc_a[g.y, i, j] = value.astype(jnp.bfloat16)

        each_block(add)
        for k in range(1, x_size):
            launch(
                ("xa", t, k), acc_a.at[g.y, :, other_x(k)], got_xa.at[k - 1], g.device(dx=k)
            )

    def stage_z(t):
        acc_a, acc_b = buffers[t][:2]
        got_xa, got_xb, got_za, got_zb = buffers[t][5:9]
        for k in range(1, x_size):
            copies["xb", t, k].wait_recv()
            copies["xa", t, k].wait_recv()

        @pl.loop(0, z_size)
        def _(i):
            value_a = acc_a[g.y, i, g.x].astype(jnp.float32)
            for k in range(1, x_size):
                value_a = plus(value_a, got_xa[k - 1, i])
            acc_a[g.y, i, g.x] = value_a.astype(jnp.bfloat16)
            value_b = acc_b[i, g.x].astype(jnp.float32)
            for k in range(1, x_size):
                value_b = plus(value_b, got_xb[k - 1, i])
            acc_b[i, g.x] = value_b.astype(jnp.bfloat16)

        for k in range(1, z_size):
            launch(
                ("zb", t, k), acc_b.at[other_z(k), g.x], got_zb.at[k - 1], g.device(dz=k)
            )
            launch(
                ("za", t, k),
                acc_a.at[g.y, other_z(k), g.x],
                got_za.at[k - 1],
                g.device(dz=k),
            )

    def stage_final(t):
        acc_a, acc_b = buffers[t][:2]
        got_za, got_zb, final_a, ring_b, final_b = buffers[t][7:12]
        split = splits[t]
        for k in range(1, z_size):
            copies["zb", t, k].wait_recv()
        value = acc_b[g.z, g.x].astype(jnp.float32)
        for k in range(1, z_size):
            value = plus(value, got_zb[k - 1])
        ring_b[0] = value.astype(jnp.bfloat16)
        for k in range(1, y_size):
            launch(("yb", t, k), ring_b.at[0], ring_b.at[k], g.device(dy=k))
        for k in range(1, z_size):
            copies["za", t, k].wait_recv()
        value = acc_a[g.y, g.z, g.x].astype(jnp.float32)
        for k in range(1, z_size):
            value = plus(value, got_za[k - 1])
        final_a[...] = value.astype(jnp.bfloat16)
        target = outs[t].at[split.piece_a(g.y, g.c)]
        for k in range(1, y_size):
            launch(("oa", t, k), final_a, target, g.device(dy=k))
        move(("fa", t), final_a, target)

    def stage_share(t):
        ring_b, final_b = buffers[t][10:12]
        split = splits[t]
        for k in range(1, y_size):
            copies["yb", t, k].wait_recv()
        value = ring_b[g.y].astype(jnp.float32)
        for k in range(1, y_size):
            value = plus(value, ring_b[lax.rem(g.y + y_size - k, y_size)])
        final_b[...] = value.astype(jnp.bfloat16)
        move(("fb", t), final_b, outs[t].at[split.piece_b(g.c)])
        for k in range(1, y_size):
            copies["oa", t, k].wait_recv()
        moves["fa", t].wait()
        moves["fb", t].wait()
        half = outs[t].at[split.piece_half(g.c)]
        launch(("h", t), half, half, g.device(dc=1))

    def sum_ring(buffer, place, size):
        value = buffer[place]
        for k in range(1, size):
            value = value + buffer[lax.rem(place + size - k, size)]
        return value

    def vector_step(name, source, got, size, **direction):
        (axis,) = direction
        got[0] = source[...]
        for k in range(1, size):
            launch((name, k), source, got.at[k], g.device(**{axis: k}))

    def vector_sum(name, got, place, size, target):
        for k in range(1, size):
            copies[name, k].wait_recv()
        target[...] = sum_ring(got, place, size)

    up_x, down_x, up_z, down_z, up_sum, down_sum, up_own, down_own = slim[:8]
    links = Links(slim[8], slim[9])
    rep = lax.axis_index("rep")
    terms = {"u": up_terms, "d": down_terms}
    sums = {"u": up_sum, "d": down_sum}
    got_x, got_z = {"u": up_x, "d": down_x}, {"u": up_z, "d": down_z}
    owned, shared = {"u": up_own, "d": down_own}, {"u": up_out, "d": down_out}

    def ranked(n):
        last = z_size - 1
        later = lax.div(lax.div(n + g.z, last) + 1, 2)
        return later * (n - last + g.z) + (1 - later) * (last - n)

    def slim_x(t, *some):
        for n in some or range(z_size):
            for k in range(1, x_size):
                links.launch(
                    ("rx" + t, k, n),
                    terms[t].at[ranked(n), other_x(k)],
                    got_x[t].at[k - 1, ranked(n)],
                    g.device(dx=k),
                )

    def fold(t, n):
        for k in range(1, x_size):
            links.arrived(("rx" + t, k, n))
        here = ranked(n)
        value = terms[t][here, g.x].astype(jnp.float32)
        for k in range(1, x_size):
            value = plus(value, got_x[t][k - 1, here])
        sums[t][here] = value.astype(jnp.bfloat16)

    def toward(t, key, step, goal, sent, got, slot, first, device):
        if step > 0:

            @pl.when(jnp.logical_and(sent, jnp.logical_not(first)))
            def _():
                links.wait((key + t, step - 1))
                sums[t][goal] = plus(sums[t][goal], got_z[t][slot]).astype(jnp.bfloat16)

        target = got_z[t].at[slot]
        links.launch((key + t, step), sums[t].at[goal], target, device, sent, got)

    def slim_z(t, step):
        fold(t, step)
        if step == z_size - 1:
            return
        goal = lax.rem(2 * z_size - 1 - step + g.z, z_size)
        got = jnp.logical_and(g.z >= 1, g.z <= step + 1)
        toward(t, "pr", step, goal, g.z <= step, got, goal + 1, g.z == 0, g.device(dz=1))
        back = z_size - 1 - g.z
        goal = lax.rem(step + 1 + g.z, z_size)
        got = jnp.logical_and(back >= 1, back <= step + 1)
        device = g.device(dz=z_size - 1)
        toward(t, "pl", step, goal, back <= step, got, goal, back == 0, device)

    def slim_end(t):
        for key, some, slot in (("pr", g.z >= 1, g.z + 1), ("pl", g.z + 1 < z_size, g.z)):

            @pl.when(some)
            def _(key=key, slot=slot):
                links.wait((key + t, z_size - 2))
                sums[t][g.z] = plus(sums[t][g.z], got_z[t][slot]).astype(jnp.bfloat16)

        owned[t][...] = sums[t][g.z]
        for k in range(1, y_size):
            links.launch(("oy" + t, k), owned[t], shared[t].at[rep], g.device(dy=k))
        links.launch(("oc" + t, 0), owned[t], shared[t].at[rep], g.device(dc=1))
        n = 0 if t == "d" else 1
        copy = pltpu.make_async_copy(owned[t], shared[t].at[rep], slim[10].at[n])
        copy.start()
        moves["own" + t] = copy

    def slim_pass(t):
        for k in range(1, y_size):
            links.arrived(("oy" + t, k))
            here = shared[t].at[lax.rem(g.y + y_size - k, y_size) * CORES + g.c]
            links.launch(("oc" + t, k), here, here, g.device(dc=1))

    def small(n):
        if n == 0:
            vector_step("vc", vector_in, v_core, CORES, dc=1)
        if n == 1:
            vector_sum("vc", v_core, g.c, CORES, v_one)
            vector_step("vy", v_one, v_y, y_size, dy=1)
        if n == 2:
            vector_sum("vy", v_y, g.y, y_size, v_two)
            vector_step("vx", v_two, v_x, x_size, dx=1)
        if n == 3:
            vector_sum("vx", v_x, g.x, x_size, v_three)
            vector_step("vz", v_three, v_z, z_size, dz=1)
        if n == 4:
            vector_sum("vz", v_z, g.z, z_size, vector_out)

    g.greet()
    table = {"c": stage_core, "y": stage_y, "x": stage_x, "z": stage_z, "f": stage_final}
    table.update({"s": stage_share, "v": small})
    for t in ("d", "u"):
        table[t] = functools.partial(slim_z, t)
        table[t + "x"] = functools.partial(slim_x, t)
        table[t + "e"] = functools.partial(slim_end, t)
        table[t + "p"] = functools.partial(slim_pass, t)
    counts = {name: count if name in "cyxzfs" else z_size for name in table}
    counts["v"] = 5
    for name, index in arrange(REDUCE_PLAN, counts):
        table[name](*index)
    for key, copy in copies.items():
        if key[0] == "h":
            copy.wait_recv()
        copy.wait_send()
    for t in ("d", "u"):
        for k in range(y_size):
            links.arrived(("oc" + t, k))
        moves["own" + t].wait()
    links.finish()


def reduce_grads(grid, whole, grads, vector_terms, up_terms, down_terms):
    z, x, y = grid.z_size, grid.x_size, grid.y_size
    splits = []
    for array, split in enumerate(whole):
        splits += split.chunked(y, 0.85, array, 3)
    scratch = []
    for split in splits:
        a, b = split.shape(split.a_size), split.shape(split.b_size)
        scratch += [
            pltpu.VMEM(shape, jnp.bfloat16)
            for shape in (
                (y, z, x) + a,
                (z, x) + b,
                (y, z, x) + a,
                (z, x) + b,
                (y - 1, z, x) + a,
                (x - 1, z) + a,
                (x - 1, z) + b,
                (z - 1,) + a,
                (z - 1,) + b,
                a,
                (y,) + b,
                b,
            )
        ]
    small = vector_terms.shape
    scratch += [pltpu.VMEM((size,) + small, jnp.float32) for size in (CORES, y, x, z)]
    scratch += [pltpu.VMEM(small, jnp.float32)] * 3
    per_tensor = (y + 1) + (y - 1) + 2 * (x - 1) + 2 * (z - 1) + 2 * (y - 1) + 1
    total = len(splits) * per_tensor + 1 + (y - 1) + (x - 1) + (z - 1)
    scratch += [
        pltpu.SemaphoreType.DMA((total,)),
        pltpu.SemaphoreType.DMA((total,)),
        pltpu.SemaphoreType.DMA((len(splits) * (y + 3),)),
    ]
    slim = [up_terms.shape[2:], down_terms.shape[2:]]
    for lead in ((x - 1, z), (z + 1,), (z,), ()):
        scratch += [pltpu.VMEM(lead + block, jnp.bfloat16) for block in slim]
    extra = 2 * (z * (x - 1) + 2 * (z - 1) + 2 * y - 1)
    scratch += [pltpu.SemaphoreType.DMA((size,)) for size in (extra, extra, 2)]
    rep_size = y * CORES
    return pl.pallas_call(
        functools.partial(reduce_kernel, grid, splits),
        out_shape=[jax.ShapeDtypeStruct(split.block(), jnp.bfloat16) for split in whole]
        + [jax.ShapeDtypeStruct(small, jnp.float32)]
        + [jax.ShapeDtypeStruct((rep_size,) + block, jnp.bfloat16) for block in slim],
        in_specs=[pl.BlockSpec(memory_space=pl.ANY)] * len(whole)
        + [pl.BlockSpec(memory_space=pltpu.VMEM)] * 3,
        out_specs=[pl.BlockSpec(memory_space=pl.ANY)] * len(whole)
        + [pl.BlockSpec(memory_space=pltpu.VMEM)]
        + [pl.BlockSpec(memory_space=pl.ANY)] * 2,
        scratch_shapes=scratch,
        compiler_params=pltpu.CompilerParams(
            collective_id=1, has_side_effects=True, vmem_limit_bytes=REDUCE_VMEM
        ),
        name="reduce_grads",
    )(*grads, vector_terms, up_terms, down_terms)


def outer_rows(left_arg, right_arg):
    return lax.dot_general(
        left_arg, right_arg, (((1,), (1,)), ((), ())), preferred_element_type=jnp.float32
    )


def dense_kernel(grid, rep_size, *refs):
    dense_ref, cot_ref, up_full, down_full, bias_ref = refs[:5]
    out_ref, back_ref, sums_ref, up_grad, down_grad = refs[5:10]
    (
        dense_all,
        cot_all,
        inputs_cut,
        hidden_cut,
        slope,
        hidden_grad,
        hidden_round,
        wide_grad,
        out_part,
        back_part,
        out_core,
        back_core,
        out_y,
        back_y,
        send_array,
        recv_array,
    ) = refs[10:]
    links = Links(send_array, recv_array)
    g = grid.locate()
    z_size, x_size, y_size = g.z_size, g.x_size, g.y_size
    shard_size = z_size * x_size
    rep = lax.axis_index("rep")
    tokens, features = dense_ref.shape
    rows, width = up_full.shape[2:]
    units = down_full.shape[2]
    total = rep_size * tokens
    split = lambda n: (n // x_size, n % x_size)
    rep_at = lambda dy, dc: lax.rem(g.y + dy, y_size) * CORES + lax.rem(g.c + dc, CORES)

    barrier = pltpu.get_barrier_semaphore()
    partners = [g.device(dy=k) for k in range(1, y_size)] + [g.device(dc=1)]
    for partner in partners:
        pl.semaphore_signal(barrier, inc=1, device_id=partner, device_id_type=MESH)
    pl.semaphore_wait(barrier, len(partners))

    def spread(name, source, target):
        for k in range(1, y_size):
            links.launch((name, "y", k), source, target.at[rep], g.device(dy=k))
        links.launch((name, "c", 0), source, target.at[rep], g.device(dc=1))

    def pass_on(name, target):
        for k in range(1, y_size):
            links.arrived((name, "y", k))
            here = target.at[rep_at(y_size - k, 0)]
            links.launch((name, "c", k), here, here, g.device(dc=1))

    def spread_end(name):
        for k in range(y_size):
            links.arrived((name, "c", k))

    def term(target, left, right):
        @pl.loop(0, shard_size)
        def _(s):
            one = left[s].reshape(total, left.shape[-1])
            two = right[...].reshape(total, right.shape[-1])
            value = inner_rows(one, two)
            target[lax.div(s, x_size), lax.rem(s, x_size)] = value.astype(jnp.bfloat16)

    def scatter(name, part, got):
        for k in range(y_size):
            links.launch((name, "c", k), part.at[rep_at(k, 1)], got.at[k], g.device(dc=1))

    def scatter_y(name, part, core, got):
        for k in list(range(1, y_size)) + [0]:
            links.arrived((name, "c", k))
            there = rep_at(k, 0)
            part[there] = plus(part[there], core[k]).astype(jnp.bfloat16)
            if k > 0:
                links.launch((name, "y", k), part.at[there], got.at[k - 1], g.device(dy=k))

    def collect(name, part, got, target):
        value = part[rep].astype(jnp.float32)
        for k in range(1, y_size):
            links.arrived((name, "y", k))
            value = plus(value, got[k - 1])
        target[...] = value

    spread("dense", dense_ref, dense_all)
    spread("cot", cot_ref, cot_all)
    dense_all[rep] = dense_ref[...]
    cot_all[rep] = cot_ref[...]

    def hidden_of(b):
        values = dense_all[b].astype(jnp.float32)
        for s in range(shard_size):
            inputs_cut[s, b] = values[:, s * rows : (s + 1) * rows].astype(jnp.bfloat16)
        pre = jnp.broadcast_to(bias_ref[...], (tokens, width))
        for s in range(shard_size):
            pre = pre + matmul(inputs_cut[s, b], up_full[split(s)])
        normal_cdf = 0.5 * (1.0 + lax.erf(pre * 0.7071067811865476))
        density = jnp.exp(-0.5 * pre * pre) * 0.3989422804014327
        slope[b] = normal_cdf + pre * density
        hidden = pre * normal_cdf
        for s in range(shard_size):
            hidden_cut[s, b] = hidden[:, s * units : (s + 1) * units].astype(jnp.bfloat16)
        value = matmul(hidden_cut[0, b], down_full[split(0)])
        for s in range(1, shard_size):
            value = value + matmul(hidden_cut[s, b], down_full[split(s)])
        out_part[b] = value.astype(jnp.bfloat16)

    pass_on("dense", dense_all)
    spread_end("dense")
    pl.loop(0, rep_size)(hidden_of)
    scatter("out", out_part, out_core)
    pass_on("cot", cot_all)
    spread_end("cot")

    for s in range(shard_size):
        value = outer_rows(cot_all[...].reshape(total, features), down_full[split(s)])
        hidden_grad[:, :, s * units : (s + 1) * units] = value.reshape(rep_size, tokens, units)
    sums_ref[...] = jnp.zeros_like(sums_ref)

    @pl.loop(0, rep_size)
    def _(b):
        value = hidden_grad[b] * slope[b]
        sums_ref[...] += jnp.sum(value, axis=0, keepdims=True)
        hidden_round[b] = value.astype(jnp.bfloat16)

    scatter_y("out", out_part, out_core, out_y)
    for s in range(shard_size):
        value = outer_rows(hidden_round[...].reshape(total, width), up_full[split(s)])
        wide_grad[:, :, s * rows : (s + 1) * rows] = value.reshape(rep_size, tokens, rows)

    @pl.loop(0, rep_size)
    def _(b):
        back_part[b] = wide_grad[b].astype(jnp.bfloat16)

    scatter("back", back_part, back_core)
    term(up_grad, inputs_cut, hidden_round)
    scatter_y("back", back_part, back_core, back_y)
    term(down_grad, hidden_cut, cot_all)
    collect("out", out_part, out_y, out_ref)
    collect("back", back_part, back_y, back_ref)
    links.finish()


def dense_step(grid, rep_size, dense_input, cotangent, up_full, down_full, bias):
    z, x, y = grid.z_size, grid.x_size, grid.y_size
    tokens, features = dense_input.shape
    rows, width = up_full.shape[2:]
    units = down_full.shape[2]
    low, high = jnp.bfloat16, jnp.float32
    vmem = lambda dtype, *shape: pltpu.VMEM(shape, dtype)
    shape = lambda dtype, *sizes: jax.ShapeDtypeStruct(sizes, dtype)
    total = 4 * (2 * y - 1)
    return pl.pallas_call(
        functools.partial(dense_kernel, grid, rep_size),
        out_shape=[
            shape(high, tokens, features),
            shape(high, tokens, features),
            shape(high, 1, width),
            shape(low, z, x, rows, width),
            shape(low, z, x, units, features),
        ],
        in_specs=[pl.BlockSpec(memory_space=pltpu.VMEM)] * 5,
        out_specs=[pl.BlockSpec(memory_space=pltpu.VMEM)] * 5,
        scratch_shapes=[
            vmem(low, rep_size, tokens, features),
            vmem(low, rep_size, tokens, features),
            vmem(low, z * x, rep_size, tokens, rows),
            vmem(low, z * x, rep_size, tokens, units),
            vmem(high, rep_size, tokens, width),
            vmem(high, rep_size, tokens, width),
            vmem(low, rep_size, tokens, width),
            vmem(high, rep_size, tokens, features),
            vmem(low, rep_size, tokens, features),
            vmem(low, rep_size, tokens, features),
            vmem(low, y, tokens, features),
            vmem(low, y, tokens, features),
            vmem(low, y - 1, tokens, features),
            vmem(low, y - 1, tokens, features),
            pltpu.SemaphoreType.DMA((total,)),
            pltpu.SemaphoreType.DMA((total,)),
        ],
        compiler_params=pltpu.CompilerParams(
            collective_id=2, has_side_effects=True, vmem_limit_bytes=DENSE_VMEM
        ),
        name="dense_step",
    )(dense_input, cotangent, up_full, down_full, bias)


def attn_term_kernel(attn_ref, joined_ref, attended_ref, resid_ref, out_ref):
    blocks, rows, _ = out_ref.shape
    inner = joined_ref.shape[1]
    for s in range(blocks):
        for left_ref, right_ref, start in (
            (attn_ref, joined_ref, 0),
            (attended_ref, resid_ref, inner),
        ):
            left = left_ref[:, s * rows : (s + 1) * rows]
            value = inner_rows(left, right_ref[...]).astype(jnp.bfloat16)
            out_ref[s, :, start : start + right_ref.shape[1]] = value


def attn_terms(blocks, attn_input, joined_round, attended, resid_round):
    features = attn_input.shape[1]
    width = joined_round.shape[1] + resid_round.shape[1]
    return pl.pallas_call(
        attn_term_kernel,
        out_shape=jax.ShapeDtypeStruct((blocks, features // blocks, width), jnp.bfloat16),
        in_specs=[pl.BlockSpec(memory_space=pltpu.VMEM)] * 4,
        out_specs=pl.BlockSpec(memory_space=pltpu.VMEM),
        compiler_params=pltpu.CompilerParams(vmem_limit_bytes=REDUCE_VMEM),
        name="attn_terms",
    )(attn_input, joined_round, attended, resid_round)


def cut_kernel(parts, source_ref, out_ref):
    shard_size, rep_size, units = parts
    mine = lax.axis_index("rep")
    for r in range(rep_size):

        @pl.when(mine == r)
        def _():
            for s in range(shard_size):
                start = (s * rep_size + r) * units
                out_ref[:, s * units : (s + 1) * units] = source_ref[:, start : start + units]


def cut_units(weight, shard_size, rep_size):
    rows, width = weight.shape
    units = width // (shard_size * rep_size)
    return pl.pallas_call(
        functools.partial(cut_kernel, (shard_size, rep_size, units)),
        out_shape=jax.ShapeDtypeStruct((rows, shard_size * units), jnp.float32),
        in_specs=[pl.BlockSpec(memory_space=pltpu.VMEM)],
        out_specs=pl.BlockSpec(memory_space=pltpu.VMEM),
        compiler_params=pltpu.CompilerParams(vmem_limit_bytes=GATHER_VMEM),
        name="cut_units",
    )(weight)


def adam_rows(weight, first, second, grad_in, decay):
    first_next = beta_one * first + (1.0 - beta_one) * grad_in
    second_next = beta_two * second + (1.0 - beta_two) * grad_in * grad_in
    correct_one = 1.0 - beta_one**ADAM_STEP
    correct_two = 1.0 - beta_two**ADAM_STEP
    scale = jnp.sqrt(second_next * (1.0 / correct_two)) + adam_eps
    shrink = 1.0 - learn_rate * decay
    updated = shrink * weight - (learn_rate / correct_one) * first_next / scale
    return updated, first_next, second_next


def adam_kernel(parts, *refs):
    shard_size, rep_size, units = parts
    vec_w, vec_m, vec_g, attn_g, up_g, down_g = refs[:6]
    streams = [refs[6 + 2 * n : 8 + 2 * n] for n in range(3)]
    vec_new, vec_next = refs[12:14]
    outs = [refs[14 + 3 * n : 17 + 3 * n] for n in range(3)]
    wides = refs[23:]
    step = pl.program_id(0)

    @pl.when(step == 0)
    def _():
        rows = attn_g.shape[0]
        wides[0][...] = attn_g[...].astype(jnp.float32)
        for r in range(rep_size):
            values = up_g[r].astype(jnp.float32)
            for s in range(shard_size):
                start = (s * rep_size + r) * units
                wides[1][:, start : start + units] = values[:, s * units : (s + 1) * units]
        for r in range(rep_size):
            wides[2][r * units : (r + 1) * units, :] = down_g[r].astype(jnp.float32)
        new, first, second = adam_rows(vec_w[...], vec_m[0], vec_m[1], vec_g[...], 0.0)
        vec_new[...] = new
        vec_next[0] = first
        vec_next[1] = second

    for (weight, moments), (grad_out, new_out, next_out), wide in zip(streams, outs, wides):
        count = weight.shape[0]
        if count == wide.shape[0]:
            grad_in = wide[...]
        else:
            grad_in = wide[pl.ds(pl.multiple_of(step * count, 8), count), :]
        new, first, second = adam_rows(
            weight[...], moments[0], moments[1], grad_in, weight_decay
        )
        grad_out[...] = grad_in
        new_out[...] = new
        next_out[0] = first
        next_out[1] = second


def adam_all(rep_size, shard_size, attn, up, down, vector):
    rows, width = attn[0].shape
    units = up[2].shape[2] // shard_size
    steps = rows // 8 if rows % 8 == 0 and down[0].shape[0] % rows == 0 else 1
    flat, lead = [], []
    for weight, moments, _ in (attn, up, down):
        tall, wide = weight.shape
        part = tall // steps
        rows_spec = pl.BlockSpec((part, wide), lambda n: (n, 0))
        pair_spec = pl.BlockSpec((2, part, wide), lambda n: (0, n, 0))
        one = jax.ShapeDtypeStruct(weight.shape, jnp.float32)
        two = jax.ShapeDtypeStruct(moments.shape, jnp.float32)
        flat.append((rows_spec, pair_spec, one, two, pltpu.VMEM(weight.shape, jnp.float32)))
    fixed = lambda values: pl.BlockSpec(values.shape, lambda n: (0,) * values.ndim)
    held = [*vector, attn[2], up[2], down[2]]
    vec_out = [jax.ShapeDtypeStruct(values.shape, jnp.float32) for values in vector[:2]]
    return pl.pallas_call(
        functools.partial(adam_kernel, (shard_size, rep_size, units)),
        grid=(steps,),
        out_shape=vec_out + [shape for f in flat for shape in (f[2], f[2], f[3])],
        in_specs=[fixed(values) for values in held]
        + [spec for f in flat for spec in (f[0], f[1])],
        out_specs=[fixed(values) for values in vector[:2]]
        + [spec for f in flat for spec in (f[0], f[0], f[1])],
        scratch_shapes=[f[4] for f in flat],
        compiler_params=pltpu.CompilerParams(vmem_limit_bytes=ADAM_VMEM),
        name="adam_all",
    )(*held, attn[0], attn[1], up[0], up[1], down[0], down[1])


def shards(
    rep_size,
    shard_size,
    hidden_in,
    cotangent,
    segment_ids,
    attn_weight,
    attn_moments,
    up_weight,
    up_moments,
    down_weight,
    down_moments,
    vectors,
    vector_moments,
):
    grid = Grid(rep_size, shard_size)
    rep = lax.axis_index("rep")
    tokens, features = hidden_in.shape
    rows, width = up_weight.shape
    units = width // (shard_size * rep_size)
    own_cols = shard_size * units
    attn_block = attn_weight.astype(jnp.bfloat16)
    mine = lambda values, axis: lax.dynamic_index_in_dim(values, rep, axis, keepdims=False)
    up_block = cut_units(up_weight, shard_size, rep_size).astype(jnp.bfloat16)
    down_block = mine(down_weight.reshape(rep_size, units, features), 0).astype(jnp.bfloat16)
    attn_split = Split(*attn_block.shape, grid.y_size, 1.0)
    blocks = [attn_split.pad(attn_block), vectors.astype(jnp.bfloat16), up_block, down_block]
    attn_wide, vector_wide, up_full, down_full = gather_params(grid, attn_split, blocks)
    attn_full = attn_wide[:, :, :rows].reshape(-1, width)
    vector_full = vector_wide.transpose(2, 0, 1, 3).reshape(vectors.shape[0], -1)
    bias = mine(
        vector_full[8:].astype(jnp.float32).reshape(shard_size, rep_size, units), 1
    ).reshape(1, own_cols)

    residual, dense_input, stored = attention_forward(
        hidden_in[None], segment_ids, attn_full, vector_full
    )
    dense_out, dense_input_grad, unit_sums, up_terms, down_terms = dense_step(
        grid, rep_size, dense_input, cotangent, up_full, down_full, bias
    )
    block_out = (residual + dense_out + vector_full[7].astype(jnp.float32)).astype(jnp.bfloat16)
    input_grad, small_rows, attn_input, joined_round, attended, resid_round = attention_backward(
        cotangent[None], segment_ids, stored, attn_full, vector_full, dense_input_grad
    )
    unit_rows = lax.dynamic_update_index_in_dim(
        jnp.zeros((shard_size, rep_size, units), jnp.float32),
        unit_sums.reshape(shard_size, units),
        rep,
        1,
    ).reshape(-1, features)
    vector_terms = jnp.concatenate([small_rows, unit_rows], axis=0)
    attn_term = attn_terms(shard_size, attn_input, joined_round, attended, resid_round)
    grads = [attn_split.pad(attn_term.reshape(grid.z_size, grid.x_size, rows, width))]
    attn_owned, vector_total, up_slices, down_slices = reduce_grads(
        grid, [attn_split], grads, vector_terms, up_terms, down_terms
    )
    own_width = vectors.shape[1]
    vector_own = lax.dynamic_slice_in_dim(
        vector_total, lax.axis_index("shard") * own_width, own_width, 1
    )
    (
        new_vectors,
        vector_next,
        attn_grad,
        new_attn,
        attn_next,
        up_grad,
        new_up,
        up_next,
        down_grad,
        new_down,
        down_next,
    ) = adam_all(
        rep_size,
        shard_size,
        (attn_weight, attn_moments, attn_owned),
        (up_weight, up_moments, up_slices),
        (down_weight, down_moments, down_slices),
        (vectors, vector_moments, vector_own),
    )
    return (
        block_out,
        input_grad[0],
        attn_grad,
        up_grad,
        down_grad,
        vector_own,
        new_attn,
        attn_next,
        new_up,
        up_next,
        new_down,
        down_next,
        new_vectors,
        vector_next,
    )


def solution(mesh):
    in_specs = (
        P(("rep", "shard"), None),
        P(("rep", "shard"), None),
        P(("rep", "shard"), None),
        P("shard", None),
        P(None, "shard", None),
        P("shard", None),
        P(None, "shard", None),
        P("shard", None),
        P(None, "shard", None),
        P(None, "shard"),
        P(None, None, "shard"),
    )
    out_specs = (
        P(("rep", "shard"), None),
        P(("rep", "shard"), None),
        P("shard", None),
        P("shard", None),
        P("shard", None),
        P(None, "shard"),
        P("shard", None),
        P(None, "shard", None),
        P("shard", None),
        P(None, "shard", None),
        P("shard", None),
        P(None, "shard", None),
        P(None, "shard"),
        P(None, None, "shard"),
    )
    body = functools.partial(shards, mesh.shape["rep"], mesh.shape["shard"])
    return jax.shard_map(body, mesh=mesh, in_specs=in_specs, out_specs=out_specs, check_vma=False)
```

```python
import functools

import jax
import jax.numpy as jnp
import numpy as np
from jax import lax
from jax.experimental import pallas as pl
from jax.experimental.pallas import tpu as pltpu
from jax.sharding import PartitionSpec as P

HEAD_DIM = 64
ADAM_STEP = 3
MESH = pl.DeviceIdType.MESH


beta_one = 0.9
beta_two = 0.999
adam_eps = 1e-08
learn_rate = 0.25
weight_decay = 0.1


def matmul(left_arg, right_arg):
    return jnp.dot(left_arg, right_arg, preferred_element_type=jnp.float32)


def inner_rows(left_arg, right_arg):
    return lax.dot_general(
        left_arg, right_arg, (((0,), (0,)), ((), ())), preferred_element_type=jnp.float32
    )


def product(pattern, left_arg, right_arg):
    return jnp.einsum(pattern, left_arg, right_arg, preferred_element_type=jnp.float32)


def normalize(values):
    average = jnp.mean(values, axis=-1, keepdims=True)
    centred = values - average
    inv_std = lax.rsqrt(jnp.mean(centred * centred, axis=-1, keepdims=True) + 1e-05)
    return (centred * inv_std, inv_std)


def normalize_back(grad_in, normed, inv_std, gain_row):
    scaled = grad_in * gain_row
    return inv_std * (
        scaled
        - jnp.mean(scaled, axis=-1, keepdims=True)
        - normed * jnp.mean(scaled * normed, axis=-1, keepdims=True)
    )


def allowed(segments):
    row_count = segments.shape[-1]
    causal = lax.broadcasted_iota(jnp.int32, (row_count, row_count), 0) >= lax.broadcasted_iota(
        jnp.int32, (row_count, row_count), 1
    )
    same_doc = segments[:, :, None] == segments[:, None, :]
    return jnp.logical_and(same_doc, causal)[:, None, :, :]


def scores_of(queries, keys_all, segments):
    logits = product("bqhe,bkhe->bhqk", queries, keys_all) * HEAD_DIM ** (-0.5)
    return jnp.where(allowed(segments), logits, -1e30)


def attention_forward(activations, segments, attn_full, vector_full):
    batch_size, row_count, features = activations.shape
    head_count = features // HEAD_DIM
    head_shape = (batch_size, row_count, head_count, HEAD_DIM)
    vector_rows = vector_full.astype(jnp.float32)
    inputs_flat = activations.astype(jnp.float32).reshape(batch_size * row_count, features)
    normed_one, inv_one = normalize(inputs_flat)
    attn_input = (normed_one * vector_rows[0] + vector_rows[1]).astype(jnp.bfloat16)
    projected = matmul(attn_input, attn_full[:, : 3 * features])
    queries = (projected[:, :features] + vector_rows[2]).astype(jnp.bfloat16).reshape(head_shape)
    keys_all = projected[:, features : 2 * features].astype(jnp.bfloat16).reshape(head_shape)
    values_all = (
        (projected[:, 2 * features :] + vector_rows[3]).astype(jnp.bfloat16).reshape(head_shape)
    )
    logits = scores_of(queries, keys_all, segments)
    row_max = jnp.max(logits, axis=-1, keepdims=True)
    exponent = jnp.exp(logits - row_max)
    totals = jnp.sum(exponent, axis=-1, keepdims=True)
    log_total = row_max + jnp.log(totals)
    soft_probs = (exponent / totals).astype(jnp.bfloat16)
    attended = (
        product("bhqk,bkhe->bqhe", soft_probs, values_all)
        .reshape(batch_size * row_count, features)
        .astype(jnp.bfloat16)
    )
    residual = inputs_flat + matmul(attended, attn_full[:, 3 * features :]) + vector_rows[4]
    normed_two, inv_two = normalize(residual)
    dense_input = (normed_two * vector_rows[5] + vector_rows[6]).astype(jnp.bfloat16)
    stored = (
        normed_one,
        inv_one,
        attn_input,
        queries,
        keys_all,
        values_all,
        log_total,
        attended,
        normed_two,
        inv_two,
    )
    return (residual, dense_input, stored)


def attention_backward(cotangent, segments, stored, attn_full, vector_full, dense_input_grad):
    (
        normed_one,
        inv_one,
        attn_input,
        queries,
        keys_all,
        values_all,
        log_total,
        attended,
        normed_two,
        inv_two,
    ) = stored
    batch_size, row_count, features = cotangent.shape
    head_count = features // HEAD_DIM
    head_shape = (batch_size, row_count, head_count, HEAD_DIM)
    vector_rows = vector_full.astype(jnp.float32)
    out_float = cotangent.reshape(batch_size * row_count, features).astype(jnp.float32)
    resid_grad = out_float + normalize_back(dense_input_grad, normed_two, inv_two, vector_rows[5])
    resid_round = resid_grad.astype(jnp.bfloat16)
    attended_grad = lax.dot_general(
        resid_round,
        attn_full[:, 3 * features :],
        (((1,), (1,)), ((), ())),
        preferred_element_type=jnp.float32,
    ).astype(jnp.bfloat16)
    heads_grad = attended_grad.reshape(head_shape)
    logits = scores_of(queries, keys_all, segments)
    recomputed = jnp.exp(logits - log_total)
    prob_round = recomputed.astype(jnp.bfloat16)
    prob_grad = product("bqhe,bkhe->bhqk", heads_grad, values_all)
    delta_row = product("bqhe,bqhe->bhq", heads_grad, attended.reshape(head_shape))[..., None]
    logit_grad = (recomputed * (prob_grad - delta_row)).astype(jnp.bfloat16)
    scale_factor = HEAD_DIM ** (-0.5)
    query_grad = product("bhqk,bkhe->bqhe", logit_grad, keys_all) * scale_factor
    key_grad = product("bhqk,bqhe->bkhe", logit_grad, queries) * scale_factor
    value_grad = product("bhqk,bqhe->bkhe", prob_round, heads_grad)
    joined_grad = jnp.concatenate(
        [
            query_grad.reshape(-1, features),
            key_grad.reshape(-1, features),
            value_grad.reshape(-1, features),
        ],
        axis=1,
    )
    joined_round = joined_grad.astype(jnp.bfloat16)
    attn_input_grad = lax.dot_general(
        joined_round,
        attn_full[:, : 3 * features],
        (((1,), (1,)), ((), ())),
        preferred_element_type=jnp.float32,
    )
    input_grad = (
        (resid_grad + normalize_back(attn_input_grad, normed_one, inv_one, vector_rows[0]))
        .astype(jnp.bfloat16)
        .reshape(batch_size, row_count, features)
    )
    small_rows = jnp.stack(
        [
            jnp.sum(attn_input_grad * normed_one, axis=0),
            jnp.sum(attn_input_grad, axis=0),
            jnp.sum(joined_grad[:, :features], axis=0),
            jnp.sum(joined_grad[:, 2 * features :], axis=0),
            jnp.sum(resid_grad, axis=0),
            jnp.sum(dense_input_grad * normed_two, axis=0),
            jnp.sum(dense_input_grad, axis=0),
            jnp.sum(out_float, axis=0),
        ]
    )
    return (input_grad, small_rows, attn_input, joined_round, attended, resid_round)


CORES = 2
ROW_UNIT = 16
LANE_UNIT = 128
GATHER_VMEM = 16 * 2**20
REDUCE_VMEM = 42 * 2**20
TERMS_VMEM = 20 * 2**20
DENSE_VMEM = 46 * 2**20
ADAM_VMEM = 56 * 2**20


class Grid:
    def __init__(self, rep_size, shard_size):
        self.cores = CORES
        self.y_size = rep_size // CORES
        self.x_size = self.y_size if shard_size % self.y_size == 0 else 1
        self.z_size = shard_size // self.x_size

    def locate(self):
        rep = lax.axis_index("rep")
        shard = lax.axis_index("shard")
        self.y, self.c = lax.div(rep, CORES), lax.rem(rep, CORES)
        self.z, self.x = lax.div(shard, self.x_size), lax.rem(shard, self.x_size)
        return self

    def device(self, dz=0, dx=0, dy=0, dc=0):
        rep = lax.rem(self.y + dy, self.y_size) * CORES + lax.rem(self.c + dc, CORES)
        shard = lax.rem(self.z + dz, self.z_size) * self.x_size + lax.rem(self.x + dx, self.x_size)
        return (rep, shard)

    def partners(self):
        found = [self.device(dz=k) for k in range(1, self.z_size)]
        found += [self.device(dx=k) for k in range(1, self.x_size)]
        found += [self.device(dy=k) for k in range(1, self.y_size)]
        return found + [self.device(dc=1)]

    def greet(self):
        barrier = pltpu.get_barrier_semaphore()
        partners = self.partners()
        for partner in partners:
            pl.semaphore_signal(barrier, inc=1, device_id=partner, device_id_type=MESH)
        pl.semaphore_wait(barrier, len(partners))


class Split:
    def __init__(self, rows, columns, y_size, share=0.7, array=0, chunk=0, chunks=1):
        self.rows, self.columns, self.array = rows, columns, array
        self.by_lane = columns % (2 * LANE_UNIT) == 0
        unit = LANE_UNIT if self.by_lane else ROW_UNIT
        extent = columns if self.by_lane else rows
        padded = -(-extent // (2 * unit)) * 2 * unit
        if not self.by_lane:
            self.rows = padded
        pairs = padded // (2 * unit)
        chunks = max(1, min(chunks, pairs // (y_size + 1)))
        self.chunks = chunks
        least = (max(1, pairs // chunks) - 1) // y_size * y_size + 1
        starts = [0] + [pairs - least * (chunks - n) for n in range(1, chunks + 1)]
        units = starts[chunk + 1] - starts[chunk]
        self.unit = unit
        self.start = 2 * unit * starts[chunk]
        self.half = units * unit
        taken = min(max(1, int(units * share / y_size + 0.5)), (units - 1) // y_size)
        self.a_size = taken * unit
        self.b_start = y_size * self.a_size
        self.b_size = self.half - self.b_start

    def chunked(self, y_size, share, array, chunks):
        found = Split(self.rows, self.columns, y_size, share, array, 0, chunks)
        return [found] + [
            Split(self.rows, self.columns, y_size, share, array, n, chunks)
            for n in range(1, found.chunks)
        ]

    def block(self):
        return (self.rows, self.columns)

    def shape(self, size):
        return (self.rows, size) if self.by_lane else (size, self.columns)

    def cut(self, start, size):
        window = pl.ds(pl.multiple_of(self.start + start, self.unit), size)
        return (slice(None), window) if self.by_lane else (window, slice(None))

    def piece_a(self, y, c):
        return self.cut(c * self.half + y * self.a_size, self.a_size)

    def piece_b(self, c):
        return self.cut(c * self.half + self.b_start, self.b_size)

    def piece_half(self, c):
        return self.cut(c * self.half, self.half)

    def pad(self, values):
        extra = self.rows - values.shape[-2]
        if extra == 0:
            return values
        return jnp.pad(values, [(0, 0)] * (values.ndim - 2) + [(0, extra), (0, 0)])


def remote(source, target, send, recv, device):
    return pltpu.make_async_remote_copy(
        src_ref=source,
        dst_ref=target,
        send_sem=send,
        recv_sem=recv,
        device_id=device,
        device_id_type=MESH,
    )


class Semaphores:
    def __init__(self, array):
        self.array, self.used = array, 0

    def take(self):
        self.used += 1
        return self.array.at[self.used - 1]


def chosen(condition):
    return (lambda body: body()) if condition is True else pl.when(condition)


class Links:
    def __init__(self, send_array, recv_array):
        self.sends, self.recvs = send_array, recv_array
        self.copies = {}

    def launch(self, key, source, target, device, sent=True, got=True):
        n = len(self.copies)
        copy = remote(source, target, self.sends.at[n], self.recvs.at[n], device)
        self.copies[key] = (copy, sent, got)
        chosen(sent)(copy.start)

    def arrived(self, *keys):
        for key in keys:
            copy, _, got = self.copies[key]
            chosen(got)(copy.wait_recv)

    def wait(self, key):
        self.copies[key][0].wait_recv()

    def finish(self):
        for copy, sent, _ in self.copies.values():
            chosen(sent)(copy.wait_send)


GATHER_PLAN = {
    "zv": 0,
    "ub": 1,
    "ux": 2,
    "za": 3,
    "dx": 4,
    "xv": (5, 6, 7, 8),
    "xa": (9, 11, 14, 18),
    "u": (10, 13, 17),
    "ya": (12, 15, 19, 21),
    "db": 16,
    "d": (20, 23, 25),
    "c": (22, 24, 26, 27),
}
REDUCE_PLAN = {
    "c": (0, 2, 4),
    "dx": (1, 3, 10, 11),
    "v": (5, 8, 16, 25, 28),
    "y": (6, 7, 9),
    "d": (12, 13, 17, 20),
    "x": (14, 19, 24),
    "ux": (15, 18, 27, 29),
    "z": (21, 30, 34),
    "de": 22,
    "u": (23, 26, 32, 36),
    "f": (31, 35, 40),
    "dp": 33,
    "s": (37, 39, 42),
    "ue": 38,
    "up": 41,
}


def arrange(plan, counts):
    timed = []
    for name, places in plan.items():
        if isinstance(places, int):
            timed.append((places, name, ()))
            continue
        marks = np.linspace(0.0, 1.0, counts[name])
        spots = np.interp(marks, np.linspace(0.0, 1.0, len(places)), places)
        timed += [(float(spot), name, (n,)) for n, spot in enumerate(spots)]
    return [(name, index) for _, name, index in sorted(timed)]


def gather_kernel(grid, split, *refs):
    attn_own, vec_own, up_own, down_own = refs[:4]
    attn_full, vec_full, up_full, down_full = refs[4:8]
    links, local_array = Links(refs[8], refs[9]), refs[10]
    g = grid.locate()
    z_size, x_size, y_size = g.z_size, g.x_size, g.y_size
    hops = range(z_size - 1)
    near = lambda j: lax.rem(g.z + j + z_size, z_size)
    place = lambda j, i: (lax.rem(g.z + z_size - j, z_size), lax.rem(g.x + x_size - i, x_size))
    own = {"a": attn_own, "v": vec_own, "u": up_own, "d": down_own}
    full = {"a": attn_full, "v": vec_full, "u": up_full, "d": down_full}

    def windows(t):
        if t == "v":
            return [(slice(None), slice(None))]
        return [split.piece_a(g.y, g.c), split.piece_b(g.c)]

    def stage_z(t):
        for k in range(1, z_size):
            for p, window in enumerate(windows(t)):
                links.launch(
                    ("z", t, p, k),
                    own[t].at[window],
                    full[t].at[(g.z, g.x) + window],
                    g.device(dz=k),
                )

    def unit_x(t, j):
        for p, window in enumerate(windows(t)):
            here = place(j, 0) + window
            if j > 0:
                links.arrived(("z", t, p, j))
            source = own[t].at[window] if j == 0 else full[t].at[here]
            for i in range(1, x_size):
                links.launch(("x", t, p, j, i), source, full[t].at[here], g.device(dx=i))
            if t == "a" and p == 0 and j > 0:
                for k in range(1, y_size):
                    links.launch(("y", t, j, 0, k), source, full[t].at[here], g.device(dy=k))

    def unit_y(t, j):
        for i in range(1, x_size):
            for p, window in enumerate(windows(t)):
                links.arrived(("x", t, p, j, i))
                if t == "a" and p == 0:
                    here = full[t].at[place(j, i) + window]
                    for k in range(1, y_size):
                        links.launch(("y", t, j, i, k), here, here, g.device(dy=k))

    def unit_core(j):
        for i in range(x_size):
            if (j, i) == (0, 0):
                continue
            for k in range(1, y_size):
                links.arrived(("y", "a", j, i, k))
            here = attn_full.at[place(j, i) + split.piece_half(g.c)]
            links.launch(("c", j, i), here, here, g.device(dc=1))

    def hop(t, k):
        source = own[t] if k == 0 else full[t].at[near(-k), g.x]
        links.launch(
            ("right" + t, k),
            source,
            full[t].at[near(-k), g.x],
            g.device(dz=1),
            jnp.logical_and(g.z >= k, g.z + 1 < z_size),
            g.z >= k + 1,
        )
        source = own[t] if k == 0 else full[t].at[near(k), g.x]
        links.launch(
            ("left" + t, k),
            source,
            full[t].at[near(k), g.x],
            g.device(dz=z_size - 1),
            jnp.logical_and(g.z + k < z_size, g.z >= 1),
            g.z + 1 + k < z_size,
        )

    def across(name, t, source, where, held):
        for i in range(1, x_size):
            target = full[t].at[where, g.x]
            links.launch((name + t, i), source, target, g.device(dx=i), held, held)

    def begin(t):
        hop(t, 0)

    def direct(t):
        across("own", t, own[t], g.z, True)

    def advance(t, k):
        links.arrived(("right" + t, k), ("left" + t, k))
        if k + 1 < z_size - 1:
            hop(t, k + 1)
        across("r%d" % k, t, full[t].at[near(-k - 1), g.x], near(-k - 1), g.z >= k + 1)
        across("l%d" % k, t, full[t].at[near(k + 1), g.x], near(k + 1), g.z + 1 + k < z_size)

    def whole(t):
        for i in range(1, x_size):
            links.arrived(("own" + t, i))
            for k in hops:
                links.arrived(("r%d" % k + t, i), ("l%d" % k + t, i))

    g.greet()
    kept = []
    for n, t in enumerate(own):
        copy = pltpu.make_async_copy(own[t], full[t].at[g.z, g.x], local_array.at[n])
        copy.start()
        kept.append(copy)
    table = {"zv": (stage_z, "v"), "za": (stage_z, "a"), "c": (unit_core,)}
    table.update({"x" + t: (unit_x, t) for t in "va"})
    table["ya"] = (unit_y, "a")
    for t in "ud":
        table.update({t: (advance, t), t + "b": (begin, t), t + "x": (direct, t)})
    counts = {name: z_size - 1 if name in "ud" else z_size for name in table}
    for name, index in arrange(GATHER_PLAN, counts):
        table[name][0](*table[name][1:], *index)
    for j in range(z_size):
        unit_y("v", j)
    whole("u")
    whole("d")
    for j in range(z_size):
        for i in range(x_size):
            if (j, i) != (0, 0):
                links.arrived(("c", j, i))
    links.finish()
    for copy in kept:
        copy.wait()


def gather_params(grid, split, blocks):
    z, x, y = grid.z_size, grid.x_size, grid.y_size
    total = 2 * (z - 1) + 2 * z * (x - 1) + (z * x - 1) * y
    total += (z - 1) + z * (x - 1) + 2 * (2 * (z - 1) + (x - 1) * (2 * z - 1))
    any_spec = pl.BlockSpec(memory_space=pl.ANY)
    return pl.pallas_call(
        functools.partial(gather_kernel, grid, split),
        out_shape=[jax.ShapeDtypeStruct((z, x) + block.shape, jnp.bfloat16) for block in blocks],
        in_specs=[pl.BlockSpec(memory_space=pltpu.VMEM)] * 4,
        out_specs=[any_spec] * 4,
        scratch_shapes=[
            pltpu.SemaphoreType.DMA((total,)),
            pltpu.SemaphoreType.DMA((total,)),
            pltpu.SemaphoreType.DMA((4,)),
        ],
        compiler_params=pltpu.CompilerParams(
            collective_id=0, has_side_effects=True, vmem_limit_bytes=GATHER_VMEM
        ),
        name="gather_params",
    )(*blocks)


def plus(left_arg, right_arg):
    return left_arg.astype(jnp.float32) + right_arg.astype(jnp.float32)


def reduce_kernel(grid, splits, *refs):
    count = len(splits)
    arrays = splits[-1].array + 1
    vector_in, up_terms, down_terms = refs[arrays : arrays + 3]
    grads = [refs[split.array] for split in splits]
    outs = [refs[arrays + 3 + split.array] for split in splits]
    vector_out, up_out, down_out = refs[2 * arrays + 3 : 2 * arrays + 6]
    scratch, slim = refs[2 * arrays + 6 : -11], refs[-11:]
    per = 12
    buffers = [scratch[per * t : per * (t + 1)] for t in range(count)]
    v_core, v_y, v_x, v_z, v_one, v_two, v_three, send_array, recv_array, local_array = scratch[
        per * count :
    ]
    sends, recvs, locals_ = (
        Semaphores(send_array),
        Semaphores(recv_array),
        Semaphores(local_array),
    )
    g = grid.locate()
    z_size, x_size, y_size = g.z_size, g.x_size, g.y_size
    copies, moves = {}, {}

    def launch(key, source, target, device):
        copy = remote(source, target, sends.take(), recvs.take(), device)
        copy.start()
        copies[key] = copy

    def move(key, source, target):
        copy = pltpu.make_async_copy(source, target, locals_.take())
        copy.start()
        moves[key] = copy

    def each_block(body):
        @pl.loop(0, z_size * x_size)
        def _(index):
            body(lax.div(index, x_size), lax.rem(index, x_size))

    everything = (slice(None), slice(None))
    other_y = lambda k: lax.rem(g.y + k, y_size)
    other_x = lambda k: lax.rem(g.x + k, x_size)
    other_z = lambda k: lax.rem(g.z + k, z_size)

    def stage_core(t):
        acc_a, acc_b, got_a, got_b = buffers[t][:4]
        split = splits[t]
        for q in range(y_size):
            launch(
                ("ca", t, q),
                grads[t].at[everything + split.piece_a(q, 1 - g.c)],
                got_a.at[q],
                g.device(dc=1),
            )
            move(("la", t, q), grads[t].at[everything + split.piece_a(q, g.c)], acc_a.at[q])
        launch(
            ("cb", t),
            grads[t].at[everything + split.piece_b(1 - g.c)],
            got_b,
            g.device(dc=1),
        )
        move(("lb", t), grads[t].at[everything + split.piece_b(g.c)], acc_b)

    def stage_y(t):
        acc_a, acc_b, got_a, got_b, got_y = buffers[t][:5]
        for q in range(y_size):
            copies["ca", t, q].wait_recv()
            moves["la", t, q].wait()

            def add_a(i, j, q=q):
                acc_a[q, i, j] = plus(acc_a[q, i, j], got_a[q, i, j]).astype(jnp.bfloat16)

            each_block(add_a)
        for k in range(1, y_size):
            launch(("ya", t, k), acc_a.at[other_y(k)], got_y.at[k - 1], g.device(dy=k))
        copies["cb", t].wait_recv()
        moves["lb", t].wait()

        def add_b(i, j):
            acc_b[i, j] = plus(acc_b[i, j], got_b[i, j]).astype(jnp.bfloat16)

        each_block(add_b)
        for k in range(1, x_size):
            launch(
                ("xb", t, k), acc_b.at[:, other_x(k)], buffers[t][6].at[k - 1], g.device(dx=k)
            )

    def stage_x(t):
        acc_a, got_y, got_xa = buffers[t][0], buffers[t][4], buffers[t][5]
        for k in range(1, y_size):
            copies["ya", t, k].wait_recv()

        def add(i, j):
            value = acc_a[g.y, i, j].astype(jnp.float32)
            for k in range(1, y_size):
                value = plus(value, got_y[k - 1, i, j])
            acc_a[g.y, i, j] = value.astype(jnp.bfloat16)

        each_block(add)
        for k in range(1, x_size):
            launch(
                ("xa", t, k), acc_a.at[g.y, :, other_x(k)], got_xa.at[k - 1], g.device(dx=k)
            )

    def stage_z(t):
        acc_a, acc_b = buffers[t][:2]
        got_xa, got_xb, got_za, got_zb = buffers[t][5:9]
        for k in range(1, x_size):
            copies["xb", t, k].wait_recv()
            copies["xa", t, k].wait_recv()

        @pl.loop(0, z_size)
        def _(i):
            value_a = acc_a[g.y, i, g.x].astype(jnp.float32)
            for k in range(1, x_size):
                value_a = plus(value_a, got_xa[k - 1, i])
            acc_a[g.y, i, g.x] = value_a.astype(jnp.bfloat16)
            value_b = acc_b[i, g.x].astype(jnp.float32)
            for k in range(1, x_size):
                value_b = plus(value_b, got_xb[k - 1, i])
            acc_b[i, g.x] = value_b.astype(jnp.bfloat16)

        for k in range(1, z_size):
            launch(
                ("zb", t, k), acc_b.at[other_z(k), g.x], got_zb.at[k - 1], g.device(dz=k)
            )
            launch(
                ("za", t, k),
                acc_a.at[g.y, other_z(k), g.x],
                got_za.at[k - 1],
                g.device(dz=k),
            )

    def stage_final(t):
        acc_a, acc_b = buffers[t][:2]
        got_za, got_zb, final_a, ring_b, final_b = buffers[t][7:12]
        split = splits[t]
        for k in range(1, z_size):
            copies["zb", t, k].wait_recv()
        value = acc_b[g.z, g.x].astype(jnp.float32)
        for k in range(1, z_size):
            value = plus(value, got_zb[k - 1])
        ring_b[0] = value.astype(jnp.bfloat16)
        for k in range(1, y_size):
            launch(("yb", t, k), ring_b.at[0], ring_b.at[k], g.device(dy=k))
        for k in range(1, z_size):
            copies["za", t, k].wait_recv()
        value = acc_a[g.y, g.z, g.x].astype(jnp.float32)
        for k in range(1, z_size):
            value = plus(value, got_za[k - 1])
        final_a[...] = value.astype(jnp.bfloat16)
        target = outs[t].at[split.piece_a(g.y, g.c)]
        for k in range(1, y_size):
            launch(("oa", t, k), final_a, target, g.device(dy=k))
        move(("fa", t), final_a, target)

    def stage_share(t):
        ring_b, final_b = buffers[t][10:12]
        split = splits[t]
        for k in range(1, y_size):
            copies["yb", t, k].wait_recv()
        value = ring_b[g.y].astype(jnp.float32)
        for k in range(1, y_size):
            value = plus(value, ring_b[lax.rem(g.y + y_size - k, y_size)])
        final_b[...] = value.astype(jnp.bfloat16)
        move(("fb", t), final_b, outs[t].at[split.piece_b(g.c)])
        for k in range(1, y_size):
            copies["oa", t, k].wait_recv()
        moves["fa", t].wait()
        moves["fb", t].wait()
        half = outs[t].at[split.piece_half(g.c)]
        launch(("h", t), half, half, g.device(dc=1))

    def sum_ring(buffer, place, size):
        value = buffer[place]
        for k in range(1, size):
            value = value + buffer[lax.rem(place + size - k, size)]
        return value

    def vector_step(name, source, got, size, **direction):
        (axis,) = direction
        got[0] = source[...]
        for k in range(1, size):
            launch((name, k), source, got.at[k], g.device(**{axis: k}))

    def vector_sum(name, got, place, size, target):
        for k in range(1, size):
            copies[name, k].wait_recv()
        target[...] = sum_ring(got, place, size)

    up_x, down_x, up_z, down_z, up_sum, down_sum, up_own, down_own = slim[:8]
    links = Links(slim[8], slim[9])
    rep = lax.axis_index("rep")
    terms = {"u": up_terms, "d": down_terms}
    sums = {"u": up_sum, "d": down_sum}
    got_x, got_z = {"u": up_x, "d": down_x}, {"u": up_z, "d": down_z}
    owned, shared = {"u": up_own, "d": down_own}, {"u": up_out, "d": down_out}

    def ranked(n):
        last = z_size - 1
        later = lax.div(lax.div(n + g.z, last) + 1, 2)
        return later * (n - last + g.z) + (1 - later) * (last - n)

    def slim_x(t, *some):
        for n in some or range(z_size):
            for k in range(1, x_size):
                links.launch(
                    ("rx" + t, k, n),
                    terms[t].at[ranked(n), other_x(k)],
                    got_x[t].at[k - 1, ranked(n)],
                    g.device(dx=k),
                )

    def fold(t, n):
        for k in range(1, x_size):
            links.arrived(("rx" + t, k, n))
        here = ranked(n)
        value = terms[t][here, g.x].astype(jnp.float32)
        for k in range(1, x_size):
            value = plus(value, got_x[t][k - 1, here])
        sums[t][here] = value.astype(jnp.bfloat16)

    def toward(t, key, step, goal, sent, got, slot, first, device):
        if step > 0:

            @pl.when(jnp.logical_and(sent, jnp.logical_not(first)))
            def _():
                links.wait((key + t, step - 1))
                sums[t][goal] = plus(sums[t][goal], got_z[t][slot]).astype(jnp.bfloat16)

        target = got_z[t].at[slot]
        links.launch((key + t, step), sums[t].at[goal], target, device, sent, got)

    def slim_z(t, step):
        fold(t, step)
        if step == z_size - 1:
            return
        goal = lax.rem(2 * z_size - 1 - step + g.z, z_size)
        got = jnp.logical_and(g.z >= 1, g.z <= step + 1)
        toward(t, "pr", step, goal, g.z <= step, got, goal + 1, g.z == 0, g.device(dz=1))
        back = z_size - 1 - g.z
        goal = lax.rem(step + 1 + g.z, z_size)
        got = jnp.logical_and(back >= 1, back <= step + 1)
        device = g.device(dz=z_size - 1)
        toward(t, "pl", step, goal, back <= step, got, goal, back == 0, device)

    def slim_end(t):
        for key, some, slot in (("pr", g.z >= 1, g.z + 1), ("pl", g.z + 1 < z_size, g.z)):

            @pl.when(some)
            def _(key=key, slot=slot):
                links.wait((key + t, z_size - 2))
                sums[t][g.z] = plus(sums[t][g.z], got_z[t][slot]).astype(jnp.bfloat16)

        owned[t][...] = sums[t][g.z]
        for k in range(1, y_size):
            links.launch(("oy" + t, k), owned[t], shared[t].at[rep], g.device(dy=k))
        links.launch(("oc" + t, 0), owned[t], shared[t].at[rep], g.device(dc=1))
        n = 0 if t == "d" else 1
        copy = pltpu.make_async_copy(owned[t], shared[t].at[rep], slim[10].at[n])
        copy.start()
        moves["own" + t] = copy

    def slim_pass(t):
        for k in range(1, y_size):
            links.arrived(("oy" + t, k))
            here = shared[t].at[lax.rem(g.y + y_size - k, y_size) * CORES + g.c]
            links.launch(("oc" + t, k), here, here, g.device(dc=1))

    def small(n):
        if n == 0:
            vector_step("vc", vector_in, v_core, CORES, dc=1)
        if n == 1:
            vector_sum("vc", v_core, g.c, CORES, v_one)
            vector_step("vy", v_one, v_y, y_size, dy=1)
        if n == 2:
            vector_sum("vy", v_y, g.y, y_size, v_two)
            vector_step("vx", v_two, v_x, x_size, dx=1)
        if n == 3:
            vector_sum("vx", v_x, g.x, x_size, v_three)
            vector_step("vz", v_three, v_z, z_size, dz=1)
        if n == 4:
            vector_sum("vz", v_z, g.z, z_size, vector_out)

    g.greet()
    table = {"c": stage_core, "y": stage_y, "x": stage_x, "z": stage_z, "f": stage_final}
    table.update({"s": stage_share, "v": small})
    for t in ("d", "u"):
        table[t] = functools.partial(slim_z, t)
        table[t + "x"] = functools.partial(slim_x, t)
        table[t + "e"] = functools.partial(slim_end, t)
        table[t + "p"] = functools.partial(slim_pass, t)
    counts = {name: count if name in "cyxzfs" else z_size for name in table}
    counts["v"] = 5
    for name, index in arrange(REDUCE_PLAN, counts):
        table[name](*index)
    for key, copy in copies.items():
        if key[0] == "h":
            copy.wait_recv()
        copy.wait_send()
    for t in ("d", "u"):
        for k in range(y_size):
            links.arrived(("oc" + t, k))
        moves["own" + t].wait()
    links.finish()


def reduce_grads(grid, whole, grads, vector_terms, up_terms, down_terms):
    z, x, y = grid.z_size, grid.x_size, grid.y_size
    splits = []
    for array, split in enumerate(whole):
        splits += split.chunked(y, 0.85, array, 3)
    scratch = []
    for split in splits:
        a, b = split.shape(split.a_size), split.shape(split.b_size)
        scratch += [
            pltpu.VMEM(shape, jnp.bfloat16)
            for shape in (
                (y, z, x) + a,
                (z, x) + b,
                (y, z, x) + a,
                (z, x) + b,
                (y - 1, z, x) + a,
                (x - 1, z) + a,
                (x - 1, z) + b,
                (z - 1,) + a,
                (z - 1,) + b,
                a,
                (y,) + b,
                b,
            )
        ]
    small = vector_terms.shape
    scratch += [pltpu.VMEM((size,) + small, jnp.float32) for size in (CORES, y, x, z)]
    scratch += [pltpu.VMEM(small, jnp.float32)] * 3
    per_tensor = (y + 1) + (y - 1) + 2 * (x - 1) + 2 * (z - 1) + 2 * (y - 1) + 1
    total = len(splits) * per_tensor + 1 + (y - 1) + (x - 1) + (z - 1)
    scratch += [
        pltpu.SemaphoreType.DMA((total,)),
        pltpu.SemaphoreType.DMA((total,)),
        pltpu.SemaphoreType.DMA((len(splits) * (y + 3),)),
    ]
    slim = [up_terms.shape[2:], down_terms.shape[2:]]
    for lead in ((x - 1, z), (z + 1,), (z,), ()):
        scratch += [pltpu.VMEM(lead + block, jnp.bfloat16) for block in slim]
    extra = 2 * (z * (x - 1) + 2 * (z - 1) + 2 * y - 1)
    scratch += [pltpu.SemaphoreType.DMA((size,)) for size in (extra, extra, 2)]
    rep_size = y * CORES
    return pl.pallas_call(
        functools.partial(reduce_kernel, grid, splits),
        out_shape=[jax.ShapeDtypeStruct(split.block(), jnp.bfloat16) for split in whole]
        + [jax.ShapeDtypeStruct(small, jnp.float32)]
        + [jax.ShapeDtypeStruct((rep_size,) + block, jnp.bfloat16) for block in slim],
        in_specs=[pl.BlockSpec(memory_space=pl.ANY)] * len(whole)
        + [pl.BlockSpec(memory_space=pltpu.VMEM)] * 3,
        out_specs=[pl.BlockSpec(memory_space=pl.ANY)] * len(whole)
        + [pl.BlockSpec(memory_space=pltpu.VMEM)]
        + [pl.BlockSpec(memory_space=pl.ANY)] * 2,
        scratch_shapes=scratch,
        compiler_params=pltpu.CompilerParams(
            collective_id=1, has_side_effects=True, vmem_limit_bytes=REDUCE_VMEM
        ),
        name="reduce_grads",
    )(*grads, vector_terms, up_terms, down_terms)


def outer_rows(left_arg, right_arg):
    return lax.dot_general(
        left_arg, right_arg, (((1,), (1,)), ((), ())), preferred_element_type=jnp.float32
    )


def dense_kernel(grid, rep_size, *refs):
    dense_ref, cot_ref, up_full, down_full, bias_ref = refs[:5]
    out_ref, back_ref, sums_ref, up_grad, down_grad = refs[5:10]
    (
        dense_all,
        cot_all,
        inputs_cut,
        hidden_cut,
        slope,
        hidden_grad,
        hidden_round,
        wide_grad,
        out_part,
        back_part,
        out_core,
        back_core,
        out_y,
        back_y,
        send_array,
        recv_array,
    ) = refs[10:]
    links = Links(send_array, recv_array)
    g = grid.locate()
    z_size, x_size, y_size = g.z_size, g.x_size, g.y_size
    shard_size = z_size * x_size
    rep = lax.axis_index("rep")
    tokens, features = dense_ref.shape
    rows, width = up_full.shape[2:]
    units = down_full.shape[2]
    total = rep_size * tokens
    split = lambda n: (n // x_size, n % x_size)
    rep_at = lambda dy, dc: lax.rem(g.y + dy, y_size) * CORES + lax.rem(g.c + dc, CORES)

    barrier = pltpu.get_barrier_semaphore()
    partners = [g.device(dy=k) for k in range(1, y_size)] + [g.device(dc=1)]
    for partner in partners:
        pl.semaphore_signal(barrier, inc=1, device_id=partner, device_id_type=MESH)
    pl.semaphore_wait(barrier, len(partners))

    def spread(name, source, target):
        for k in range(1, y_size):
            links.launch((name, "y", k), source, target.at[rep], g.device(dy=k))
        links.launch((name, "c", 0), source, target.at[rep], g.device(dc=1))

    def pass_on(name, target):
        for k in range(1, y_size):
            links.arrived((name, "y", k))
            here = target.at[rep_at(y_size - k, 0)]
            links.launch((name, "c", k), here, here, g.device(dc=1))

    def spread_end(name):
        for k in range(y_size):
            links.arrived((name, "c", k))

    def term(target, left, right):
        @pl.loop(0, shard_size)
        def _(s):
            one = left[s].reshape(total, left.shape[-1])
            two = right[...].reshape(total, right.shape[-1])
            value = inner_rows(one, two)
            target[lax.div(s, x_size), lax.rem(s, x_size)] = value.astype(jnp.bfloat16)

    def scatter(name, part, got):
        for k in range(y_size):
            links.launch((name, "c", k), part.at[rep_at(k, 1)], got.at[k], g.device(dc=1))

    def scatter_y(name, part, core, got):
        for k in list(range(1, y_size)) + [0]:
            links.arrived((name, "c", k))
            there = rep_at(k, 0)
            part[there] = plus(part[there], core[k]).astype(jnp.bfloat16)
            if k > 0:
                links.launch((name, "y", k), part.at[there], got.at[k - 1], g.device(dy=k))

    def collect(name, part, got, target):
        value = part[rep].astype(jnp.float32)
        for k in range(1, y_size):
            links.arrived((name, "y", k))
            value = plus(value, got[k - 1])
        target[...] = value

    spread("dense", dense_ref, dense_all)
    spread("cot", cot_ref, cot_all)
    dense_all[rep] = dense_ref[...]
    cot_all[rep] = cot_ref[...]

    def hidden_of(b):
        values = dense_all[b].astype(jnp.float32)
        for s in range(shard_size):
            inputs_cut[s, b] = values[:, s * rows : (s + 1) * rows].astype(jnp.bfloat16)
        pre = jnp.broadcast_to(bias_ref[...], (tokens, width))
        for s in range(shard_size):
            pre = pre + matmul(inputs_cut[s, b], up_full[split(s)])
        normal_cdf = 0.5 * (1.0 + lax.erf(pre * 0.7071067811865476))
        density = jnp.exp(-0.5 * pre * pre) * 0.3989422804014327
        slope[b] = normal_cdf + pre * density
        hidden = pre * normal_cdf
        for s in range(shard_size):
            hidden_cut[s, b] = hidden[:, s * units : (s + 1) * units].astype(jnp.bfloat16)
        value = matmul(hidden_cut[0, b], down_full[split(0)])
        for s in range(1, shard_size):
            value = value + matmul(hidden_cut[s, b], down_full[split(s)])
        out_part[b] = value.astype(jnp.bfloat16)

    pass_on("dense", dense_all)
    spread_end("dense")
    pl.loop(0, rep_size)(hidden_of)
    scatter("out", out_part, out_core)
    pass_on("cot", cot_all)
    spread_end("cot")

    for s in range(shard_size):
        value = outer_rows(cot_all[...].reshape(total, features), down_full[split(s)])
        hidden_grad[:, :, s * units : (s + 1) * units] = value.reshape(rep_size, tokens, units)
    sums_ref[...] = jnp.zeros_like(sums_ref)

    @pl.loop(0, rep_size)
    def _(b):
        value = hidden_grad[b] * slope[b]
        sums_ref[...] += jnp.sum(value, axis=0, keepdims=True)
        hidden_round[b] = value.astype(jnp.bfloat16)

    scatter_y("out", out_part, out_core, out_y)
    for s in range(shard_size):
        value = outer_rows(hidden_round[...].reshape(total, width), up_full[split(s)])
        wide_grad[:, :, s * rows : (s + 1) * rows] = value.reshape(rep_size, tokens, rows)

    @pl.loop(0, rep_size)
    def _(b):
        back_part[b] = wide_grad[b].astype(jnp.bfloat16)

    scatter("back", back_part, back_core)
    term(up_grad, inputs_cut, hidden_round)
    scatter_y("back", back_part, back_core, back_y)
    term(down_grad, hidden_cut, cot_all)
    collect("out", out_part, out_y, out_ref)
    collect("back", back_part, back_y, back_ref)
    links.finish()


def dense_step(grid, rep_size, dense_input, cotangent, up_full, down_full, bias):
    z, x, y = grid.z_size, grid.x_size, grid.y_size
    tokens, features = dense_input.shape
    rows, width = up_full.shape[2:]
    units = down_full.shape[2]
    low, high = jnp.bfloat16, jnp.float32
    vmem = lambda dtype, *shape: pltpu.VMEM(shape, dtype)
    shape = lambda dtype, *sizes: jax.ShapeDtypeStruct(sizes, dtype)
    total = 4 * (2 * y - 1)
    return pl.pallas_call(
        functools.partial(dense_kernel, grid, rep_size),
        out_shape=[
            shape(high, tokens, features),
            shape(high, tokens, features),
            shape(high, 1, width),
            shape(low, z, x, rows, width),
            shape(low, z, x, units, features),
        ],
        in_specs=[pl.BlockSpec(memory_space=pltpu.VMEM)] * 5,
        out_specs=[pl.BlockSpec(memory_space=pltpu.VMEM)] * 5,
        scratch_shapes=[
            vmem(low, rep_size, tokens, features),
            vmem(low, rep_size, tokens, features),
            vmem(low, z * x, rep_size, tokens, rows),
            vmem(low, z * x, rep_size, tokens, units),
            vmem(high, rep_size, tokens, width),
            vmem(high, rep_size, tokens, width),
            vmem(low, rep_size, tokens, width),
            vmem(high, rep_size, tokens, features),
            vmem(low, rep_size, tokens, features),
            vmem(low, rep_size, tokens, features),
            vmem(low, y, tokens, features),
            vmem(low, y, tokens, features),
            vmem(low, y - 1, tokens, features),
            vmem(low, y - 1, tokens, features),
            pltpu.SemaphoreType.DMA((total,)),
            pltpu.SemaphoreType.DMA((total,)),
        ],
        compiler_params=pltpu.CompilerParams(
            collective_id=2, has_side_effects=True, vmem_limit_bytes=DENSE_VMEM
        ),
        name="dense_step",
    )(dense_input, cotangent, up_full, down_full, bias)


def attn_term_kernel(attn_ref, joined_ref, attended_ref, resid_ref, out_ref):
    blocks, rows, _ = out_ref.shape
    inner = joined_ref.shape[1]
    for s in range(blocks):
        for left_ref, right_ref, start in (
            (attn_ref, joined_ref, 0),
            (attended_ref, resid_ref, inner),
        ):
            left = left_ref[:, s * rows : (s + 1) * rows]
            value = inner_rows(left, right_ref[...]).astype(jnp.bfloat16)
            out_ref[s, :, start : start + right_ref.shape[1]] = value


def attn_terms(blocks, attn_input, joined_round, attended, resid_round):
    features = attn_input.shape[1]
    width = joined_round.shape[1] + resid_round.shape[1]
    return pl.pallas_call(
        attn_term_kernel,
        out_shape=jax.ShapeDtypeStruct((blocks, features // blocks, width), jnp.bfloat16),
        in_specs=[pl.BlockSpec(memory_space=pltpu.VMEM)] * 4,
        out_specs=pl.BlockSpec(memory_space=pltpu.VMEM),
        compiler_params=pltpu.CompilerParams(vmem_limit_bytes=TERMS_VMEM),
        name="attn_terms",
    )(attn_input, joined_round, attended, resid_round)


def cut_kernel(parts, source_ref, out_ref):
    shard_size, rep_size, units = parts
    mine = lax.axis_index("rep")
    for r in range(rep_size):

        @pl.when(mine == r)
        def _():
            for s in range(shard_size):
                start = (s * rep_size + r) * units
                out_ref[:, s * units : (s + 1) * units] = source_ref[:, start : start + units]


def cut_units(weight, shard_size, rep_size):
    rows, width = weight.shape
    units = width // (shard_size * rep_size)
    return pl.pallas_call(
        functools.partial(cut_kernel, (shard_size, rep_size, units)),
        out_shape=jax.ShapeDtypeStruct((rows, shard_size * units), jnp.float32),
        in_specs=[pl.BlockSpec(memory_space=pltpu.VMEM)],
        out_specs=pl.BlockSpec(memory_space=pltpu.VMEM),
        compiler_params=pltpu.CompilerParams(vmem_limit_bytes=GATHER_VMEM),
        name="cut_units",
    )(weight)


def adam_rows(weight, first, second, grad_in, decay):
    first_next = beta_one * first + (1.0 - beta_one) * grad_in
    second_next = beta_two * second + (1.0 - beta_two) * grad_in * grad_in
    correct_one = 1.0 - beta_one**ADAM_STEP
    correct_two = 1.0 - beta_two**ADAM_STEP
    scale = jnp.sqrt(second_next * (1.0 / correct_two)) + adam_eps
    shrink = 1.0 - learn_rate * decay
    updated = shrink * weight - (learn_rate / correct_one) * first_next / scale
    return updated, first_next, second_next


def adam_kernel(parts, *refs):
    shard_size, rep_size, units, steps = parts
    vec_w, vec_m, vec_g, attn_g, up_g, down_g = refs[:6]
    sources = [refs[6 + 2 * n : 8 + 2 * n] for n in range(3)]
    vec_new, vec_next = refs[12:14]
    targets = [refs[14 + 3 * n : 17 + 3 * n] for n in range(3)]
    held = [refs[23 + 3 * n : 26 + 3 * n] for n in range(3)]
    in_array, out_array = refs[32:34]

    def window(ref, n):
        count = ref.shape[-2] // steps
        rows = slice(None) if steps == 1 else pl.ds(pl.multiple_of(n * count, 8), count)
        return (slice(None),) * (len(ref.shape) - 2) + (rows, slice(None))

    def loads(t, n):
        pairs = zip(sources[t], held[t][1:])
        return [
            pltpu.make_async_copy(
                source.at[window(source, n)], kept.at[window(kept, n)], in_array.at[t, k, n]
            )
            for k, (source, kept) in enumerate(pairs)
        ]

    def stores(t, n):
        pairs = zip(held[t], targets[t])
        return [
            pltpu.make_async_copy(
                kept.at[window(kept, n)], target.at[window(target, n)], out_array.at[t, k, n]
            )
            for k, (kept, target) in enumerate(pairs)
        ]

    @pl.loop(0, steps)
    def _(n):
        for t in range(3):
            for copy in loads(t, n):
                copy.start()

    held[0][0][...] = attn_g[...].astype(jnp.float32)
    for r in range(rep_size):
        values = up_g[r].astype(jnp.float32)
        for s in range(shard_size):
            start = (s * rep_size + r) * units
            held[1][0][:, start : start + units] = values[:, s * units : (s + 1) * units]
    for r in range(rep_size):
        held[2][0][r * units : (r + 1) * units, :] = down_g[r].astype(jnp.float32)
    new, first, second = adam_rows(vec_w[...], vec_m[0], vec_m[1], vec_g[...], 0.0)
    vec_new[...] = new
    vec_next[0] = first
    vec_next[1] = second

    @pl.loop(0, steps)
    def _(n):
        for t in range(3):
            for copy in loads(t, n):
                copy.wait()
            grads, weight, moments = held[t]
            here, both = window(weight, n), window(moments, n)[1:]
            new, first, second = adam_rows(
                weight[here], moments[(0,) + both], moments[(1,) + both], grads[here], weight_decay
            )
            weight[here] = new
            moments[(0,) + both] = first
            moments[(1,) + both] = second
            for copy in stores(t, n):
                copy.start()

    @pl.loop(0, steps)
    def _(n):
        for t in range(3):
            for copy in stores(t, n):
                copy.wait()


def adam_all(rep_size, shard_size, attn, up, down, vector):
    rows, width = attn[0].shape
    units = up[2].shape[2] // shard_size
    steps = rows // 8 if rows % 8 == 0 and down[0].shape[0] % rows == 0 else 1
    shapes, scratch = [], []
    for weight, moments, _ in (attn, up, down):
        for values in (weight, weight, moments):
            shapes.append(jax.ShapeDtypeStruct(values.shape, jnp.float32))
            scratch.append(pltpu.VMEM(values.shape, jnp.float32))
    vmem_spec, any_spec = (pl.BlockSpec(memory_space=space) for space in (pltpu.VMEM, pl.ANY))
    vec_out = [jax.ShapeDtypeStruct(values.shape, jnp.float32) for values in vector[:2]]
    return pl.pallas_call(
        functools.partial(adam_kernel, (shard_size, rep_size, units, steps)),
        out_shape=vec_out + shapes,
        in_specs=[vmem_spec] * 6 + [any_spec] * 6,
        out_specs=[vmem_spec] * 2 + [any_spec] * 9,
        scratch_shapes=scratch
        + [pltpu.SemaphoreType.DMA((3, 2, steps)), pltpu.SemaphoreType.DMA((3, 3, steps))],
        compiler_params=pltpu.CompilerParams(vmem_limit_bytes=ADAM_VMEM),
        name="adam_all",
    )(*vector, attn[2], up[2], down[2], attn[0], attn[1], up[0], up[1], down[0], down[1])


def shards(
    rep_size,
    shard_size,
    hidden_in,
    cotangent,
    segment_ids,
    attn_weight,
    attn_moments,
    up_weight,
    up_moments,
    down_weight,
    down_moments,
    vectors,
    vector_moments,
):
    grid = Grid(rep_size, shard_size)
    rep = lax.axis_index("rep")
    tokens, features = hidden_in.shape
    rows, width = up_weight.shape
    units = width // (shard_size * rep_size)
    own_cols = shard_size * units
    attn_block = attn_weight.astype(jnp.bfloat16)
    mine = lambda values, axis: lax.dynamic_index_in_dim(values, rep, axis, keepdims=False)
    up_block = cut_units(up_weight, shard_size, rep_size).astype(jnp.bfloat16)
    down_block = mine(down_weight.reshape(rep_size, units, features), 0).astype(jnp.bfloat16)
    attn_split = Split(*attn_block.shape, grid.y_size, 1.0)
    blocks = [attn_split.pad(attn_block), vectors.astype(jnp.bfloat16), up_block, down_block]
    attn_wide, vector_wide, up_full, down_full = gather_params(grid, attn_split, blocks)
    attn_full = attn_wide[:, :, :rows].reshape(-1, width)
    vector_full = vector_wide.transpose(2, 0, 1, 3).reshape(vectors.shape[0], -1)
    bias = mine(
        vector_full[8:].astype(jnp.float32).reshape(shard_size, rep_size, units), 1
    ).reshape(1, own_cols)

    residual, dense_input, stored = attention_forward(
        hidden_in[None], segment_ids, attn_full, vector_full
    )
    dense_out, dense_input_grad, unit_sums, up_terms, down_terms = dense_step(
        grid, rep_size, dense_input, cotangent, up_full, down_full, bias
    )
    block_out = (residual + dense_out + vector_full[7].astype(jnp.float32)).astype(jnp.bfloat16)
    input_grad, small_rows, attn_input, joined_round, attended, resid_round = attention_backward(
        cotangent[None], segment_ids, stored, attn_full, vector_full, dense_input_grad
    )
    unit_rows = lax.dynamic_update_index_in_dim(
        jnp.zeros((shard_size, rep_size, units), jnp.float32),
        unit_sums.reshape(shard_size, units),
        rep,
        1,
    ).reshape(-1, features)
    vector_terms = jnp.concatenate([small_rows, unit_rows], axis=0)
    attn_term = attn_terms(shard_size, attn_input, joined_round, attended, resid_round)
    grads = [attn_split.pad(attn_term.reshape(grid.z_size, grid.x_size, rows, width))]
    attn_owned, vector_total, up_slices, down_slices = reduce_grads(
        grid, [attn_split], grads, vector_terms, up_terms, down_terms
    )
    own_width = vectors.shape[1]
    vector_own = lax.dynamic_slice_in_dim(
        vector_total, lax.axis_index("shard") * own_width, own_width, 1
    )
    (
        new_vectors,
        vector_next,
        attn_grad,
        new_attn,
        attn_next,
        up_grad,
        new_up,
        up_next,
        down_grad,
        new_down,
        down_next,
    ) = adam_all(
        rep_size,
        shard_size,
        (attn_weight, attn_moments, attn_owned),
        (up_weight, up_moments, up_slices),
        (down_weight, down_moments, down_slices),
        (vectors, vector_moments, vector_own),
    )
    return (
        block_out,
        input_grad[0],
        attn_grad,
        up_grad,
        down_grad,
        vector_own,
        new_attn,
        attn_next,
        new_up,
        up_next,
        new_down,
        down_next,
        new_vectors,
        vector_next,
    )


def solution(mesh):
    in_specs = (
        P(("rep", "shard"), None),
        P(("rep", "shard"), None),
        P(("rep", "shard"), None),
        P("shard", None),
        P(None, "shard", None),
        P("shard", None),
        P(None, "shard", None),
        P("shard", None),
        P(None, "shard", None),
        P(None, "shard"),
        P(None, None, "shard"),
    )
    out_specs = (
        P(("rep", "shard"), None),
        P(("rep", "shard"), None),
        P("shard", None),
        P("shard", None),
        P("shard", None),
        P(None, "shard"),
        P("shard", None),
        P(None, "shard", None),
        P("shard", None),
        P(None, "shard", None),
        P("shard", None),
        P(None, "shard", None),
        P(None, "shard"),
        P(None, None, "shard"),
    )
    body = functools.partial(shards, mesh.shape["rep"], mesh.shape["shard"])
    return jax.shard_map(body, mesh=mesh, in_specs=in_specs, out_specs=out_specs, check_vma=False)
```

```python
import functools

import jax
import jax.numpy as jnp
import numpy as np
from jax import lax
from jax.experimental import pallas as pl
from jax.experimental.pallas import tpu as pltpu
from jax.sharding import PartitionSpec as P

HEAD_DIM = 64
ADAM_STEP = 3
MESH = pl.DeviceIdType.MESH


beta_one = 0.9
beta_two = 0.999
adam_eps = 1e-08
learn_rate = 0.25
weight_decay = 0.1


def matmul(left_arg, right_arg):
    return jnp.dot(left_arg, right_arg, preferred_element_type=jnp.float32)


def inner_rows(left_arg, right_arg):
    return lax.dot_general(
        left_arg, right_arg, (((0,), (0,)), ((), ())), preferred_element_type=jnp.float32
    )


def product(pattern, left_arg, right_arg):
    return jnp.einsum(pattern, left_arg, right_arg, preferred_element_type=jnp.float32)


def normalize(values):
    average = jnp.mean(values, axis=-1, keepdims=True)
    centred = values - average
    inv_std = lax.rsqrt(jnp.mean(centred * centred, axis=-1, keepdims=True) + 1e-05)
    return (centred * inv_std, inv_std)


def normalize_back(grad_in, normed, inv_std, gain_row):
    scaled = grad_in * gain_row
    return inv_std * (
        scaled
        - jnp.mean(scaled, axis=-1, keepdims=True)
        - normed * jnp.mean(scaled * normed, axis=-1, keepdims=True)
    )


def allowed(segments):
    row_count = segments.shape[-1]
    causal = lax.broadcasted_iota(jnp.int32, (row_count, row_count), 0) >= lax.broadcasted_iota(
        jnp.int32, (row_count, row_count), 1
    )
    same_doc = segments[:, :, None] == segments[:, None, :]
    return jnp.logical_and(same_doc, causal)[:, None, :, :]


def scores_of(queries, keys_all, segments):
    logits = product("bqhe,bkhe->bhqk", queries, keys_all) * HEAD_DIM ** (-0.5)
    return jnp.where(allowed(segments), logits, -1e30)


def attention_forward(activations, segments, attn_full, vector_full):
    batch_size, row_count, features = activations.shape
    head_count = features // HEAD_DIM
    head_shape = (batch_size, row_count, head_count, HEAD_DIM)
    vector_rows = vector_full.astype(jnp.float32)
    inputs_flat = activations.astype(jnp.float32).reshape(batch_size * row_count, features)
    normed_one, inv_one = normalize(inputs_flat)
    attn_input = (normed_one * vector_rows[0] + vector_rows[1]).astype(jnp.bfloat16)
    projected = matmul(attn_input, attn_full[:, : 3 * features])
    queries = (projected[:, :features] + vector_rows[2]).astype(jnp.bfloat16).reshape(head_shape)
    keys_all = projected[:, features : 2 * features].astype(jnp.bfloat16).reshape(head_shape)
    values_all = (
        (projected[:, 2 * features :] + vector_rows[3]).astype(jnp.bfloat16).reshape(head_shape)
    )
    logits = scores_of(queries, keys_all, segments)
    row_max = jnp.max(logits, axis=-1, keepdims=True)
    exponent = jnp.exp(logits - row_max)
    totals = jnp.sum(exponent, axis=-1, keepdims=True)
    log_total = row_max + jnp.log(totals)
    soft_probs = (exponent / totals).astype(jnp.bfloat16)
    attended = (
        product("bhqk,bkhe->bqhe", soft_probs, values_all)
        .reshape(batch_size * row_count, features)
        .astype(jnp.bfloat16)
    )
    residual = inputs_flat + matmul(attended, attn_full[:, 3 * features :]) + vector_rows[4]
    normed_two, inv_two = normalize(residual)
    dense_input = (normed_two * vector_rows[5] + vector_rows[6]).astype(jnp.bfloat16)
    stored = (
        normed_one,
        inv_one,
        attn_input,
        queries,
        keys_all,
        values_all,
        log_total,
        attended,
        normed_two,
        inv_two,
    )
    return (residual, dense_input, stored)


def attention_backward(cotangent, segments, stored, attn_full, vector_full, dense_input_grad):
    (
        normed_one,
        inv_one,
        attn_input,
        queries,
        keys_all,
        values_all,
        log_total,
        attended,
        normed_two,
        inv_two,
    ) = stored
    batch_size, row_count, features = cotangent.shape
    head_count = features // HEAD_DIM
    head_shape = (batch_size, row_count, head_count, HEAD_DIM)
    vector_rows = vector_full.astype(jnp.float32)
    out_float = cotangent.reshape(batch_size * row_count, features).astype(jnp.float32)
    resid_grad = out_float + normalize_back(dense_input_grad, normed_two, inv_two, vector_rows[5])
    resid_round = resid_grad.astype(jnp.bfloat16)
    attended_grad = lax.dot_general(
        resid_round,
        attn_full[:, 3 * features :],
        (((1,), (1,)), ((), ())),
        preferred_element_type=jnp.float32,
    ).astype(jnp.bfloat16)
    heads_grad = attended_grad.reshape(head_shape)
    logits = scores_of(queries, keys_all, segments)
    recomputed = jnp.exp(logits - log_total)
    prob_round = recomputed.astype(jnp.bfloat16)
    prob_grad = product("bqhe,bkhe->bhqk", heads_grad, values_all)
    delta_row = product("bqhe,bqhe->bhq", heads_grad, attended.reshape(head_shape))[..., None]
    logit_grad = (recomputed * (prob_grad - delta_row)).astype(jnp.bfloat16)
    scale_factor = HEAD_DIM ** (-0.5)
    query_grad = product("bhqk,bkhe->bqhe", logit_grad, keys_all) * scale_factor
    key_grad = product("bhqk,bqhe->bkhe", logit_grad, queries) * scale_factor
    value_grad = product("bhqk,bqhe->bkhe", prob_round, heads_grad)
    joined_grad = jnp.concatenate(
        [
            query_grad.reshape(-1, features),
            key_grad.reshape(-1, features),
            value_grad.reshape(-1, features),
        ],
        axis=1,
    )
    joined_round = joined_grad.astype(jnp.bfloat16)
    attn_input_grad = lax.dot_general(
        joined_round,
        attn_full[:, : 3 * features],
        (((1,), (1,)), ((), ())),
        preferred_element_type=jnp.float32,
    )
    input_grad = (
        (resid_grad + normalize_back(attn_input_grad, normed_one, inv_one, vector_rows[0]))
        .astype(jnp.bfloat16)
        .reshape(batch_size, row_count, features)
    )
    small_rows = jnp.stack(
        [
            jnp.sum(attn_input_grad * normed_one, axis=0),
            jnp.sum(attn_input_grad, axis=0),
            jnp.sum(joined_grad[:, :features], axis=0),
            jnp.sum(joined_grad[:, 2 * features :], axis=0),
            jnp.sum(resid_grad, axis=0),
            jnp.sum(dense_input_grad * normed_two, axis=0),
            jnp.sum(dense_input_grad, axis=0),
            jnp.sum(out_float, axis=0),
        ]
    )
    return (input_grad, small_rows, attn_input, joined_round, attended, resid_round)


CORES = 2
ROW_UNIT = 16
LANE_UNIT = 128
GATHER_VMEM = 16 * 2**20
REDUCE_VMEM = 36 * 2**20
TERMS_VMEM = 20 * 2**20
DENSE_VMEM = 46 * 2**20
ADAM_VMEM = 56 * 2**20


class Grid:
    def __init__(self, rep_size, shard_size):
        self.cores = CORES
        self.y_size = rep_size // CORES
        self.x_size = self.y_size if shard_size % self.y_size == 0 else 1
        self.z_size = shard_size // self.x_size

    def locate(self):
        rep = lax.axis_index("rep")
        shard = lax.axis_index("shard")
        self.y, self.c = lax.div(rep, CORES), lax.rem(rep, CORES)
        self.z, self.x = lax.div(shard, self.x_size), lax.rem(shard, self.x_size)
        return self

    def device(self, dz=0, dx=0, dy=0, dc=0):
        rep = lax.rem(self.y + dy, self.y_size) * CORES + lax.rem(self.c + dc, CORES)
        shard = lax.rem(self.z + dz, self.z_size) * self.x_size + lax.rem(self.x + dx, self.x_size)
        return (rep, shard)

    def partners(self):
        found = [self.device(dz=k) for k in range(1, self.z_size)]
        found += [self.device(dx=k) for k in range(1, self.x_size)]
        found += [self.device(dy=k) for k in range(1, self.y_size)]
        return found + [self.device(dc=1)]

    def greet(self):
        barrier = pltpu.get_barrier_semaphore()
        partners = self.partners()
        for partner in partners:
            pl.semaphore_signal(barrier, inc=1, device_id=partner, device_id_type=MESH)
        pl.semaphore_wait(barrier, len(partners))


class Split:
    def __init__(self, rows, columns, y_size, share=0.7, array=0, chunk=0, chunks=1):
        self.rows, self.columns, self.array = rows, columns, array
        self.by_lane = columns % (2 * LANE_UNIT) == 0
        unit = LANE_UNIT if self.by_lane else ROW_UNIT
        extent = columns if self.by_lane else rows
        padded = -(-extent // (2 * unit)) * 2 * unit
        if not self.by_lane:
            self.rows = padded
        pairs = padded // (2 * unit)
        chunks = max(1, min(chunks, pairs // (y_size + 1)))
        self.chunks = chunks
        least = (max(1, pairs // chunks) - 1) // y_size * y_size + 1
        starts = [0] + [pairs - least * (chunks - n) for n in range(1, chunks + 1)]
        units = starts[chunk + 1] - starts[chunk]
        self.unit = unit
        self.start = 2 * unit * starts[chunk]
        self.half = units * unit
        taken = min(max(1, int(units * share / y_size + 0.5)), (units - 1) // y_size)
        self.a_size = taken * unit
        self.b_start = y_size * self.a_size
        self.b_size = self.half - self.b_start

    def chunked(self, y_size, share, array, chunks):
        found = Split(self.rows, self.columns, y_size, share, array, 0, chunks)
        return [found] + [
            Split(self.rows, self.columns, y_size, share, array, n, chunks)
            for n in range(1, found.chunks)
        ]

    def block(self):
        return (self.rows, self.columns)

    def shape(self, size):
        return (self.rows, size) if self.by_lane else (size, self.columns)

    def cut(self, start, size):
        window = pl.ds(pl.multiple_of(self.start + start, self.unit), size)
        return (slice(None), window) if self.by_lane else (window, slice(None))

    def piece_a(self, y, c):
        return self.cut(c * self.half + y * self.a_size, self.a_size)

    def piece_b(self, c):
        return self.cut(c * self.half + self.b_start, self.b_size)

    def piece_half(self, c):
        return self.cut(c * self.half, self.half)

    def pad(self, values):
        extra = self.rows - values.shape[-2]
        if extra == 0:
            return values
        return jnp.pad(values, [(0, 0)] * (values.ndim - 2) + [(0, extra), (0, 0)])


def remote(source, target, send, recv, device):
    return pltpu.make_async_remote_copy(
        src_ref=source,
        dst_ref=target,
        send_sem=send,
        recv_sem=recv,
        device_id=device,
        device_id_type=MESH,
    )


class Semaphores:
    def __init__(self, array):
        self.array, self.used = array, 0

    def take(self):
        self.used += 1
        return self.array.at[self.used - 1]


def chosen(condition):
    return (lambda body: body()) if condition is True else pl.when(condition)


class Links:
    def __init__(self, send_array, recv_array):
        self.sends, self.recvs = send_array, recv_array
        self.copies = {}

    def launch(self, key, source, target, device, sent=True, got=True):
        n = len(self.copies)
        copy = remote(source, target, self.sends.at[n], self.recvs.at[n], device)
        self.copies[key] = (copy, sent, got)
        chosen(sent)(copy.start)

    def arrived(self, *keys):
        for key in keys:
            copy, _, got = self.copies[key]
            chosen(got)(copy.wait_recv)

    def wait(self, key):
        self.copies[key][0].wait_recv()

    def finish(self):
        for copy, sent, _ in self.copies.values():
            chosen(sent)(copy.wait_send)


GATHER_PLAN = {
    "zv": 0,
    "ub": 1,
    "ux": 2,
    "za": 3,
    "dx": 4,
    "xv": (5, 6, 7, 8),
    "xa": (9, 11, 14, 18),
    "u": (10, 13, 17),
    "ya": (12, 15, 19, 21),
    "db": 16,
    "d": (20, 23, 25),
    "c": (22, 24, 26, 27),
}
REDUCE_PLAN = {
    "c": (0, 2, 4),
    "dx": (1, 3, 10, 11),
    "v": (5, 8, 16, 25, 28),
    "y": (6, 7, 9),
    "d": (12, 13, 17, 20),
    "x": (14, 19, 24),
    "ux": (15, 18, 27, 29),
    "z": (21, 30, 34),
    "de": 22,
    "u": (23, 26, 32, 36),
    "f": (31, 35, 40),
    "dp": 33,
    "s": (37, 39, 42),
    "ue": 38,
    "up": 41,
}


def arrange(plan, counts):
    timed = []
    for name, places in plan.items():
        if isinstance(places, int):
            timed.append((places, name, ()))
            continue
        marks = np.linspace(0.0, 1.0, counts[name])
        spots = np.interp(marks, np.linspace(0.0, 1.0, len(places)), places)
        timed += [(float(spot), name, (n,)) for n, spot in enumerate(spots)]
    return [(name, index) for _, name, index in sorted(timed)]


def gather_kernel(grid, split, *refs):
    attn_own, vec_own, up_own, down_own = refs[:4]
    attn_full, vec_full, up_full, down_full = refs[4:8]
    links, local_array = Links(refs[8], refs[9]), refs[10]
    g = grid.locate()
    z_size, x_size, y_size = g.z_size, g.x_size, g.y_size
    hops = range(z_size - 1)
    near = lambda j: lax.rem(g.z + j + z_size, z_size)
    place = lambda j, i: (lax.rem(g.z + z_size - j, z_size), lax.rem(g.x + x_size - i, x_size))
    own = {"a": attn_own, "v": vec_own, "u": up_own, "d": down_own}
    full = {"a": attn_full, "v": vec_full, "u": up_full, "d": down_full}

    def windows(t):
        if t == "v":
            return [(slice(None), slice(None))]
        return [split.piece_a(g.y, g.c), split.piece_b(g.c)]

    def stage_z(t):
        for k in range(1, z_size):
            for p, window in enumerate(windows(t)):
                links.launch(
                    ("z", t, p, k),
                    own[t].at[window],
                    full[t].at[(g.z, g.x) + window],
                    g.device(dz=k),
                )

    def unit_x(t, j):
        for p, window in enumerate(windows(t)):
            here = place(j, 0) + window
            if j > 0:
                links.arrived(("z", t, p, j))
            source = own[t].at[window] if j == 0 else full[t].at[here]
            for i in range(1, x_size):
                links.launch(("x", t, p, j, i), source, full[t].at[here], g.device(dx=i))
            if t == "a" and p == 0 and j > 0:
                for k in range(1, y_size):
                    links.launch(("y", t, j, 0, k), source, full[t].at[here], g.device(dy=k))

    def unit_y(t, j):
        for i in range(1, x_size):
            for p, window in enumerate(windows(t)):
                links.arrived(("x", t, p, j, i))
                if t == "a" and p == 0:
                    here = full[t].at[place(j, i) + window]
                    for k in range(1, y_size):
                        links.launch(("y", t, j, i, k), here, here, g.device(dy=k))

    def unit_core(j):
        for i in range(x_size):
            if (j, i) == (0, 0):
                continue
            for k in range(1, y_size):
                links.arrived(("y", "a", j, i, k))
            here = attn_full.at[place(j, i) + split.piece_half(g.c)]
            links.launch(("c", j, i), here, here, g.device(dc=1))

    def hop(t, k):
        source = own[t] if k == 0 else full[t].at[near(-k), g.x]
        links.launch(
            ("right" + t, k),
            source,
            full[t].at[near(-k), g.x],
            g.device(dz=1),
            jnp.logical_and(g.z >= k, g.z + 1 < z_size),
            g.z >= k + 1,
        )
        source = own[t] if k == 0 else full[t].at[near(k), g.x]
        links.launch(
            ("left" + t, k),
            source,
            full[t].at[near(k), g.x],
            g.device(dz=z_size - 1),
            jnp.logical_and(g.z + k < z_size, g.z >= 1),
            g.z + 1 + k < z_size,
        )

    def across(name, t, source, where, held):
        for i in range(1, x_size):
            target = full[t].at[where, g.x]
            links.launch((name + t, i), source, target, g.device(dx=i), held, held)

    def begin(t):
        hop(t, 0)

    def direct(t):
        across("own", t, own[t], g.z, True)

    def advance(t, k):
        links.arrived(("right" + t, k), ("left" + t, k))
        if k + 1 < z_size - 1:
            hop(t, k + 1)
        across("r%d" % k, t, full[t].at[near(-k - 1), g.x], near(-k - 1), g.z >= k + 1)
        across("l%d" % k, t, full[t].at[near(k + 1), g.x], near(k + 1), g.z + 1 + k < z_size)

    def whole(t):
        for i in range(1, x_size):
            links.arrived(("own" + t, i))
            for k in hops:
                links.arrived(("r%d" % k + t, i), ("l%d" % k + t, i))

    g.greet()
    kept = []
    for n, t in enumerate(own):
        copy = pltpu.make_async_copy(own[t], full[t].at[g.z, g.x], local_array.at[n])
        copy.start()
        kept.append(copy)
    table = {"zv": (stage_z, "v"), "za": (stage_z, "a"), "c": (unit_core,)}
    table.update({"x" + t: (unit_x, t) for t in "va"})
    table["ya"] = (unit_y, "a")
    for t in "ud":
        table.update({t: (advance, t), t + "b": (begin, t), t + "x": (direct, t)})
    counts = {name: z_size - 1 if name in "ud" else z_size for name in table}
    for name, index in arrange(GATHER_PLAN, counts):
        table[name][0](*table[name][1:], *index)
    for j in range(z_size):
        unit_y("v", j)
    whole("u")
    whole("d")
    for j in range(z_size):
        for i in range(x_size):
            if (j, i) != (0, 0):
                links.arrived(("c", j, i))
    links.finish()
    for copy in kept:
        copy.wait()


def gather_params(grid, split, blocks):
    z, x, y = grid.z_size, grid.x_size, grid.y_size
    total = 2 * (z - 1) + 2 * z * (x - 1) + (z * x - 1) * y
    total += (z - 1) + z * (x - 1) + 2 * (2 * (z - 1) + (x - 1) * (2 * z - 1))
    any_spec = pl.BlockSpec(memory_space=pl.ANY)
    return pl.pallas_call(
        functools.partial(gather_kernel, grid, split),
        out_shape=[jax.ShapeDtypeStruct((z, x) + block.shape, jnp.bfloat16) for block in blocks],
        in_specs=[pl.BlockSpec(memory_space=pltpu.VMEM)] * 4,
        out_specs=[any_spec] * 4,
        scratch_shapes=[
            pltpu.SemaphoreType.DMA((total,)),
            pltpu.SemaphoreType.DMA((total,)),
            pltpu.SemaphoreType.DMA((4,)),
        ],
        compiler_params=pltpu.CompilerParams(
            collective_id=0, has_side_effects=True, vmem_limit_bytes=GATHER_VMEM
        ),
        name="gather_params",
    )(*blocks)


def plus(left_arg, right_arg):
    return left_arg.astype(jnp.float32) + right_arg.astype(jnp.float32)


def reduce_kernel(grid, splits, *refs):
    count = len(splits)
    arrays = splits[-1].array + 1
    vector_in, up_terms, down_terms = refs[arrays : arrays + 3]
    grads = [refs[split.array] for split in splits]
    outs = [refs[arrays + 3 + split.array] for split in splits]
    vector_out, up_out, down_out = refs[2 * arrays + 3 : 2 * arrays + 6]
    scratch, slim = refs[2 * arrays + 6 : -11], refs[-11:]
    per = 12
    buffers = [scratch[per * t : per * (t + 1)] for t in range(count)]
    v_core, v_y, v_x, v_z, v_one, v_two, v_three, send_array, recv_array, local_array = scratch[
        per * count :
    ]
    sends, recvs, locals_ = (
        Semaphores(send_array),
        Semaphores(recv_array),
        Semaphores(local_array),
    )
    g = grid.locate()
    z_size, x_size, y_size = g.z_size, g.x_size, g.y_size
    copies, moves = {}, {}

    def launch(key, source, target, device):
        copy = remote(source, target, sends.take(), recvs.take(), device)
        copy.start()
        copies[key] = copy

    def move(key, source, target):
        copy = pltpu.make_async_copy(source, target, locals_.take())
        copy.start()
        moves[key] = copy

    def each_block(body):
        @pl.loop(0, z_size * x_size)
        def _(index):
            body(lax.div(index, x_size), lax.rem(index, x_size))

    everything = (slice(None), slice(None))
    other_y = lambda k: lax.rem(g.y + k, y_size)
    other_x = lambda k: lax.rem(g.x + k, x_size)
    other_z = lambda k: lax.rem(g.z + k, z_size)

    def stage_core(t):
        acc_a, acc_b, got_a, got_b = buffers[t][:4]
        split = splits[t]
        for q in range(y_size):
            launch(
                ("ca", t, q),
                grads[t].at[everything + split.piece_a(q, 1 - g.c)],
                got_a.at[q],
                g.device(dc=1),
            )
            move(("la", t, q), grads[t].at[everything + split.piece_a(q, g.c)], acc_a.at[q])
        launch(
            ("cb", t),
            grads[t].at[everything + split.piece_b(1 - g.c)],
            got_b,
            g.device(dc=1),
        )
        move(("lb", t), grads[t].at[everything + split.piece_b(g.c)], acc_b)

    def stage_y(t):
        acc_a, acc_b, got_a, got_b, got_y = buffers[t][:5]
        for q in range(y_size):
            copies["ca", t, q].wait_recv()
            moves["la", t, q].wait()

            def add_a(i, j, q=q):
                acc_a[q, i, j] = plus(acc_a[q, i, j], got_a[q, i, j]).astype(jnp.bfloat16)

            each_block(add_a)
        for k in range(1, y_size):
            launch(("ya", t, k), acc_a.at[other_y(k)], got_y.at[k - 1], g.device(dy=k))
        copies["cb", t].wait_recv()
        moves["lb", t].wait()

        def add_b(i, j):
            acc_b[i, j] = plus(acc_b[i, j], got_b[i, j]).astype(jnp.bfloat16)

        each_block(add_b)
        for k in range(1, x_size):
            launch(
                ("xb", t, k), acc_b.at[:, other_x(k)], buffers[t][6].at[k - 1], g.device(dx=k)
            )

    def stage_x(t):
        acc_a, got_y, got_xa = buffers[t][0], buffers[t][4], buffers[t][5]
        for k in range(1, y_size):
            copies["ya", t, k].wait_recv()

        def add(i, j):
            value = acc_a[g.y, i, j].astype(jnp.float32)
            for k in range(1, y_size):
                value = plus(value, got_y[k - 1, i, j])
            acc_a[g.y, i, j] = value.astype(jnp.bfloat16)

        each_block(add)
        for k in range(1, x_size):
            launch(
                ("xa", t, k), acc_a.at[g.y, :, other_x(k)], got_xa.at[k - 1], g.device(dx=k)
            )

    def stage_z(t):
        acc_a, acc_b = buffers[t][:2]
        got_xa, got_xb, got_za, got_zb = buffers[t][5:9]
        for k in range(1, x_size):
            copies["xb", t, k].wait_recv()
            copies["xa", t, k].wait_recv()

        @pl.loop(0, z_size)
        def _(i):
            value_a = acc_a[g.y, i, g.x].astype(jnp.float32)
            for k in range(1, x_size):
                value_a = plus(value_a, got_xa[k - 1, i])
            acc_a[g.y, i, g.x] = value_a.astype(jnp.bfloat16)
            value_b = acc_b[i, g.x].astype(jnp.float32)
            for k in range(1, x_size):
                value_b = plus(value_b, got_xb[k - 1, i])
            acc_b[i, g.x] = value_b.astype(jnp.bfloat16)

        for k in range(1, z_size):
            launch(
                ("zb", t, k), acc_b.at[other_z(k), g.x], got_zb.at[k - 1], g.device(dz=k)
            )
            launch(
                ("za", t, k),
                acc_a.at[g.y, other_z(k), g.x],
                got_za.at[k - 1],
                g.device(dz=k),
            )

    def stage_final(t):
        acc_a, acc_b = buffers[t][:2]
        got_za, got_zb, final_a, ring_b, final_b = buffers[t][7:12]
        split = splits[t]
        for k in range(1, z_size):
            copies["zb", t, k].wait_recv()
        value = acc_b[g.z, g.x].astype(jnp.float32)
        for k in range(1, z_size):
            value = plus(value, got_zb[k - 1])
        ring_b[0] = value.astype(jnp.bfloat16)
        for k in range(1, y_size):
            launch(("yb", t, k), ring_b.at[0], ring_b.at[k], g.device(dy=k))
        for k in range(1, z_size):
            copies["za", t, k].wait_recv()
        value = acc_a[g.y, g.z, g.x].astype(jnp.float32)
        for k in range(1, z_size):
            value = plus(value, got_za[k - 1])
        final_a[...] = value.astype(jnp.bfloat16)
        target = outs[t].at[split.piece_a(g.y, g.c)]
        for k in range(1, y_size):
            launch(("oa", t, k), final_a, target, g.device(dy=k))
        move(("fa", t), final_a, target)

    def stage_share(t):
        ring_b, final_b = buffers[t][10:12]
        split = splits[t]
        for k in range(1, y_size):
            copies["yb", t, k].wait_recv()
        value = ring_b[g.y].astype(jnp.float32)
        for k in range(1, y_size):
            value = plus(value, ring_b[lax.rem(g.y + y_size - k, y_size)])
        final_b[...] = value.astype(jnp.bfloat16)
        move(("fb", t), final_b, outs[t].at[split.piece_b(g.c)])
        for k in range(1, y_size):
            copies["oa", t, k].wait_recv()
        moves["fa", t].wait()
        moves["fb", t].wait()
        half = outs[t].at[split.piece_half(g.c)]
        launch(("h", t), half, half, g.device(dc=1))

    def sum_ring(buffer, place, size):
        value = buffer[place]
        for k in range(1, size):
            value = value + buffer[lax.rem(place + size - k, size)]
        return value

    def vector_step(name, source, got, size, **direction):
        (axis,) = direction
        got[0] = source[...]
        for k in range(1, size):
            launch((name, k), source, got.at[k], g.device(**{axis: k}))

    def vector_sum(name, got, place, size, target):
        for k in range(1, size):
            copies[name, k].wait_recv()
        target[...] = sum_ring(got, place, size)

    up_x, down_x, up_z, down_z, up_sum, down_sum, up_own, down_own = slim[:8]
    links = Links(slim[8], slim[9])
    rep = lax.axis_index("rep")
    terms = {"u": up_terms, "d": down_terms}
    sums = {"u": up_sum, "d": down_sum}
    got_x, got_z = {"u": up_x, "d": down_x}, {"u": up_z, "d": down_z}
    owned, shared = {"u": up_own, "d": down_own}, {"u": up_out, "d": down_out}

    def ranked(n):
        last = z_size - 1
        later = lax.div(lax.div(n + g.z, last) + 1, 2)
        return later * (n - last + g.z) + (1 - later) * (last - n)

    def slim_x(t, *some):
        for n in some or range(z_size):
            for k in range(1, x_size):
                links.launch(
                    ("rx" + t, k, n),
                    terms[t].at[ranked(n), other_x(k)],
                    got_x[t].at[k - 1, ranked(n)],
                    g.device(dx=k),
                )

    def fold(t, n):
        for k in range(1, x_size):
            links.arrived(("rx" + t, k, n))
        here = ranked(n)
        value = terms[t][here, g.x].astype(jnp.float32)
        for k in range(1, x_size):
            value = plus(value, got_x[t][k - 1, here])
        sums[t][here] = value.astype(jnp.bfloat16)

    def toward(t, key, step, goal, sent, got, slot, first, device):
        if step > 0:

            @pl.when(jnp.logical_and(sent, jnp.logical_not(first)))
            def _():
                links.wait((key + t, step - 1))
                sums[t][goal] = plus(sums[t][goal], got_z[t][slot]).astype(jnp.bfloat16)

        target = got_z[t].at[slot]
        links.launch((key + t, step), sums[t].at[goal], target, device, sent, got)

    def slim_z(t, step):
        fold(t, step)
        if step == z_size - 1:
            return
        goal = lax.rem(2 * z_size - 1 - step + g.z, z_size)
        got = jnp.logical_and(g.z >= 1, g.z <= step + 1)
        toward(t, "pr", step, goal, g.z <= step, got, goal + 1, g.z == 0, g.device(dz=1))
        back = z_size - 1 - g.z
        goal = lax.rem(step + 1 + g.z, z_size)
        got = jnp.logical_and(back >= 1, back <= step + 1)
        device = g.device(dz=z_size - 1)
        toward(t, "pl", step, goal, back <= step, got, goal, back == 0, device)

    def slim_end(t):
        for key, some, slot in (("pr", g.z >= 1, g.z + 1), ("pl", g.z + 1 < z_size, g.z)):

            @pl.when(some)
            def _(key=key, slot=slot):
                links.wait((key + t, z_size - 2))
                sums[t][g.z] = plus(sums[t][g.z], got_z[t][slot]).astype(jnp.bfloat16)

        owned[t][...] = sums[t][g.z]
        for k in range(1, y_size):
            links.launch(("oy" + t, k), owned[t], shared[t].at[rep], g.device(dy=k))
        links.launch(("oc" + t, 0), owned[t], shared[t].at[rep], g.device(dc=1))
        n = 0 if t == "d" else 1
        copy = pltpu.make_async_copy(owned[t], shared[t].at[rep], slim[10].at[n])
        copy.start()
        moves["own" + t] = copy

    def slim_pass(t):
        for k in range(1, y_size):
            links.arrived(("oy" + t, k))
            here = shared[t].at[lax.rem(g.y + y_size - k, y_size) * CORES + g.c]
            links.launch(("oc" + t, k), here, here, g.device(dc=1))

    def small(n):
        if n == 0:
            vector_step("vc", vector_in, v_core, CORES, dc=1)
        if n == 1:
            vector_sum("vc", v_core, g.c, CORES, v_one)
            vector_step("vy", v_one, v_y, y_size, dy=1)
        if n == 2:
            vector_sum("vy", v_y, g.y, y_size, v_two)
            vector_step("vx", v_two, v_x, x_size, dx=1)
        if n == 3:
            vector_sum("vx", v_x, g.x, x_size, v_three)
            vector_step("vz", v_three, v_z, z_size, dz=1)
        if n == 4:
            vector_sum("vz", v_z, g.z, z_size, vector_out)

    g.greet()
    table = {"c": stage_core, "y": stage_y, "x": stage_x, "z": stage_z, "f": stage_final}
    table.update({"s": stage_share, "v": small})
    for t in ("d", "u"):
        table[t] = functools.partial(slim_z, t)
        table[t + "x"] = functools.partial(slim_x, t)
        table[t + "e"] = functools.partial(slim_end, t)
        table[t + "p"] = functools.partial(slim_pass, t)
    counts = {name: count if name in "cyxzfs" else z_size for name in table}
    counts["v"] = 5
    for name, index in arrange(REDUCE_PLAN, counts):
        table[name](*index)
    for key, copy in copies.items():
        if key[0] == "h":
            copy.wait_recv()
        copy.wait_send()
    for t in ("d", "u"):
        for k in range(y_size):
            links.arrived(("oc" + t, k))
        moves["own" + t].wait()
    links.finish()


def reduce_grads(grid, whole, grads, vector_terms, up_terms, down_terms):
    z, x, y = grid.z_size, grid.x_size, grid.y_size
    splits = []
    for array, split in enumerate(whole):
        splits += split.chunked(y, 0.85, array, 3)
    scratch = []
    for split in splits:
        a, b = split.shape(split.a_size), split.shape(split.b_size)
        scratch += [
            pltpu.VMEM(shape, jnp.bfloat16)
            for shape in (
                (y, z, x) + a,
                (z, x) + b,
                (y, z, x) + a,
                (z, x) + b,
                (y - 1, z, x) + a,
                (x - 1, z) + a,
                (x - 1, z) + b,
                (z - 1,) + a,
                (z - 1,) + b,
                a,
                (y,) + b,
                b,
            )
        ]
    small = vector_terms.shape
    scratch += [pltpu.VMEM((size,) + small, jnp.float32) for size in (CORES, y, x, z)]
    scratch += [pltpu.VMEM(small, jnp.float32)] * 3
    per_tensor = (y + 1) + (y - 1) + 2 * (x - 1) + 2 * (z - 1) + 2 * (y - 1) + 1
    total = len(splits) * per_tensor + 1 + (y - 1) + (x - 1) + (z - 1)
    scratch += [
        pltpu.SemaphoreType.DMA((total,)),
        pltpu.SemaphoreType.DMA((total,)),
        pltpu.SemaphoreType.DMA((len(splits) * (y + 3),)),
    ]
    slim = [up_terms.shape[2:], down_terms.shape[2:]]
    for lead in ((x - 1, z), (z + 1,), (z,), ()):
        scratch += [pltpu.VMEM(lead + block, jnp.bfloat16) for block in slim]
    extra = 2 * (z * (x - 1) + 2 * (z - 1) + 2 * y - 1)
    scratch += [pltpu.SemaphoreType.DMA((size,)) for size in (extra, extra, 2)]
    rep_size = y * CORES
    return pl.pallas_call(
        functools.partial(reduce_kernel, grid, splits),
        out_shape=[jax.ShapeDtypeStruct(split.block(), jnp.bfloat16) for split in whole]
        + [jax.ShapeDtypeStruct(small, jnp.float32)]
        + [jax.ShapeDtypeStruct((rep_size,) + block, jnp.bfloat16) for block in slim],
        in_specs=[pl.BlockSpec(memory_space=pl.ANY)] * len(whole)
        + [pl.BlockSpec(memory_space=pltpu.VMEM)] * 3,
        out_specs=[pl.BlockSpec(memory_space=pl.ANY)] * len(whole)
        + [pl.BlockSpec(memory_space=pltpu.VMEM)]
        + [pl.BlockSpec(memory_space=pl.ANY)] * 2,
        scratch_shapes=scratch,
        compiler_params=pltpu.CompilerParams(
            collective_id=1, has_side_effects=True, vmem_limit_bytes=REDUCE_VMEM
        ),
        name="reduce_grads",
    )(*grads, vector_terms, up_terms, down_terms)


def outer_rows(left_arg, right_arg):
    return lax.dot_general(
        left_arg, right_arg, (((1,), (1,)), ((), ())), preferred_element_type=jnp.float32
    )


def dense_kernel(grid, rep_size, *refs):
    dense_ref, cot_ref, up_full, down_full, bias_ref = refs[:5]
    out_ref, back_ref, sums_ref, up_grad, down_grad = refs[5:10]
    (
        dense_all,
        cot_all,
        inputs_cut,
        hidden_cut,
        slope,
        hidden_grad,
        hidden_round,
        wide_grad,
        out_part,
        back_part,
        out_core,
        back_core,
        out_y,
        back_y,
        send_array,
        recv_array,
    ) = refs[10:]
    links = Links(send_array, recv_array)
    g = grid.locate()
    z_size, x_size, y_size = g.z_size, g.x_size, g.y_size
    shard_size = z_size * x_size
    rep = lax.axis_index("rep")
    tokens, features = dense_ref.shape
    rows, width = up_full.shape[2:]
    units = down_full.shape[2]
    total = rep_size * tokens
    split = lambda n: (n // x_size, n % x_size)
    rep_at = lambda dy, dc: lax.rem(g.y + dy, y_size) * CORES + lax.rem(g.c + dc, CORES)

    barrier = pltpu.get_barrier_semaphore()
    partners = [g.device(dy=k) for k in range(1, y_size)] + [g.device(dc=1)]
    for partner in partners:
        pl.semaphore_signal(barrier, inc=1, device_id=partner, device_id_type=MESH)
    pl.semaphore_wait(barrier, len(partners))

    def spread(name, source, target):
        for k in range(1, y_size):
            links.launch((name, "y", k), source, target.at[rep], g.device(dy=k))
        links.launch((name, "c", 0), source, target.at[rep], g.device(dc=1))

    def pass_on(name, target):
        for k in range(1, y_size):
            links.arrived((name, "y", k))
            here = target.at[rep_at(y_size - k, 0)]
            links.launch((name, "c", k), here, here, g.device(dc=1))

    def spread_end(name):
        for k in range(y_size):
            links.arrived((name, "c", k))

    def term(target, left, right):
        @pl.loop(0, shard_size)
        def _(s):
            one = left[s].reshape(total, left.shape[-1])
            two = right[...].reshape(total, right.shape[-1])
            value = inner_rows(one, two)
            target[lax.div(s, x_size), lax.rem(s, x_size)] = value.astype(jnp.bfloat16)

    def scatter(name, part, got):
        for k in range(y_size):
            links.launch((name, "c", k), part.at[rep_at(k, 1)], got.at[k], g.device(dc=1))

    def scatter_y(name, part, core, got):
        for k in list(range(1, y_size)) + [0]:
            links.arrived((name, "c", k))
            there = rep_at(k, 0)
            part[there] = plus(part[there], core[k]).astype(jnp.bfloat16)
            if k > 0:
                links.launch((name, "y", k), part.at[there], got.at[k - 1], g.device(dy=k))

    def collect(name, part, got, target):
        value = part[rep].astype(jnp.float32)
        for k in range(1, y_size):
            links.arrived((name, "y", k))
            value = plus(value, got[k - 1])
        target[...] = value

    spread("dense", dense_ref, dense_all)
    spread("cot", cot_ref, cot_all)
    dense_all[rep] = dense_ref[...]
    cot_all[rep] = cot_ref[...]

    def hidden_of(b):
        values = dense_all[b].astype(jnp.float32)
        for s in range(shard_size):
            inputs_cut[s, b] = values[:, s * rows : (s + 1) * rows].astype(jnp.bfloat16)
        pre = jnp.broadcast_to(bias_ref[...], (tokens, width))
        for s in range(shard_size):
            pre = pre + matmul(inputs_cut[s, b], up_full[split(s)])
        normal_cdf = 0.5 * (1.0 + lax.erf(pre * 0.7071067811865476))
        density = jnp.exp(-0.5 * pre * pre) * 0.3989422804014327
        slope[b] = normal_cdf + pre * density
        hidden = pre * normal_cdf
        for s in range(shard_size):
            hidden_cut[s, b] = hidden[:, s * units : (s + 1) * units].astype(jnp.bfloat16)
        value = matmul(hidden_cut[0, b], down_full[split(0)])
        for s in range(1, shard_size):
            value = value + matmul(hidden_cut[s, b], down_full[split(s)])
        out_part[b] = value.astype(jnp.bfloat16)

    pass_on("dense", dense_all)
    spread_end("dense")
    pl.loop(0, rep_size)(hidden_of)
    scatter("out", out_part, out_core)
    pass_on("cot", cot_all)
    spread_end("cot")

    for s in range(shard_size):
        value = outer_rows(cot_all[...].reshape(total, features), down_full[split(s)])
        hidden_grad[:, :, s * units : (s + 1) * units] = value.reshape(rep_size, tokens, units)
    sums_ref[...] = jnp.zeros_like(sums_ref)

    @pl.loop(0, rep_size)
    def _(b):
        value = hidden_grad[b] * slope[b]
        sums_ref[...] += jnp.sum(value, axis=0, keepdims=True)
        hidden_round[b] = value.astype(jnp.bfloat16)

    scatter_y("out", out_part, out_core, out_y)
    for s in range(shard_size):
        value = outer_rows(hidden_round[...].reshape(total, width), up_full[split(s)])
        wide_grad[:, :, s * rows : (s + 1) * rows] = value.reshape(rep_size, tokens, rows)

    @pl.loop(0, rep_size)
    def _(b):
        back_part[b] = wide_grad[b].astype(jnp.bfloat16)

    scatter("back", back_part, back_core)
    term(up_grad, inputs_cut, hidden_round)
    scatter_y("back", back_part, back_core, back_y)
    term(down_grad, hidden_cut, cot_all)
    collect("out", out_part, out_y, out_ref)
    collect("back", back_part, back_y, back_ref)
    links.finish()


def dense_step(grid, rep_size, dense_input, cotangent, up_full, down_full, bias):
    z, x, y = grid.z_size, grid.x_size, grid.y_size
    tokens, features = dense_input.shape
    rows, width = up_full.shape[2:]
    units = down_full.shape[2]
    low, high = jnp.bfloat16, jnp.float32
    vmem = lambda dtype, *shape: pltpu.VMEM(shape, dtype)
    shape = lambda dtype, *sizes: jax.ShapeDtypeStruct(sizes, dtype)
    total = 4 * (2 * y - 1)
    return pl.pallas_call(
        functools.partial(dense_kernel, grid, rep_size),
        out_shape=[
            shape(high, tokens, features),
            shape(high, tokens, features),
            shape(high, 1, width),
            shape(low, z, x, rows, width),
            shape(low, z, x, units, features),
        ],
        in_specs=[pl.BlockSpec(memory_space=pltpu.VMEM)] * 5,
        out_specs=[pl.BlockSpec(memory_space=pltpu.VMEM)] * 5,
        scratch_shapes=[
            vmem(low, rep_size, tokens, features),
            vmem(low, rep_size, tokens, features),
            vmem(low, z * x, rep_size, tokens, rows),
            vmem(low, z * x, rep_size, tokens, units),
            vmem(high, rep_size, tokens, width),
            vmem(high, rep_size, tokens, width),
            vmem(low, rep_size, tokens, width),
            vmem(high, rep_size, tokens, features),
            vmem(low, rep_size, tokens, features),
            vmem(low, rep_size, tokens, features),
            vmem(low, y, tokens, features),
            vmem(low, y, tokens, features),
            vmem(low, y - 1, tokens, features),
            vmem(low, y - 1, tokens, features),
            pltpu.SemaphoreType.DMA((total,)),
            pltpu.SemaphoreType.DMA((total,)),
        ],
        compiler_params=pltpu.CompilerParams(
            collective_id=2, has_side_effects=True, vmem_limit_bytes=DENSE_VMEM
        ),
        name="dense_step",
    )(dense_input, cotangent, up_full, down_full, bias)


def attn_term_kernel(attn_ref, joined_ref, attended_ref, resid_ref, out_ref):
    blocks, rows, _ = out_ref.shape
    inner = joined_ref.shape[1]
    for s in range(blocks):
        for left_ref, right_ref, start in (
            (attn_ref, joined_ref, 0),
            (attended_ref, resid_ref, inner),
        ):
            left = left_ref[:, s * rows : (s + 1) * rows]
            value = inner_rows(left, right_ref[...]).astype(jnp.bfloat16)
            out_ref[s, :, start : start + right_ref.shape[1]] = value


def attn_terms(blocks, attn_input, joined_round, attended, resid_round):
    features = attn_input.shape[1]
    width = joined_round.shape[1] + resid_round.shape[1]
    return pl.pallas_call(
        attn_term_kernel,
        out_shape=jax.ShapeDtypeStruct((blocks, features // blocks, width), jnp.bfloat16),
        in_specs=[pl.BlockSpec(memory_space=pltpu.VMEM)] * 4,
        out_specs=pl.BlockSpec(memory_space=pltpu.VMEM),
        compiler_params=pltpu.CompilerParams(vmem_limit_bytes=TERMS_VMEM),
        name="attn_terms",
    )(attn_input, joined_round, attended, resid_round)


def cut_kernel(parts, source_ref, out_ref):
    shard_size, rep_size, units = parts
    mine = lax.axis_index("rep")
    for r in range(rep_size):

        @pl.when(mine == r)
        def _():
            for s in range(shard_size):
                start = (s * rep_size + r) * units
                out_ref[:, s * units : (s + 1) * units] = source_ref[:, start : start + units]


def cut_units(weight, shard_size, rep_size):
    rows, width = weight.shape
    units = width // (shard_size * rep_size)
    return pl.pallas_call(
        functools.partial(cut_kernel, (shard_size, rep_size, units)),
        out_shape=jax.ShapeDtypeStruct((rows, shard_size * units), jnp.float32),
        in_specs=[pl.BlockSpec(memory_space=pltpu.VMEM)],
        out_specs=pl.BlockSpec(memory_space=pltpu.VMEM),
        compiler_params=pltpu.CompilerParams(vmem_limit_bytes=GATHER_VMEM),
        name="cut_units",
    )(weight)


def adam_rows(weight, first, second, grad_in, decay):
    first_next = beta_one * first + (1.0 - beta_one) * grad_in
    second_next = beta_two * second + (1.0 - beta_two) * grad_in * grad_in
    correct_one = 1.0 - beta_one**ADAM_STEP
    correct_two = 1.0 - beta_two**ADAM_STEP
    scale = jnp.sqrt(second_next * (1.0 / correct_two)) + adam_eps
    shrink = 1.0 - learn_rate * decay
    updated = shrink * weight - (learn_rate / correct_one) * first_next / scale
    return updated, first_next, second_next


def adam_kernel(parts, *refs):
    shard_size, rep_size, units, steps = parts
    vec_w, vec_m, vec_g, attn_g, up_g, down_g = refs[:6]
    sources = [refs[6 + 2 * n : 8 + 2 * n] for n in range(3)]
    vec_new, vec_next = refs[12:14]
    targets = [refs[14 + 3 * n : 17 + 3 * n] for n in range(3)]
    held = [refs[23 + 3 * n : 26 + 3 * n] for n in range(3)]
    in_array, out_array = refs[32:34]

    def window(ref, n):
        count = ref.shape[-2] // steps
        rows = slice(None) if steps == 1 else pl.ds(pl.multiple_of(n * count, 8), count)
        return (slice(None),) * (len(ref.shape) - 2) + (rows, slice(None))

    def loads(t, n):
        pairs = zip(sources[t], held[t][1:])
        return [
            pltpu.make_async_copy(
                source.at[window(source, n)], kept.at[window(kept, n)], in_array.at[t, k, n]
            )
            for k, (source, kept) in enumerate(pairs)
        ]

    def stores(t, n):
        pairs = zip(held[t], targets[t])
        return [
            pltpu.make_async_copy(
                kept.at[window(kept, n)], target.at[window(target, n)], out_array.at[t, k, n]
            )
            for k, (kept, target) in enumerate(pairs)
        ]

    @pl.loop(0, steps)
    def _(n):
        for t in range(3):
            for copy in loads(t, n):
                copy.start()

    held[0][0][...] = attn_g[...].astype(jnp.float32)
    for r in range(rep_size):
        values = up_g[r].astype(jnp.float32)
        for s in range(shard_size):
            start = (s * rep_size + r) * units
            held[1][0][:, start : start + units] = values[:, s * units : (s + 1) * units]
    for r in range(rep_size):
        held[2][0][r * units : (r + 1) * units, :] = down_g[r].astype(jnp.float32)
    new, first, second = adam_rows(vec_w[...], vec_m[0], vec_m[1], vec_g[...], 0.0)
    vec_new[...] = new
    vec_next[0] = first
    vec_next[1] = second

    @pl.loop(0, steps)
    def _(n):
        for t in range(3):
            for copy in loads(t, n):
                copy.wait()
            grads, weight, moments = held[t]
            here, both = window(weight, n), window(moments, n)[1:]
            new, first, second = adam_rows(
                weight[here], moments[(0,) + both], moments[(1,) + both], grads[here], weight_decay
            )
            weight[here] = new
            moments[(0,) + both] = first
            moments[(1,) + both] = second
            for copy in stores(t, n):
                copy.start()

    @pl.loop(0, steps)
    def _(n):
        for t in range(3):
            for copy in stores(t, n):
                copy.wait()


def adam_all(rep_size, shard_size, attn, up, down, vector):
    rows, width = attn[0].shape
    units = up[2].shape[2] // shard_size
    steps = rows // 8 if rows % 8 == 0 and down[0].shape[0] % rows == 0 else 1
    shapes, scratch = [], []
    for weight, moments, _ in (attn, up, down):
        for values in (weight, weight, moments):
            shapes.append(jax.ShapeDtypeStruct(values.shape, jnp.float32))
            scratch.append(pltpu.VMEM(values.shape, jnp.float32))
    vmem_spec, any_spec = (pl.BlockSpec(memory_space=space) for space in (pltpu.VMEM, pl.ANY))
    vec_out = [jax.ShapeDtypeStruct(values.shape, jnp.float32) for values in vector[:2]]
    return pl.pallas_call(
        functools.partial(adam_kernel, (shard_size, rep_size, units, steps)),
        out_shape=vec_out + shapes,
        in_specs=[vmem_spec] * 6 + [any_spec] * 6,
        out_specs=[vmem_spec] * 2 + [any_spec] * 9,
        scratch_shapes=scratch
        + [pltpu.SemaphoreType.DMA((3, 2, steps)), pltpu.SemaphoreType.DMA((3, 3, steps))],
        compiler_params=pltpu.CompilerParams(vmem_limit_bytes=ADAM_VMEM),
        name="adam_all",
    )(*vector, attn[2], up[2], down[2], attn[0], attn[1], up[0], up[1], down[0], down[1])


def shards(
    rep_size,
    shard_size,
    hidden_in,
    cotangent,
    segment_ids,
    attn_weight,
    attn_moments,
    up_weight,
    up_moments,
    down_weight,
    down_moments,
    vectors,
    vector_moments,
):
    grid = Grid(rep_size, shard_size)
    rep = lax.axis_index("rep")
    tokens, features = hidden_in.shape
    rows, width = up_weight.shape
    units = width // (shard_size * rep_size)
    own_cols = shard_size * units
    attn_block = attn_weight.astype(jnp.bfloat16)
    mine = lambda values, axis: lax.dynamic_index_in_dim(values, rep, axis, keepdims=False)
    up_block = cut_units(up_weight, shard_size, rep_size).astype(jnp.bfloat16)
    down_block = mine(down_weight.reshape(rep_size, units, features), 0).astype(jnp.bfloat16)
    attn_split = Split(*attn_block.shape, grid.y_size, 1.0)
    blocks = [attn_split.pad(attn_block), vectors.astype(jnp.bfloat16), up_block, down_block]
    attn_wide, vector_wide, up_full, down_full = gather_params(grid, attn_split, blocks)
    attn_full = attn_wide[:, :, :rows].reshape(-1, width)
    vector_full = vector_wide.transpose(2, 0, 1, 3).reshape(vectors.shape[0], -1)
    bias = mine(
        vector_full[8:].astype(jnp.float32).reshape(shard_size, rep_size, units), 1
    ).reshape(1, own_cols)

    residual, dense_input, stored = attention_forward(
        hidden_in[None], segment_ids, attn_full, vector_full
    )
    dense_out, dense_input_grad, unit_sums, up_terms, down_terms = dense_step(
        grid, rep_size, dense_input, cotangent, up_full, down_full, bias
    )
    block_out = (residual + dense_out + vector_full[7].astype(jnp.float32)).astype(jnp.bfloat16)
    input_grad, small_rows, attn_input, joined_round, attended, resid_round = attention_backward(
        cotangent[None], segment_ids, stored, attn_full, vector_full, dense_input_grad
    )
    unit_rows = lax.dynamic_update_index_in_dim(
        jnp.zeros((shard_size, rep_size, units), jnp.float32),
        unit_sums.reshape(shard_size, units),
        rep,
        1,
    ).reshape(-1, features)
    vector_terms = jnp.concatenate([small_rows, unit_rows], axis=0)
    attn_term = attn_terms(shard_size, attn_input, joined_round, attended, resid_round)
    grads = [attn_split.pad(attn_term.reshape(grid.z_size, grid.x_size, rows, width))]
    attn_owned, vector_total, up_slices, down_slices = reduce_grads(
        grid, [attn_split], grads, vector_terms, up_terms, down_terms
    )
    own_width = vectors.shape[1]
    vector_own = lax.dynamic_slice_in_dim(
        vector_total, lax.axis_index("shard") * own_width, own_width, 1
    )
    (
        new_vectors,
        vector_next,
        attn_grad,
        new_attn,
        attn_next,
        up_grad,
        new_up,
        up_next,
        down_grad,
        new_down,
        down_next,
    ) = adam_all(
        rep_size,
        shard_size,
        (attn_weight, attn_moments, attn_owned),
        (up_weight, up_moments, up_slices),
        (down_weight, down_moments, down_slices),
        (vectors, vector_moments, vector_own),
    )
    return (
        block_out,
        input_grad[0],
        attn_grad,
        up_grad,
        down_grad,
        vector_own,
        new_attn,
        attn_next,
        new_up,
        up_next,
        new_down,
        down_next,
        new_vectors,
        vector_next,
    )


def solution(mesh):
    in_specs = (
        P(("rep", "shard"), None),
        P(("rep", "shard"), None),
        P(("rep", "shard"), None),
        P("shard", None),
        P(None, "shard", None),
        P("shard", None),
        P(None, "shard", None),
        P("shard", None),
        P(None, "shard", None),
        P(None, "shard"),
        P(None, None, "shard"),
    )
    out_specs = (
        P(("rep", "shard"), None),
        P(("rep", "shard"), None),
        P("shard", None),
        P("shard", None),
        P("shard", None),
        P(None, "shard"),
        P("shard", None),
        P(None, "shard", None),
        P("shard", None),
        P(None, "shard", None),
        P("shard", None),
        P(None, "shard", None),
        P(None, "shard"),
        P(None, None, "shard"),
    )
    body = functools.partial(shards, mesh.shape["rep"], mesh.shape["shard"])
    return jax.shard_map(body, mesh=mesh, in_specs=in_specs, out_specs=out_specs, check_vma=False)
```
